32 devices in a mesh: dp: 8 (over z, x), tensor: 4 (over y, core).
Axes of the slice: x: 2, y: 2, z: 4, core: 2. Of those that a mesh axis runs over, the one named last changes fastest.
Arguments:
- tokens: bfloat16 [16384, 1024], P(('dp', 'tensor'))
- w_query: bfloat16 [1024, 2048], P(None, 'tensor'), may hold values from -0.1875 to 0.1875
- w_key: bfloat16 [1024, 1024], P(None, 'tensor'), may hold values from -0.1875 to 0.1875
- w_value: bfloat16 [1024, 1024], P(None, 'tensor'), may hold values from -0.1875 to 0.1875
- w_out: bfloat16 [2048, 1024], P('tensor'), may hold values from -0.5 to 0.5
- w_gate: bfloat16 [1024, 3072], P(None, 'tensor'), may hold values from -0.1875 to 0.1875
- w_up: bfloat16 [1024, 3072], P(None, 'tensor'), may hold values from -0.1875 to 0.1875
- w_down: bfloat16 [3072, 1024], P('tensor'), may hold values from -0.109375 to 0.109375
- norm_attn: bfloat16 [1024], replicated, may hold values from 0.099609375 to 1.8984375
- norm_mlp: bfloat16 [1024], replicated, may hold values from 0.099609375 to 1.8984375
- norm_query: bfloat16 [128], replicated, may hold values from 0.796875 to 1.59375
- norm_key: bfloat16 [128], replicated, may hold values from 0.796875 to 1.59375
- cotangent: bfloat16 [16384, 1024], P(('dp', 'tensor')), may hold values from -6 to 6
- segments: int32 [8, 2048], P('dp'), may hold values from 0 to 3, as said below
- positions: int32 [8, 2048], P('dp'), may hold values from 0 to 1023, as said below
Outputs:
- output: bfloat16 [16384, 1024], P(('dp', 'tensor'))
- d_tokens: float32 [16384, 1024], P(('dp', 'tensor'))
- d_w_query: float32 [1024, 2048], P(None, 'tensor')
- d_w_key: float32 [1024, 1024], P(None, 'tensor')
- d_w_value: float32 [1024, 1024], P(None, 'tensor')
- d_w_out: float32 [2048, 1024], P('tensor')
- d_w_gate: float32 [1024, 3072], P(None, 'tensor')
- d_w_up: float32 [1024, 3072], P(None, 'tensor')
- d_w_down: float32 [3072, 1024], P('tensor')
- d_norm_attn: float32 [1024], replicated
- d_norm_mlp: float32 [1024], replicated
- d_norm_query: float32 [128], replicated
- d_norm_key: float32 [128], replicated
The draws below stay inside these ranges and needn't reach their ends.
Inputs may be any that keep to these rules, and one draw needn't show every extreme that they name: `segments`: each sequence holds four documents numbered 0 to 3 in order; one has 1024 tokens, the others 2048 // 10 or more. `positions`: the position of a token within its document, from 0.
All inputs are finite; a program needn't handle non-finite values.
Results may differ from the reference program's by a relative error of at most 0.019.
Values may be sent and summed in bfloat16 or wider, within the bound.
A program may use at most 320 MiB of HBM per device.

```python
import math
import jax
import jax.numpy as jnp
from jax import lax

D = 1024
H = 16
KV = 8
HD = 128
FF = 3072
SEQ = 2048
SEQUENCES = 8
TOKENS = 16384


def document_layout(key):
    base = jax.random.fold_in(key, 7)
    first_key, second_key, slot_key = jax.random.split(base, 3)
    half = SEQ // 2
    least = SEQ // 10
    first = jax.random.randint(first_key, (SEQUENCES,), least, (half - least) // 2 + 1).astype(jnp.int32)
    second = jax.random.randint(second_key, (SEQUENCES,), least, (half - least) // 2 + 1).astype(jnp.int32)
    third = (half - first - second).astype(jnp.int32)
    slot = jax.random.randint(slot_key, (SEQUENCES, 1), 0, 4).astype(jnp.int32)
    shorts = jnp.stack([first, second, third], 1)
    column = jnp.arange(4, dtype=jnp.int32)[None, :]
    below = jnp.take_along_axis(shorts, jnp.broadcast_to(jnp.clip(column, 0, 2), (SEQUENCES, 4)), 1)
    above = jnp.take_along_axis(shorts, jnp.broadcast_to(jnp.clip(column - 1, 0, 2), (SEQUENCES, 4)), 1)
    lengths = jnp.where(column < slot, below, jnp.where(column == slot, half, above)).astype(jnp.int32)
    ends = jnp.cumsum(lengths, 1).astype(jnp.int32)
    starts = (ends - lengths).astype(jnp.int32)
    index = jnp.arange(SEQ, dtype=jnp.int32)[None, :, None]
    segment = jnp.sum((index >= ends[:, None, :]).astype(jnp.int32), 2).astype(jnp.int32)
    begin = jnp.take_along_axis(starts, segment, 1)
    position = (jnp.arange(SEQ, dtype=jnp.int32)[None, :] - begin).astype(jnp.int32)
    return (segment, position)


def draw_segments(key, part):
    return document_layout(key)[0]


def draw_positions(key, part):
    return document_layout(key)[1]


def draw_tokens(key, part):
    keys = jax.random.split(key, 3)
    rough = jnp.clip(jax.random.normal(keys[0], (TOKENS, D), jnp.float32), -6.0, 6.0)
    row_scale = jnp.exp(jax.random.uniform(keys[1], (TOKENS, 1), jnp.float32, math.log(0.3), math.log(3.0)))
    col_scale = jnp.exp(jax.random.uniform(keys[2], (1, D), jnp.float32, math.log(0.3), math.log(3.0)))
    return (rough * row_scale * col_scale).astype(jnp.bfloat16)


def level_of(rng, shape, shards, low, high):
    loudness = 1.0
    for dim, blocks in shards:
        steps = jax.random.uniform(jax.random.fold_in(jax.random.fold_in(rng, 6), dim), (blocks,), jnp.float32, low / len(shards), high / len(shards))
        loudness = loudness * jnp.repeat(jnp.exp(steps), shape[dim] // blocks).reshape((-1,) + (1,) * (len(shape) - 1 - dim))
    return loudness


def gaussian(stream_key, extent, spread, reach, pieces=(), kind=jnp.bfloat16):
    level = level_of(stream_key, extent, pieces, -0.22, 0.18) if pieces else 1.0
    array = jax.random.normal(stream_key, extent, jnp.float32) * spread * level
    return jnp.minimum(jnp.maximum(array, -reach), reach).astype(kind)


def setup_inputs(seed: int = 0) -> dict:
    key_of = jax.random.split(jax.random.key(seed), 16)
    tokens = draw_tokens(jax.random.fold_in(key_of[15], 71), 0)
    w_query = gaussian(key_of[1], (D, H * HD), D ** -0.5, 0.1875, ((1, 4),))
    w_key = gaussian(key_of[2], (D, KV * HD), D ** -0.5, 0.1875, ((1, 4),))
    w_value = gaussian(key_of[3], (D, KV * HD), D ** -0.5, 0.1875, ((1, 4),))
    w_out = gaussian(key_of[4], (H * HD, D), (H * HD // 16) ** -0.5, 0.5, ((0, 4),))
    w_gate = gaussian(key_of[5], (D, FF), D ** -0.5, 0.1875, ((1, 4),))
    w_up = gaussian(key_of[6], (D, FF), D ** -0.5, 0.1875, ((1, 4),))
    w_down = gaussian(key_of[7], (FF, D), FF ** -0.5, 0.109375, ((0, 4),))
    norm_attn = jnp.clip(1.0 + 0.18 * jax.random.normal(key_of[8], (D,), jnp.float32), 0.099609375, 1.8984375).astype(jnp.bfloat16)
    norm_mlp = jnp.clip(1.0 + 0.18 * jax.random.normal(key_of[9], (D,), jnp.float32), 0.099609375, 1.8984375).astype(jnp.bfloat16)
    norm_query = jnp.clip(jnp.exp(jax.random.uniform(key_of[10], (HD,), jnp.float32, math.log(0.796875), math.log(1.59375))), 0.796875, 1.59375).astype(jnp.bfloat16)
    norm_key = jnp.clip(jnp.exp(jax.random.uniform(key_of[11], (HD,), jnp.float32, math.log(0.796875), math.log(1.59375))), 0.796875, 1.59375).astype(jnp.bfloat16)
    cotangent = gaussian(key_of[12], (TOKENS, D), 1.0, 6.0, ((0, 32),))
    segments = draw_segments(jax.random.fold_in(key_of[15], 71), 0)
    positions = draw_positions(jax.random.fold_in(key_of[15], 71), 0)
    return dict(tokens=tokens, w_query=w_query, w_key=w_key, w_value=w_value, w_out=w_out, w_gate=w_gate, w_up=w_up, w_down=w_down, norm_attn=norm_attn, norm_mlp=norm_mlp, norm_query=norm_query, norm_key=norm_key, cotangent=cotangent, segments=segments, positions=positions)


@jax.custom_vjp
def low(v):
    return lax.optimization_barrier(v.astype(jnp.bfloat16)).astype(jnp.float32)

@jax.custom_vjp
def low_back(v):
    return v

def low_keep(v):
    return (low(v), None)

def low_pass(kept, grad):
    return (grad,)

def back_keep(v):
    return (v, None)

def back_low(kept, grad):
    return (low(grad),)
low.defvjp(low_keep, low_pass)
low_back.defvjp(back_keep, back_low)
EPSILON = 1e-06
THETA = 1000000.0
NEGATIVE = -1e+30

def norm_rows(values, gain):
    return values * lax.rsqrt(lax.optimization_barrier(jnp.mean(values * values, -1, keepdims=True)) + EPSILON) * gain

def rotate_half(values):
    middle = values.shape[-1] // 2
    return jnp.concatenate([-values[..., middle:], values[..., :middle]], -1)

def rotary(values, cosine, sine):
    return values * cosine[:, None, :] + rotate_half(values) * sine[:, None, :]

def rope_tables(position_flat, head_size):
    freqs = THETA ** (-jnp.arange(0, head_size, 2).astype(jnp.float32) / head_size)
    angles = position_flat.astype(jnp.float32)[:, None] * freqs[None, :]
    angles = jnp.concatenate([angles, angles], -1)
    return (jnp.cos(angles), jnp.sin(angles))

def matmul(left, right):
    return jnp.dot(left, right, precision=lax.Precision.HIGHEST)

def attention(query, keys, values, segs, posn):
    length = query.shape[0]
    block = min(512, length)
    count = length // block
    ratio = H // KV
    scale = HD ** (-0.5)
    query_blocks = query.reshape(count, block, KV, ratio, HD)
    seg_blocks = segs.reshape(count, block)
    pos_blocks = posn.reshape(count, block)

    def one_block(items):
        query_block, seg_block, pos_block = items
        scores = jnp.einsum('qgrd,kgd->grqk', query_block, keys, precision=lax.Precision.HIGHEST) * scale
        scores = low_back(scores)
        mask = (seg_block[:, None] == segs[None, :]) & (posn[None, :] <= pos_block[:, None])
        scores = jnp.where(mask[None, None], scores, NEGATIVE)
        soft = jax.nn.softmax(scores, -1)
        return jnp.einsum('grqk,kgd->qgrd', low(soft), values, precision=lax.Precision.HIGHEST)
    result = lax.map(jax.checkpoint(one_block), (query_blocks, seg_blocks, pos_blocks))
    return result.reshape(length, H * HD)

def layer(x, w_query, w_key, w_value, w_out, w_gate, w_up, w_down, norm_attn, norm_mlp, norm_query, norm_key, segs, posn):
    length = x.shape[0]
    cosine, sine = rope_tables(posn, HD)
    normed_in = low(norm_rows(x, norm_attn))
    query_raw = low_back(matmul(normed_in, w_query)).reshape(length, H, HD)
    key_raw = low_back(matmul(normed_in, w_key)).reshape(length, KV, HD)
    values = low_back(low(matmul(normed_in, w_value))).reshape(length, KV, HD)
    query = low(rotary(norm_rows(query_raw, norm_query), cosine, sine))
    keys = low(rotary(norm_rows(key_raw, norm_key), cosine, sine))
    attended = low_back(low(attention(query, keys, values, segs, posn)))
    hidden = x + low_back(matmul(attended, w_out))
    normed_mid = low(norm_rows(hidden, norm_mlp))
    gate = low_back(matmul(normed_mid, w_gate))
    up = low_back(matmul(normed_mid, w_up))
    inner = low(jax.nn.silu(gate) * up)
    return hidden + low_back(matmul(inner, w_down))

def reference(tokens, w_query, w_key, w_value, w_out, w_gate, w_up, w_down, norm_attn, norm_mlp, norm_query, norm_key, cotangent, segments, positions):
    weights = tuple((w.astype(jnp.float32) for w in (w_query, w_key, w_value, w_out, w_gate, w_up, w_down, norm_attn, norm_mlp, norm_query, norm_key)))
    inputs = tokens.astype(jnp.float32).reshape(SEQUENCES, SEQ, D)
    grads_in = cotangent.astype(jnp.float32).reshape(SEQUENCES, SEQ, D)

    def step(carry, items):
        x, grad_y, segs, posn = items

        def forward(x_in, *params):
            return layer(x_in, *params, segs, posn)
        result, pull = jax.vjp(forward, x, *weights)
        grads = pull(grad_y)
        carry = tuple((a + b for a, b in zip(carry, grads[1:])))
        return (carry, (result.astype(jnp.bfloat16), grads[0]))
    init = tuple((jnp.zeros_like(w) for w in weights))
    totals, (results, d_rows) = lax.scan(step, init, (inputs, grads_in, segments, positions))
    return (results.reshape(TOKENS, D), d_rows.reshape(TOKENS, D), totals[0], totals[1], totals[2], totals[3], totals[4], totals[5], totals[6], totals[7], totals[8], totals[9], totals[10])
```

```python
import functools, math
import jax, jax.numpy as jnp
from jax import lax
from jax.sharding import PartitionSpec as P
from jax.experimental import pallas as pl
from jax.experimental.pallas import tpu as pltpu
HD=128
EPS=1e-6
F32=jnp.float32; BF=jnp.bfloat16
NT=(((1,),(1,)),((),()))
TN=(((0,),(0,)),((),()))
NN=(((1,),(0,)),((),()))
def dot(a,b,dims=NN): return lax.dot_general(a,b,dims,preferred_element_type=F32)
LOG2E=math.log2(math.e)

def attn_fwd_kernel(bq,bk,ratio,scale,lo_ref,q_ref,k_ref,v_ref,end_ref,o_ref,l_ref,vx_ref,acc_ref):
    i=pl.program_id(1)
    n=k_ref.shape[0]
    @pl.when(i==0)
    def _():
        vx_ref[:,:HD]=v_ref[...]
        vx_ref[:,HD:]=jnp.ones((n,HD),BF)
    q=q_ref[...]
    qs=jnp.concatenate([q[:,h*HD:(h+1)*HD] for h in range(ratio)],0)
    rows=lax.rem(lax.broadcasted_iota(jnp.int32,(ratio*bq,1),0),bq)+i*bq
    acc_ref[...]=jnp.zeros_like(acc_ref)
    c=scale*LOG2E
    def step(j,_):
        b=pl.multiple_of(j*bk,bk)
        s=dot(qs,k_ref[pl.ds(b,bk),:],NT)
        cols=lax.broadcasted_iota(jnp.int32,(1,bk),1)+b
        m=(rows>=cols)&(rows<end_ref[:,pl.ds(b,bk)])
        e=jnp.where(m,jnp.exp2(s*c),0.0).astype(BF)
        acc_ref[...]+=dot(e,vx_ref[pl.ds(b,bk),:])
        return 0
    lax.fori_loop(lo_ref[i],(i*bq+bq-1)//bk+1,step,0)
    a=acc_ref[...]
    l=a[:,HD:]
    o=(a[:,:HD]/l).astype(BF)
    lt=jnp.log2(l).T[0:1]
    for h in range(ratio):
        o_ref[:,h*HD:(h+1)*HD]=o[h*bq:(h+1)*bq]
        l_ref[0,h:h+1,:]=lt[:,h*bq:(h+1)*bq]

def attn_fwd(q,k,v,end,lo,bq,bk,scale):
    n,wq=q.shape; g=k.shape[1]//HD; ratio=wq//HD//g
    gs=pltpu.PrefetchScalarGridSpec(num_scalar_prefetch=1,grid=(g,n//bq),
        in_specs=[pl.BlockSpec((bq,ratio*HD),lambda g,i,lo:(i,g)),
                  pl.BlockSpec((n,HD),lambda g,i,lo:(0,g)),
                  pl.BlockSpec((n,HD),lambda g,i,lo:(0,g)),
                  pl.BlockSpec((1,n),lambda g,i,lo:(0,0))],
        out_specs=[pl.BlockSpec((bq,ratio*HD),lambda g,i,lo:(i,g)),
                   pl.BlockSpec((1,ratio,bq),lambda g,i,lo:(g,0,i))],
        scratch_shapes=[pltpu.VMEM((n,2*HD),BF),pltpu.VMEM((ratio*bq,2*HD),F32)])
    return pl.pallas_call(functools.partial(attn_fwd_kernel,bq,bk,ratio,scale),grid_spec=gs,
        out_shape=[jax.ShapeDtypeStruct((n,wq),BF),jax.ShapeDtypeStruct((g,ratio,n),F32)],name='attn_fwd')(lo,q,k,v,end)

def norm_rot_bwd(d,raw,gain,cos,sin):
    du=d*cos-pltpu.roll(d,HD//2,1)*sin
    r=lax.rsqrt(jnp.mean(raw*raw,-1,keepdims=True)+EPS)
    xh=raw*r
    ge=du*gain
    dx=r*(ge-xh*jnp.mean(xh*ge,-1,keepdims=True))
    return dx,jnp.sum(du*xh,0,keepdims=True)

def attn_bwd_kernel(bq,bk,ratio,scale,lo_ref,q_ref,k_ref,v_ref,do_ref,o_ref,l_ref,start_ref,qraw_ref,kraw_ref,cos_ref,sin_ref,gq_ref,gk_ref,
                    dq_ref,dk_ref,dv_ref,dgq_ref,dgk_ref,dka,dva,dqa):
    g=pl.program_id(0); i=pl.program_id(1); nb=pl.num_programs(1)
    @pl.when(i==0)
    def _():
        dka[...]=jnp.zeros_like(dka); dva[...]=jnp.zeros_like(dva)
    @pl.when((i==0)&(g==0))
    def _():
        dgq_ref[...]=jnp.zeros_like(dgq_ref); dgk_ref[...]=jnp.zeros_like(dgk_ref)
    q=q_ref[...]; do=do_ref[...]
    qs=jnp.concatenate([q[:,h*HD:(h+1)*HD] for h in range(ratio)],0)
    ds_=jnp.concatenate([do[:,h*HD:(h+1)*HD] for h in range(ratio)],0)
    pr=do.astype(F32)*o_ref[...].astype(F32)
    prs=jnp.concatenate([pr[:,h*HD:(h+1)*HD] for h in range(ratio)],0)
    D=jnp.sum(prs.T,0,keepdims=True)
    lse=jnp.concatenate([l_ref[0,h:h+1,:] for h in range(ratio)],1)
    st=start_ref[...]
    st=jnp.concatenate([st]*ratio,1)
    cols=lax.rem(lax.broadcasted_iota(jnp.int32,(1,ratio*bq),1),bq)+i*bq
    dqa[...]=jnp.zeros_like(dqa)
    c=scale*LOG2E
    def step(j,_):
        b=pl.multiple_of(j*bk,bk)
        kb=k_ref[pl.ds(b,bk),:]; vb=v_ref[pl.ds(b,bk),:]
        s=dot(kb,qs,NT)
        rows=lax.broadcasted_iota(jnp.int32,(bk,1),0)+b
        m=(cols>=rows)&(st<=rows)
        p=jnp.where(m,jnp.exp2(s*c-lse),0.0)
        dp=dot(vb,ds_,NT)
        dsT=(p*(dp-D)).astype(BF)
        dva[pl.ds(b,bk),:]+=dot(p.astype(BF),ds_)
        dka[pl.ds(b,bk),:]+=dot(dsT,qs)
        dqa[...]+=dot(dsT,kb,TN)
        return 0
    lax.fori_loop(lo_ref[i],(i*bq+bq-1)//bk+1,step,0)
    r0=pl.multiple_of(i*bq,bq)
    cos=cos_ref[pl.ds(r0,bq),:]; sin=sin_ref[pl.ds(r0,bq),:]
    gq=gq_ref[...]
    tot=jnp.zeros((1,HD),F32)
    for h in range(ratio):
        dx,dg=norm_rot_bwd(dqa[h*bq:(h+1)*bq,:]*scale,qraw_ref[:,h*HD:(h+1)*HD],gq,cos,sin)
        dq_ref[:,h*HD:(h+1)*HD]=dx.astype(BF)
        tot=tot+dg
    dgq_ref[...]+=tot
    @pl.when(i==nb-1)
    def _():
        gk=gk_ref[...]
        def fin(t,acc):
            r=pl.multiple_of(t*bq,bq)
            dx,dg=norm_rot_bwd(dka[pl.ds(r,bq),:]*scale,kraw_ref[pl.ds(r,bq),:],gk,cos_ref[pl.ds(r,bq),:],sin_ref[pl.ds(r,bq),:])
            dk_ref[pl.ds(r,bq),:]=dx.astype(BF)
            dv_ref[pl.ds(r,bq),:]=dva[pl.ds(r,bq),:].astype(BF)
            return acc+dg
        dgk_ref[...]+=lax.fori_loop(0,dka.shape[0]//bq,fin,jnp.zeros((1,HD),F32))

def attn_bwd(q,k,v,do,o,l,start,lo,qraw,kraw,cos,sin,gq,gk,bq,bk,scale):
    n,wq=q.shape; wk=k.shape[1]; g=wk//HD; ratio=wq//HD//g
    qs=pl.BlockSpec((bq,ratio*HD),lambda g,i,lo:(i,g))
    ks=pl.BlockSpec((n,HD),lambda g,i,lo:(0,g))
    full=pl.BlockSpec((n,HD),lambda g,i,lo:(0,0))
    one=pl.BlockSpec((1,HD),lambda g,i,lo:(0,0))
    gs=pltpu.PrefetchScalarGridSpec(num_scalar_prefetch=1,grid=(g,n//bq),
        in_specs=[qs,ks,ks,qs,qs,pl.BlockSpec((1,ratio,bq),lambda g,i,lo:(g,0,i)),pl.BlockSpec((1,bq),lambda g,i,lo:(0,i)),
                  qs,ks,full,full,one,one],
        out_specs=[qs,ks,ks,one,one],
        scratch_shapes=[pltpu.VMEM((n,HD),F32),pltpu.VMEM((n,HD),F32),pltpu.VMEM((ratio*bq,HD),F32)])
    return pl.pallas_call(functools.partial(attn_bwd_kernel,bq,bk,ratio,scale),grid_spec=gs,
        out_shape=[jax.ShapeDtypeStruct((n,wq),BF),jax.ShapeDtypeStruct((n,wk),BF),jax.ShapeDtypeStruct((n,wk),BF),
                   jax.ShapeDtypeStruct((1,HD),F32),jax.ShapeDtypeStruct((1,HD),F32)],name='attn_bwd')(lo,q,k,v,do,o,l,start,qraw,kraw,cos,sin,gq,gk)

def norm_rot(raw,gain,cos,sin):
    u=raw*lax.rsqrt(jnp.mean(raw*raw,-1,keepdims=True)+EPS)*gain
    return u*cos+pltpu.roll(u,HD//2,1)*sin

def qkv_kernel(x_ref,g_ref,wq_ref,wk_ref,wv_ref,cos_ref,sin_ref,gq_ref,gk_ref,a_ref,q_ref,k_ref,v_ref,qraw_ref,kraw_ref):
    x=x_ref[...].astype(F32)
    a=(x*lax.rsqrt(jnp.mean(x*x,-1,keepdims=True)+EPS)*g_ref[...]).astype(BF)
    a_ref[...]=a
    qr=dot(a,wq_ref[...]); kr=dot(a,wk_ref[...])
    v_ref[...]=dot(a,wv_ref[...]).astype(BF)
    qraw_ref[...]=qr; kraw_ref[...]=kr
    cos=cos_ref[...]; sin=sin_ref[...]
    gq=gq_ref[...]; gk=gk_ref[...]
    for h in range(qr.shape[1]//HD):
        q_ref[:,h*HD:(h+1)*HD]=norm_rot(qr[:,h*HD:(h+1)*HD],gq,cos,sin).astype(BF)
    for h in range(kr.shape[1]//HD):
        k_ref[:,h*HD:(h+1)*HD]=norm_rot(kr[:,h*HD:(h+1)*HD],gk,cos,sin).astype(BF)

def qkv(x,gain,wq,wk,wv,cos,sin,gq,gk,r=256):
    n,d=x.shape
    rb=lambda w: pl.BlockSpec((r,w),lambda i:(i,0))
    fb=lambda a: pl.BlockSpec(a.shape,lambda i:(0,0))
    return pl.pallas_call(qkv_kernel,grid=(n//r,),
        in_specs=[rb(d),fb(gain),fb(wq),fb(wk),fb(wv),rb(HD),rb(HD),fb(gq),fb(gk)],
        out_specs=[rb(d),rb(wq.shape[1]),rb(wk.shape[1]),rb(wv.shape[1]),rb(wq.shape[1]),rb(wk.shape[1])],
        out_shape=[jax.ShapeDtypeStruct((n,d),BF),jax.ShapeDtypeStruct((n,wq.shape[1]),BF),jax.ShapeDtypeStruct((n,wk.shape[1]),BF),jax.ShapeDtypeStruct((n,wv.shape[1]),BF),
                   jax.ShapeDtypeStruct((n,wq.shape[1]),F32),jax.ShapeDtypeStruct((n,wk.shape[1]),F32)],name='qkv')(x,gain,wq,wk,wv,cos,sin,gq,gk)

def mlp_kernel(a_ref,dy_ref,wg_ref,wu_ref,wd_ref,act_ref,dg_ref,du_ref,o_ref,da_ref):
    a=a_ref[...]
    gate=dot(a,wg_ref[...]); up=dot(a,wu_ref[...])
    dact=dot(dy_ref[...],wd_ref[...],NT)
    sig=1.0/(1.0+jnp.exp(-gate))
    sl=gate*sig
    act=(sl*up).astype(BF)
    act_ref[...]=act
    dg=(dact*up*(sig*(1.0+gate*(1.0-sig)))).astype(BF)
    du=(dact*sl).astype(BF)
    dg_ref[...]=dg; du_ref[...]=du
    o_ref[...]=dot(act,wd_ref[...]).astype(BF)
    da_ref[...]=(dot(dg,wg_ref[...],NT)+dot(du,wu_ref[...],NT)).astype(BF)

def mlp(a2,dy,wg,wu,wd,r=256):
    n,d=a2.shape; f=wg.shape[1]
    rb=lambda w: pl.BlockSpec((r,w),lambda i:(i,0))
    fb=lambda a: pl.BlockSpec(a.shape,lambda i:(0,0))
    S=jax.ShapeDtypeStruct
    return pl.pallas_call(mlp_kernel,grid=(n//r,),in_specs=[rb(d),rb(d),fb(wg),fb(wu),fb(wd)],
        out_specs=[rb(f)]*3+[rb(d)]*2,out_shape=[S((n,f),BF)]*3+[S((n,d),BF)]*2,name='mlp')(a2,dy,wg,wu,wd)
MESH=pl.DeviceIdType.MESH
def ring_neighbours(d):
    me=lax.axis_index('dp')
    half=d//2
    odd=lax.rem(me,2); up=me//2
    pos=odd*(d-1-2*up)+up
    def at(p):
        hi=p//half
        return hi*(2*(d-1-p)+1)+(1-hi)*2*p
    return pos,at(lax.rem(pos+1,d)),at(lax.rem(pos+d-1,d))

def ring_kernel(d,ns,na,*refs):
    ins=refs[:na]; outs=refs[na:2*na]; recv=refs[2*na:3*na]; ssem,rsem,asem,bsem=refs[3*na:]
    pos,right,left=ring_neighbours(d)
    to={0:right,1:left}
    barrier=pltpu.get_barrier_semaphore()
    for n in (left,right):
        pl.semaphore_signal(barrier,inc=1,device_id={'dp':n},device_id_type=MESH)
    pl.semaphore_wait(barrier,2)
    rows=[r.shape[0]//d for r in ins]
    wid=[r.shape[1]//ns for r in ins]
    def chunk(s,k):
        return lax.rem(pos-k+2*d,d) if s%2==0 else lax.rem(pos+k,d)
    def rs(a,s,k,src):
        return pltpu.make_async_remote_copy(src_ref=src,dst_ref=recv[a].at[k,:,s*wid[a]:(s+1)*wid[a]],send_sem=ssem.at[a,s,k],recv_sem=rsem.at[a,s,k],
            device_id={'dp':to[s%2]},device_id_type=MESH)
    def at(ref,a,s,c):
        return ref.at[pl.ds(pl.multiple_of(c*rows[a],rows[a]),rows[a]),s*wid[a]:(s+1)*wid[a]]
    def ag(a,s,k,c):
        return pltpu.make_async_remote_copy(src_ref=at(outs[a],a,s,c),dst_ref=at(outs[a],a,s,c),send_sem=asem.at[a,s,k],recv_sem=bsem.at[a,s,k],
            device_id={'dp':to[s%2]},device_id_type=MESH)
    cps={}
    for s in range(ns):
        for a in range(na):
            cps[a,s,0]=rs(a,s,0,at(ins[a],a,s,chunk(s,0))); cps[a,s,0].start()
    ags={}
    for k in range(1,d):
        for s in range(ns):
            c=chunk(s,k)
            for a in range(na):
                cps[a,s,k-1].wait_recv()
                sl=slice(s*wid[a],(s+1)*wid[a])
                src=at(ins[a],a,s,c)
                val=(src[...].astype(F32)+recv[a][k-1,:,sl].astype(F32)).astype(BF)
                if k<d-1:
                    recv[a][k-1,:,sl]=val
                    cps[a,s,k]=rs(a,s,k,recv[a].at[k-1,:,sl]); cps[a,s,k].start()
                else:
                    at(outs[a],a,s,c)[...]=val
                    ags[a,s,0]=ag(a,s,0,c); ags[a,s,0].start()
    for k in range(1,d):
        for s in range(ns):
            c=chunk(s,k-1)
            for a in range(na):
                ags[a,s,k-1].wait_recv()
                if k<d-1:
                    ags[a,s,k]=ag(a,s,k,c); ags[a,s,k].start()
    for s in range(ns):
        for a in range(na):
            for k in range(d-1):
                cps[a,s,k].wait_send(); ags[a,s,k].wait_send()

def ring(arrays,d,cid,ns=4):
    na=len(arrays)
    S=jax.ShapeDtypeStruct
    V=pl.BlockSpec(memory_space=pltpu.VMEM)
    return pl.pallas_call(functools.partial(ring_kernel,d,ns,na),
        in_specs=[V]*na,out_specs=[V]*na,out_shape=[S(a.shape,BF) for a in arrays],
        scratch_shapes=[pltpu.VMEM((d-1,a.shape[0]//d,a.shape[1]),BF) for a in arrays]+[pltpu.SemaphoreType.DMA((na,ns,d-1))]*4,
        compiler_params=pltpu.CompilerParams(collective_id=cid,has_side_effects=True,vmem_limit_bytes=60<<20),name='ring%d'%cid)(*arrays)

def gains_kernel(sizes,x_ref,o_ref,recv,ssem,rsem):
    steps=[]
    for axis,n in sizes:
        b=1
        while b<n:
            steps.append((axis,b)); b*=2
    def partner(axis,b):
        me=lax.axis_index(axis)
        return me+b-2*b*lax.rem(me//b,2)
    barrier=pltpu.get_barrier_semaphore()
    for axis,b in steps:
        pl.semaphore_signal(barrier,inc=1,device_id={axis:partner(axis,b)},device_id_type=MESH)
    pl.semaphore_wait(barrier,len(steps))
    o_ref[...]=x_ref[...]
    cps=[]
    for i,(axis,b) in enumerate(steps):
        src=recv.at[2*i+1]
        src[...]=o_ref[...]
        c=pltpu.make_async_remote_copy(src_ref=src,dst_ref=recv.at[2*i],send_sem=ssem.at[i],recv_sem=rsem.at[i],device_id={axis:partner(axis,b)},device_id_type=MESH)
        c.start(); c.wait_recv()
        o_ref[...]+=recv[2*i]
        cps.append(c)
    for c in cps: c.wait_send()

def sum_gains(x,sizes,cid):
    n=sum((s-1).bit_length() for _,s in sizes)
    V=pl.BlockSpec(memory_space=pltpu.VMEM)
    return pl.pallas_call(functools.partial(gains_kernel,sizes),in_specs=[V],out_specs=V,out_shape=jax.ShapeDtypeStruct(x.shape,F32),
        scratch_shapes=[pltpu.VMEM((2*n,)+x.shape,F32),pltpu.SemaphoreType.DMA((n,)),pltpu.SemaphoreType.DMA((n,))],
        compiler_params=pltpu.CompilerParams(collective_id=cid,has_side_effects=True),name='gains')(x)

THETA=1000000.0
def rope_tables(pos):
    freqs=THETA**(-jnp.arange(0,HD,2).astype(F32)/HD)
    ang=pos.astype(F32)[:,None]*freqs[None,:]
    c,s=jnp.cos(ang),jnp.sin(ang)
    return jnp.concatenate([c,c],1),jnp.concatenate([-s,s],1)

def norm_bwd(v,gain,e):
    r=lax.rsqrt(jnp.mean(v*v,-1,keepdims=True)+EPS)
    vh=v*r
    ge=e*gain
    return r*(ge-vh*jnp.mean(vh*ge,-1,keepdims=True)),jnp.sum(e*vh,0)

def gather(a): return lax.all_gather(a,'tensor',axis=0,tiled=True)
def scatter(a): return lax.psum_scatter(a,'tensor',scatter_dimension=0,tiled=True).astype(F32)

def local(nd,nt,tokens,w_query,w_key,w_value,w_out,w_gate,w_up,w_down,norm_attn,norm_mlp,norm_query,norm_key,cotangent,segments,positions):
    n=segments.shape[1]
    scale=HD**-0.5
    seg=segments.reshape(-1); pos=positions.reshape(-1)
    idx=jnp.arange(n,dtype=jnp.int32)
    start=idx-pos
    ends=jnp.sum((seg[None,:]<=jnp.arange(4,dtype=jnp.int32)[:,None]).astype(jnp.int32),1)
    end=jnp.sum(jnp.where(seg[None,:]==jnp.arange(4,dtype=jnp.int32)[:,None],ends[:,None],0),0)
    bq=512; bk=512
    lo=start[::bq]//bk
    cos,sin=rope_tables(pos)
    g_attn=norm_attn.astype(F32); g_mlp=norm_mlp.astype(F32)
    gq=norm_query.astype(F32)[None]; gk=norm_key.astype(F32)[None]
    xs=gather(tokens)
    dy=gather(cotangent)
    a1,q,k,v,qraw,kraw=qkv(xs,g_attn[None],w_query,w_key,w_value,cos,sin,gq,gk)
    att,lse=attn_fwd(q,k,v,end[None],lo,bq,bk,scale)
    att,dy=lax.optimization_barrier((att,dy))
    x_own=tokens.astype(F32)
    hid=x_own+scatter(dot(att,w_out).astype(BF))
    a2=gather((hid*lax.rsqrt(jnp.mean(hid*hid,-1,keepdims=True)+EPS)*g_mlp).astype(BF))
    act,dg,du,outp,dap=mlp(a2,dy,w_gate,w_up,w_down)
    da2=scatter(dap)
    dwd=dot(act,dy,TN).astype(BF)
    dwg=dot(a2,dg,TN).astype(BF); dwu=dot(a2,du,TN).astype(BF)
    dwd,=ring([dwd],nd,1)
    da2,dwd,dwg,dwu=lax.optimization_barrier((da2,dwd,dwg,dwu))
    dh,dg_mlp=norm_bwd(hid,g_mlp,da2)
    dhid=cotangent.astype(F32)+dh
    dhb=gather(dhid.astype(BF))
    dwg,dwu=ring([dwg,dwu],nd,2,ns=2)
    dhb,dwg,dwu=lax.optimization_barrier((dhb,dwg,dwu))
    output=(hid+scatter(outp)).astype(BF)
    dwo=dot(att,dhb,TN).astype(BF)
    dout=dot(dhb,w_out,NT).astype(BF)
    dq,dk,dv,dgq,dgk=attn_bwd(q,k,v,dout,att,lse,start[None],lo,qraw,kraw,cos,sin,gq,gk,bq,bk,scale)
    dap1=(dot(dq,w_query,NT)+dot(dk,w_key,NT)+dot(dv,w_value,NT)).astype(BF)
    da1=scatter(dap1)
    dwq=dot(a1,dq,TN).astype(BF); dwk=dot(a1,dk,TN).astype(BF); dwv=dot(a1,dv,TN).astype(BF)
    dwq,dwk,dwv,dwo=ring([dwq,dwk,dwv,dwo],nd,3,ns=2)
    da1,dwq,dwk,dwv,dwo=lax.optimization_barrier((da1,dwq,dwk,dwv,dwo))
    dx,dg_attn=norm_bwd(x_own,g_attn,da1)
    d_tokens=dhid+dx
    gains=jnp.concatenate([dg_attn,dg_mlp,dgq[0],dgk[0]]).reshape(-1,HD)
    rows=gains.shape[0]
    gains=sum_gains(jnp.pad(gains,((0,-rows%8),(0,0))),(('dp',nd),('tensor',nt)),4).reshape(-1)
    D=g_attn.shape[0]
    up=lambda a: a.astype(F32)
    return (output,d_tokens,up(dwq),up(dwk),up(dwv),up(dwo),up(dwg),up(dwu),up(dwd),gains[:D],gains[D:2*D],gains[2*D:2*D+HD],gains[2*D+HD:2*D+2*HD])

def solution(mesh):
    nd,nt=mesh.shape['dp'],mesh.shape['tensor']
    row=P(('dp','tensor'),None); col=P(None,'tensor'); rw=P('tensor',None)
    return jax.shard_map(functools.partial(local,nd,nt),mesh=mesh,
        in_specs=(row,col,col,col,rw,col,col,rw,P(),P(),P(),P(),row,P('dp',None),P('dp',None)),
        out_specs=(row,row,col,col,col,rw,col,col,rw,P(),P(),P(),P()),check_vma=False)
```

```python
import functools, math
import jax, jax.numpy as jnp
from jax import lax
from jax.sharding import PartitionSpec as P
from jax.experimental import pallas as pl
from jax.experimental.pallas import tpu as pltpu
HD=128
EPS=1e-6
F32=jnp.float32; BF=jnp.bfloat16
NT=(((1,),(1,)),((),()))
TN=(((0,),(0,)),((),()))
NN=(((1,),(0,)),((),()))
def dot(a,b,dims=NN): return lax.dot_general(a,b,dims,preferred_element_type=F32)
LOG2E=math.log2(math.e)

def attn_fwd_kernel(bq,bk,ratio,scale,lo_ref,q_ref,k_ref,v_ref,end_ref,o_ref,l_ref,vx_ref,acc_ref):
    i=pl.program_id(1)
    n=k_ref.shape[0]
    @pl.when(i==0)
    def _():
        vx_ref[:,:HD]=v_ref[...]
        vx_ref[:,HD:]=jnp.ones((n,HD),BF)
    q=q_ref[...]
    qs=jnp.concatenate([q[:,h*HD:(h+1)*HD] for h in range(ratio)],0)
    rows=lax.rem(lax.broadcasted_iota(jnp.int32,(ratio*bq,1),0),bq)+i*bq
    acc_ref[...]=jnp.zeros_like(acc_ref)
    c=scale*LOG2E
    def step(j,_):
        b=pl.multiple_of(j*bk,bk)
        s=dot(qs,k_ref[pl.ds(b,bk),:],NT)
        cols=lax.broadcasted_iota(jnp.int32,(1,bk),1)+b
        m=(rows>=cols)&(rows<end_ref[:,pl.ds(b,bk)])
        e=jnp.where(m,jnp.exp2(s*c),0.0).astype(BF)
        acc_ref[...]+=dot(e,vx_ref[pl.ds(b,bk),:])
        return 0
    lax.fori_loop(lo_ref[i],(i*bq+bq-1)//bk+1,step,0)
    a=acc_ref[...]
    l=a[:,HD:]
    o=(a[:,:HD]/l).astype(BF)
    lt=jnp.log2(l).T[0:1]
    for h in range(ratio):
        o_ref[:,h*HD:(h+1)*HD]=o[h*bq:(h+1)*bq]
        l_ref[0,h:h+1,:]=lt[:,h*bq:(h+1)*bq]

def attn_fwd(q,k,v,end,lo,bq,bk,scale):
    n,wq=q.shape; g=k.shape[1]//HD; ratio=wq//HD//g
    gs=pltpu.PrefetchScalarGridSpec(num_scalar_prefetch=1,grid=(g,n//bq),
        in_specs=[pl.BlockSpec((bq,ratio*HD),lambda g,i,lo:(i,g)),
                  pl.BlockSpec((n,HD),lambda g,i,lo:(0,g)),
                  pl.BlockSpec((n,HD),lambda g,i,lo:(0,g)),
                  pl.BlockSpec((1,n),lambda g,i,lo:(0,0))],
        out_specs=[pl.BlockSpec((bq,ratio*HD),lambda g,i,lo:(i,g)),
                   pl.BlockSpec((1,ratio,bq),lambda g,i,lo:(g,0,i))],
        scratch_shapes=[pltpu.VMEM((n,2*HD),BF),pltpu.VMEM((ratio*bq,2*HD),F32)])
    return pl.pallas_call(functools.partial(attn_fwd_kernel,bq,bk,ratio,scale),grid_spec=gs,
        out_shape=[jax.ShapeDtypeStruct((n,wq),BF),jax.ShapeDtypeStruct((g,ratio,n),F32)],name='attn_fwd')(lo,q,k,v,end)

def norm_rot_bwd(d,raw,gain,cos,sin):
    du=d*cos-pltpu.roll(d,HD//2,1)*sin
    r=lax.rsqrt(jnp.mean(raw*raw,-1,keepdims=True)+EPS)
    xh=raw*r
    ge=du*gain
    dx=r*(ge-xh*jnp.mean(xh*ge,-1,keepdims=True))
    return dx,jnp.sum(du*xh,0,keepdims=True)

def attn_bwd_kernel(bq,bk,ratio,scale,lo_ref,q_ref,k_ref,v_ref,do_ref,o_ref,l_ref,start_ref,qraw_ref,kraw_ref,cos_ref,sin_ref,gq_ref,gk_ref,
                    wa_ref,wb_ref,wc_ref,dq_ref,dk_ref,dv_ref,dgq_ref,dgk_ref,wa_o,wb_o,wc_o,dka,dva,dqa):
    wa_o[...]=wa_ref[...].astype(F32); wb_o[...]=wb_ref[...].astype(F32); wc_o[...]=wc_ref[...].astype(F32)
    g=pl.program_id(0); i=pl.program_id(1); nb=pl.num_programs(1)
    @pl.when(i==0)
    def _():
        dka[...]=jnp.zeros_like(dka); dva[...]=jnp.zeros_like(dva)
    @pl.when((i==0)&(g==0))
    def _():
        dgq_ref[...]=jnp.zeros_like(dgq_ref); dgk_ref[...]=jnp.zeros_like(dgk_ref)
    q=q_ref[...]; do=do_ref[...]
    qs=jnp.concatenate([q[:,h*HD:(h+1)*HD] for h in range(ratio)],0)
    ds_=jnp.concatenate([do[:,h*HD:(h+1)*HD] for h in range(ratio)],0)
    pr=do.astype(F32)*o_ref[...].astype(F32)
    prs=jnp.concatenate([pr[:,h*HD:(h+1)*HD] for h in range(ratio)],0)
    D=jnp.sum(prs.T,0,keepdims=True)
    lse=jnp.concatenate([l_ref[0,h:h+1,:] for h in range(ratio)],1)
    st=start_ref[...]
    st=jnp.concatenate([st]*ratio,1)
    cols=lax.rem(lax.broadcasted_iota(jnp.int32,(1,ratio*bq),1),bq)+i*bq
    dqa[...]=jnp.zeros_like(dqa)
    c=scale*LOG2E
    def step(j,_):
        b=pl.multiple_of(j*bk,bk)
        kb=k_ref[pl.ds(b,bk),:]; vb=v_ref[pl.ds(b,bk),:]
        s=dot(kb,qs,NT)
        rows=lax.broadcasted_iota(jnp.int32,(bk,1),0)+b
        m=(cols>=rows)&(st<=rows)
        p=jnp.where(m,jnp.exp2(s*c-lse),0.0)
        dp=dot(vb,ds_,NT)
        dsT=(p*(dp-D)).astype(BF)
        dva[pl.ds(b,bk),:]+=dot(p.astype(BF),ds_)
        dka[pl.ds(b,bk),:]+=dot(dsT,qs)
        dqa[...]+=dot(dsT,kb,TN)
        return 0
    lax.fori_loop(lo_ref[i],(i*bq+bq-1)//bk+1,step,0)
    r0=pl.multiple_of(i*bq,bq)
    cos=cos_ref[pl.ds(r0,bq),:]; sin=sin_ref[pl.ds(r0,bq),:]
    gq=gq_ref[...]
    tot=jnp.zeros((1,HD),F32)
    for h in range(ratio):
        dx,dg=norm_rot_bwd(dqa[h*bq:(h+1)*bq,:]*scale,qraw_ref[:,h*HD:(h+1)*HD],gq,cos,sin)
        dq_ref[:,h*HD:(h+1)*HD]=dx.astype(BF)
        tot=tot+dg
    dgq_ref[...]+=tot
    @pl.when(i==nb-1)
    def _():
        gk=gk_ref[...]
        def fin(t,acc):
            r=pl.multiple_of(t*bq,bq)
            dx,dg=norm_rot_bwd(dka[pl.ds(r,bq),:]*scale,kraw_ref[pl.ds(r,bq),:],gk,cos_ref[pl.ds(r,bq),:],sin_ref[pl.ds(r,bq),:])
            dk_ref[pl.ds(r,bq),:]=dx.astype(BF)
            dv_ref[pl.ds(r,bq),:]=dva[pl.ds(r,bq),:].astype(BF)
            return acc+dg
        dgk_ref[...]+=lax.fori_loop(0,dka.shape[0]//bq,fin,jnp.zeros((1,HD),F32))

def attn_bwd(q,k,v,do,o,l,start,lo,qraw,kraw,cos,sin,gq,gk,wide,bq,bk,scale):
    n,wq=q.shape; wk=k.shape[1]; g=wk//HD; ratio=wq//HD//g
    qs=pl.BlockSpec((bq,ratio*HD),lambda g,i,lo:(i,g))
    ks=pl.BlockSpec((n,HD),lambda g,i,lo:(0,g))
    full=pl.BlockSpec((n,HD),lambda g,i,lo:(0,0))
    one=pl.BlockSpec((1,HD),lambda g,i,lo:(0,0))
    nb=n//bq
    ws=[pl.BlockSpec((w.shape[0]//(g*nb),w.shape[1]),lambda g,i,lo: (g*nb+i,0)) for w in wide]
    gs=pltpu.PrefetchScalarGridSpec(num_scalar_prefetch=1,grid=(g,nb),
        in_specs=[qs,ks,ks,qs,qs,pl.BlockSpec((1,ratio,bq),lambda g,i,lo:(g,0,i)),pl.BlockSpec((1,bq),lambda g,i,lo:(0,i)),
                  qs,ks,full,full,one,one]+ws,
        out_specs=[qs,ks,ks,one,one]+ws,
        scratch_shapes=[pltpu.VMEM((n,HD),F32),pltpu.VMEM((n,HD),F32),pltpu.VMEM((ratio*bq,HD),F32)])
    return pl.pallas_call(functools.partial(attn_bwd_kernel,bq,bk,ratio,scale),grid_spec=gs,
        out_shape=[jax.ShapeDtypeStruct((n,wq),BF),jax.ShapeDtypeStruct((n,wk),BF),jax.ShapeDtypeStruct((n,wk),BF),
                   jax.ShapeDtypeStruct((1,HD),F32),jax.ShapeDtypeStruct((1,HD),F32)]+[jax.ShapeDtypeStruct(w.shape,F32) for w in wide],name='attn_bwd')(lo,q,k,v,do,o,l,start,qraw,kraw,cos,sin,gq,gk,*wide)

def norm_rot(raw,gain,cos,sin):
    u=raw*lax.rsqrt(jnp.mean(raw*raw,-1,keepdims=True)+EPS)*gain
    return u*cos+pltpu.roll(u,HD//2,1)*sin


MESH=pl.DeviceIdType.MESH
def ring_neighbours(d):
    me=lax.axis_index('dp')
    half=d//2
    odd=lax.rem(me,2); up=me//2
    pos=odd*(d-1-2*up)+up
    def at(p):
        hi=p//half
        return hi*(2*(d-1-p)+1)+(1-hi)*2*p
    return pos,at(lax.rem(pos+1,d)),at(lax.rem(pos+d-1,d))


def group():
    t=lax.axis_index('tensor')
    mate=t+1-2*lax.rem(t,2)
    return t,mate,lax.rem(t+2,4),lax.rem(mate+2,4)

def greet(*peers):
    barrier=pltpu.get_barrier_semaphore()
    for p in peers:
        pl.semaphore_signal(barrier,inc=1,device_id={'tensor':p},device_id_type=MESH)
    pl.semaphore_wait(barrier,len(peers))

def send(src,dst,ss,rs,peer,axis='tensor'):
    return pltpu.make_async_remote_copy(src_ref=src,dst_ref=dst,send_sem=ss,recv_sem=rs,device_id={axis:peer},device_id_type=MESH)

def rows_of(ref,b,j,r,per):
    return ref.at[pl.ds(pl.multiple_of(b*per+j*r,r),r)]

def front_kernel(nc,x_ref,pos_ref,fr_ref,g_ref,wq_ref,wk_ref,wv_ref,gq_ref,gk_ref,
                 a_o,q_o,k_o,v_o,qr_o,kr_o,cos_o,sin_o,
                 xf,a_s,q_s,k_s,v_s,qr_s,kr_s,cos_s,sin_s,lsem,osem,ss,rs):
    t,mate,far,diag=group()
    per=x_ref.shape[0]; r=per//nc; n=xf.shape[0]
    outs=[(a_s,a_o),(q_s,q_o),(k_s,k_o),(v_s,v_o),(qr_s,qr_o),(kr_s,kr_o)]
    own=pltpu.make_async_copy(x_ref,rows_of(xf,t,0,per,per),lsem)
    own.start()
    greet(mate,far)
    tof=[send(x_ref.at[j*r:(j+1)*r],rows_of(xf,t,j,r,per),ss.at[0,j],rs.at[0,j],far) for j in range(nc)]
    tom=[send(x_ref.at[j*r:(j+1)*r],rows_of(xf,t,j,r,per),ss.at[1,j],rs.at[1,j],mate) for j in range(nc)]
    fwd=[send(rows_of(xf,far,j,r,per),rows_of(xf,far,j,r,per),ss.at[2,j],rs.at[2,j],mate) for j in range(nc)]
    for j in range(nc):
        tof[j].start(); tom[j].start()
    gain=g_ref[...]; gq=gq_ref[...]; gk=gk_ref[...]
    tt=256
    def table(i,_):
        p=pl.multiple_of(i*tt,tt)
        ang=pos_ref[pl.ds(p,tt),:]*fr_ref[...]
        cos_s[pl.ds(p,tt),:]=jnp.cos(ang)
        sn=jnp.sin(ang)
        lane=lax.broadcasted_iota(jnp.int32,sn.shape,1)
        sin_s[pl.ds(p,tt),:]=jnp.where(lane<HD//2,-sn,sn)
        return 0
    lax.fori_loop(0,n//tt,table,0)
    tabs=[pltpu.make_async_copy(cos_s,cos_o,osem.at[6,0]),pltpu.make_async_copy(sin_s,sin_o,osem.at[7,0])]
    for c in tabs: c.start()
    def tile(b,j):
        p=pl.multiple_of(b*per+j*r,r)
        rows=pl.ds(p,r)
        x=xf[rows,:].astype(F32)
        a=(x*lax.rsqrt(jnp.mean(x*x,-1,keepdims=True)+EPS)*gain).astype(BF)
        a_s[rows,:]=a
        qr=dot(a,wq_ref[...]); kr=dot(a,wk_ref[...])
        v_s[rows,:]=dot(a,wv_ref[...]).astype(BF)
        qr_s[rows,:]=qr; kr_s[rows,:]=kr
        cos=cos_s[rows,:]; sin=sin_s[rows,:]
        for h in range(qr.shape[1]//HD):
            q_s[rows,h*HD:(h+1)*HD]=norm_rot(qr[:,h*HD:(h+1)*HD],gq,cos,sin).astype(BF)
        for h in range(kr.shape[1]//HD):
            k_s[rows,h*HD:(h+1)*HD]=norm_rot(kr[:,h*HD:(h+1)*HD],gk,cos,sin).astype(BF)
        for o,(s,d) in enumerate(outs):
            pltpu.make_async_copy(s.at[rows],d.at[rows],osem.at[o,b*nc+j]).start()
    def loop(b):
        def body(j,_):
            tile(b,j); return 0
        lax.fori_loop(0,nc,body,0)
    own.wait()
    loop(t)
    for j in range(nc): tom[j].wait_recv()
    loop(mate)
    def body(j,_):
        send(rows_of(xf,far,j,r,per),rows_of(xf,far,j,r,per),ss.at[0,j],rs.at[0,j],far).wait_recv()
        send(rows_of(xf,far,j,r,per),rows_of(xf,far,j,r,per),ss.at[2,j],rs.at[2,j],mate).start()
        tile(far,j)
        send(rows_of(xf,far,j,r,per),rows_of(xf,far,j,r,per),ss.at[2,j],rs.at[2,j],mate).wait_recv()
        tile(diag,j)
        return 0
    lax.fori_loop(0,nc,body,0)
    for j in range(nc):
        tof[j].wait_send(); tom[j].wait_send(); fwd[j].wait_send()
    def drain(i,_):
        rows=pl.ds(pl.multiple_of(i*r,r),r)
        for o,(s,d) in enumerate(outs):
            pltpu.make_async_copy(s.at[rows],d.at[rows],osem.at[o,i]).wait()
        return 0
    lax.fori_loop(0,n//r,drain,0)
    for c in tabs: c.wait()

def front(x,posb,freqs,gain,wq,wk,wv,gq,gk,nc,cid):
    n=4*x.shape[0]; d=x.shape[1]
    S=jax.ShapeDtypeStruct
    V=pl.BlockSpec(memory_space=pltpu.VMEM); A=pl.BlockSpec(memory_space=pl.ANY)
    shapes=[((n,d),BF),((n,wq.shape[1]),BF),((n,wk.shape[1]),BF),((n,wv.shape[1]),BF),((n,wq.shape[1]),F32),((n,wk.shape[1]),F32),((n,HD),F32),((n,HD),F32)]
    return pl.pallas_call(functools.partial(front_kernel,nc),in_specs=[A]+[V]*8,out_specs=[A]*8,out_shape=[S(*s) for s in shapes],
        scratch_shapes=[pltpu.VMEM((n,d),BF)]+[pltpu.VMEM(*s) for s in shapes]+[pltpu.SemaphoreType.DMA,pltpu.SemaphoreType.DMA((8,4*nc)),pltpu.SemaphoreType.DMA((3,nc)),pltpu.SemaphoreType.DMA((3,nc))],
        compiler_params=pltpu.CompilerParams(collective_id=cid,has_side_effects=True,vmem_limit_bytes=60<<20),name='front')(x,posb,freqs,gain,wq,wk,wv,gq,gk)

def mid_kernel(nc,att_ref,wo_ref,x_ref,dy_ref,wg_ref,wu_ref,wd_ref,g_ref,
               hid_ref,a_o,act_o,dg_o,du_o,op_o,da_o,
               attv,wov,dyv,wgv,wuv,wdv,full,act_s,dg_s,du_s,op_s,da_s,acc,pbuf,rbuf,fbuf,ybuf,lsem,osem,ss,rs):
    t,mate,far,diag=group()
    per=x_ref.shape[0]; r=per//nc; n=full.shape[0]
    loads=[pltpu.make_async_copy(s,d,lsem.at[i]) for i,(s,d) in enumerate(((att_ref,attv),(wo_ref,wov),(dy_ref,dyv),(wg_ref,wgv),(wu_ref,wuv),(wd_ref,wdv)))]
    for c in loads: c.start()
    greet(mate,far)
    outs=[(full,a_o),(act_s,act_o),(dg_s,dg_o),(du_s,du_o),(op_s,op_o),(da_s,da_o)]
    gain=g_ref[...]
    def proj(b,j):
        return dot(rows_of(attv,b,j,r,per)[...],wov[...])
    def to_mate(i,j):
        return send(pbuf.at[i,pl.ds(pl.multiple_of(j*r,r),r)],rbuf.at[i,pl.ds(pl.multiple_of(j*r,r),r)],ss.at[i,j],rs.at[i,j],mate)
    def to_far(j):
        rr=pl.ds(pl.multiple_of(j*r,r),r)
        return send(fbuf.at[rr],ybuf.at[rr],ss.at[2,j],rs.at[2,j],far)
    def share(j,i,peer):
        return send(rows_of(full,t,j,r,per),rows_of(full,t,j,r,per),ss.at[i,j],rs.at[i,j],peer)
    def forward(j):
        return send(rows_of(full,far,j,r,per),rows_of(full,far,j,r,per),ss.at[5,j],rs.at[5,j],mate)
    loads[0].wait(); loads[1].wait()
    def reduce(j,_):
        rr=pl.ds(pl.multiple_of(j*r,r),r)
        pbuf[1,rr,:]=proj(diag,j).astype(BF); to_mate(1,j).start()
        pbuf[0,rr,:]=proj(mate,j).astype(BF); to_mate(0,j).start()
        f=proj(far,j)
        to_mate(1,j).wait_recv()
        fbuf[rr,:]=(f+rbuf[1,rr,:].astype(F32)).astype(BF)
        to_far(j).start()
        o=proj(t,j)
        to_mate(0,j).wait_recv()
        acc[rr,:]=o+rbuf[0,rr,:].astype(F32)+x_ref[rr,:].astype(F32)
        return 0
    lax.fori_loop(0,nc,reduce,0)
    for i in range(2,6): loads[i].wait()
    def mlp_rows(b,j):
        rows=pl.ds(pl.multiple_of(b*per+j*r,r),r)
        a=full[rows,:]
        gate=dot(a,wgv[...]); up=dot(a,wuv[...])
        dact=dot(dyv[rows,:],wdv[...],NT)
        sig=1.0/(1.0+jnp.exp(-gate))
        sl=gate*sig
        act=(sl*up).astype(BF)
        act_s[rows,:]=act
        dg=(dact*up*(sig*(1.0+gate*(1.0-sig)))).astype(BF)
        du=(dact*sl).astype(BF)
        dg_s[rows,:]=dg; du_s[rows,:]=du
        op_s[rows,:]=dot(act,wdv[...]).astype(BF)
        da_s[rows,:]=(dot(dg,wgv[...],NT)+dot(du,wuv[...],NT)).astype(BF)
        for o,(s,d) in enumerate(outs):
            pltpu.make_async_copy(s.at[rows],d.at[rows],osem.at[o,b*nc+j]).start()
    def near(j,_):
        rr=pl.ds(pl.multiple_of(j*r,r),r)
        to_far(j).wait_recv()
        h=acc[rr,:]+ybuf[rr,:].astype(F32)
        hid_ref[rr,:]=h
        rows_of(full,t,j,r,per)[...]=(h*lax.rsqrt(jnp.mean(h*h,-1,keepdims=True)+EPS)*gain).astype(BF)
        share(j,3,far).start(); share(j,4,mate).start()
        def both(i,_):
            @pl.when(i==1)
            def _(): share(j,4,mate).wait_recv()
            mlp_rows(t+i*(mate-t),j)
            return 0
        lax.fori_loop(0,2,both,0)
        return 0
    lax.fori_loop(0,nc,near,0)
    def away(j,_):
        share(j,3,far).wait_recv()
        forward(j).start()
        def both(i,_):
            @pl.when(i==1)
            def _(): forward(j).wait_recv()
            mlp_rows(far+i*(diag-far),j)
            return 0
        lax.fori_loop(0,2,both,0)
        return 0
    lax.fori_loop(0,nc,away,0)
    def drain(j,_):
        to_mate(0,j).wait_send(); to_mate(1,j).wait_send(); to_far(j).wait_send()
        share(j,3,far).wait_send(); share(j,4,mate).wait_send(); forward(j).wait_send()
        return 0
    lax.fori_loop(0,nc,drain,0)
    def flush(i,_):
        rows=pl.ds(pl.multiple_of(i*r,r),r)
        for o,(s,d) in enumerate(outs):
            pltpu.make_async_copy(s.at[rows],d.at[rows],osem.at[o,i]).wait()
        return 0
    lax.fori_loop(0,n//r,flush,0)

def middle(att,wo,x,dy,wg,wu,wd,gain,nc,cid):
    n=att.shape[0]; per,d=x.shape; f=wg.shape[1]
    S=jax.ShapeDtypeStruct
    V=pl.BlockSpec(memory_space=pltpu.VMEM); A=pl.BlockSpec(memory_space=pl.ANY)
    rows=[((n,d),BF),((n,f),BF),((n,f),BF),((n,f),BF),((n,d),BF),((n,d),BF)]
    return pl.pallas_call(functools.partial(mid_kernel,nc),in_specs=[A,A,V,A,A,A,A,V],out_specs=[V]+[A]*6,out_shape=[S((per,d),F32)]+[S(*s) for s in rows],
        scratch_shapes=[pltpu.VMEM(a.shape,BF) for a in (att,wo,dy,wg,wu,wd)]+[pltpu.VMEM(*s) for s in rows]+
            [pltpu.VMEM((per,d),F32),pltpu.VMEM((2,per,d),BF),pltpu.VMEM((2,per,d),BF),pltpu.VMEM((per,d),BF),pltpu.VMEM((per,d),BF),
             pltpu.SemaphoreType.DMA((6,)),pltpu.SemaphoreType.DMA((6,4*nc)),pltpu.SemaphoreType.DMA((6,nc)),pltpu.SemaphoreType.DMA((6,nc))],
        compiler_params=pltpu.CompilerParams(collective_id=cid,has_side_effects=True,vmem_limit_bytes=62<<20),name='middle')(att,wo,x,dy,wg,wu,wd,gain)

class Ring:
    def __init__(self,d,k,own,full,sbuf,recv,g,ssem,rsem,asem,bsem,subs):
        self.d,self.k,self.rc=d,k,k//d
        self.own,self.full,self.sbuf,self.recv,self.g=own,full,sbuf,recv,g
        self.sem=(ssem,rsem,asem,bsem); self.subs=subs
        self.pos,right,left=ring_neighbours(d)
        self.to=(right,left)
    @staticmethod
    def scratch(d,k,w,nsub):
        rc=k//d
        fused=rc%128==0
        return [pltpu.VMEM((2,rc,w),BF),pltpu.VMEM((2,d-1,rc,w),BF),pltpu.VMEM((2,k,w),BF)]+[pltpu.SemaphoreType.DMA((2,nsub,d-1))]*4+([] if fused else [pltpu.VMEM((2,k,w),BF)])
    def chunk(self,s,k): return lax.rem(self.pos-k+2*self.d,self.d) if s==0 else lax.rem(self.pos+k,self.d)
    def prepare(self):
        if self.rc%128:
            for s in range(2):
                def tile(i,_):
                    self.own(s,i*128,lambda lo,hi,v: self.store_full(s,i,lo,hi,v),128)
                    return 0
                lax.fori_loop(0,self.k//128,tile,0)
    def store_full(self,s,i,lo,hi,v): self.full[s,pl.ds(pl.multiple_of(i*128,128),128),lo:hi]=v.astype(BF)
    def part(self,s,c,put):
        if self.rc%128==0: self.own(s,c*self.rc,put,self.rc)
        else:
            w=self.subs[-1]
            put(0,w,self.full[s,pl.ds(pl.multiple_of(c*self.rc,self.rc),self.rc),:].astype(F32))
    def rs(self,s,u,k,src):
        lo,hi=self.subs[u],self.subs[u+1]
        return pltpu.make_async_remote_copy(src_ref=src.at[:,lo:hi],dst_ref=self.recv.at[s,k,:,lo:hi],send_sem=self.sem[0].at[s,u,k],recv_sem=self.sem[1].at[s,u,k],
            device_id={'dp':self.to[s]},device_id_type=MESH)
    def ag(self,s,u,k,c):
        lo,hi=self.subs[u],self.subs[u+1]
        ref=self.g.at[s,pl.ds(pl.multiple_of(c*self.rc,self.rc),self.rc),lo:hi]
        return pltpu.make_async_remote_copy(src_ref=ref,dst_ref=ref,send_sem=self.sem[2].at[s,u,k],recv_sem=self.sem[3].at[s,u,k],
            device_id={'dp':self.to[s]},device_id_type=MESH)
    def units(self): return [(s,u) for u in range(len(self.subs)-1) for s in range(2)]
    def start(self):
        for s in range(2):
            def put(lo,hi,v,s=s): self.sbuf[s,:,lo:hi]=v.astype(BF)
            self.part(s,self.chunk(s,0),put)
        for s,u in self.units(): self.rs(s,u,0,self.sbuf.at[s]).start()
    def reduce_step(self,k,ownbuf):
        for s in range(2):
            def put(lo,hi,v,s=s): ownbuf[s,:,lo:hi]=v
            self.part(s,self.chunk(s,k),put)
        for s,u in self.units():
            lo,hi=self.subs[u],self.subs[u+1]
            self.rs(s,u,k-1,self.sbuf.at[s]).wait_recv()
            val=(ownbuf[s,:,lo:hi]+self.recv[s,k-1,:,lo:hi].astype(F32)).astype(BF)
            @pl.when(k<self.d-1)
            def _():
                self.recv[s,k-1,:,lo:hi]=val
                self.rs(s,u,k,self.recv.at[s,k-1]).start()
            @pl.when(k==self.d-1)
            def _():
                c=self.chunk(s,k)
                self.g[s,pl.ds(pl.multiple_of(c*self.rc,self.rc),self.rc),lo:hi]=val
                self.ag(s,u,0,c).start()
    def gather_step(self,k):
        for s,u in self.units():
            c=self.chunk(s,k-1)
            self.ag(s,u,k-1,c).wait_recv()
            @pl.when(k<self.d-1)
            def _(): self.ag(s,u,k,c).start()
    def drain(self):
        def body(k,_):
            for s,u in self.units():
                self.rs(s,u,k,self.sbuf.at[s]).wait_send()
                self.ag(s,u,k,0).wait_send()
            return 0
        lax.fori_loop(0,self.d-1,body,0)

def greet_all(peers):
    barrier=pltpu.get_barrier_semaphore()
    for axis,p in peers:
        pl.semaphore_signal(barrier,inc=1,device_id={axis:p},device_id_type=MESH)
    pl.semaphore_wait(barrier,len(peers))

def each_rows(n,f,step=64):
    def body(i,_):
        f(pl.ds(pl.multiple_of(i*step,step),step))
        return 0
    lax.fori_loop(0,n//step,body,0)

class Scatter:
    def __init__(self,ids,per,rbuf,fbuf,ybuf,acc,ss,rs):
        self.t,self.mate,self.far,self.diag=ids
        self.per=per; self.rbuf,self.fbuf,self.ybuf,self.acc,self.ss,self.rs=rbuf,fbuf,ybuf,acc,ss,rs
    @staticmethod
    def scratch(per,w): return [pltpu.VMEM((2,per,w),BF),pltpu.VMEM((per,w),BF),pltpu.VMEM((per,w),BF),pltpu.VMEM((per,w),F32),pltpu.SemaphoreType.DMA((3,)),pltpu.SemaphoreType.DMA((3,))]
    def to_mate(self,i,src): return send(src,self.rbuf.at[i],self.ss.at[i],self.rs.at[i],self.mate)
    def across(self): return send(self.fbuf,self.ybuf,self.ss.at[2],self.rs.at[2],self.far)
    def pair(self,far_part,own_part):
        self.to_mate(1,self.fbuf).wait_recv()
        def far_rows(r): self.fbuf[r,:]=(far_part[r,:].astype(F32)+self.rbuf[1,r,:].astype(F32)).astype(BF)
        each_rows(self.per,far_rows)
        self.to_mate(0,self.fbuf).wait_recv()
        def own_rows(r): self.acc[r,:]=own_part[r,:].astype(F32)+self.rbuf[0,r,:].astype(F32)
        each_rows(self.per,own_rows)
    def result(self,f):
        self.across().wait_recv()
        each_rows(self.per,lambda r: f(r,self.acc[r,:]+self.ybuf[r,:].astype(F32)))
    def drain(self):
        self.to_mate(0,self.fbuf).wait_send(); self.to_mate(1,self.fbuf).wait_send(); self.across().wait_send()

def norm_bwd(v,gain,e):
    r=lax.rsqrt(jnp.mean(v*v,-1,keepdims=True)+EPS)
    vh=v*r
    ge=e*gain
    return r*(ge-vh*jnp.mean(vh*ge,-1,keepdims=True)),jnp.sum(e*vh,0,keepdims=True)

def when_each(k,table):
    for at,f in table:
        pl.when(k==at)(f)

def post_kernel(d,fused,hid_ref,cot_ref,g_ref,wo_ref,a_ref,dy_ref,act_ref,dg_ref,du_ref,op_ref,da_ref,
                out_ref,dhid_ref,gg_ref,dwg_ref,dwu_ref,dwd_ref,dhf_o,dout_o,
                av,dyv,actv,dgv,duv,full,doutv,parts,ownbuf,lsem,osem,ss,rs,*rest):
    ids=t,mate,far,diag=group()
    per,dm=hid_ref.shape; n=full.shape[0]; f=dgv.shape[1]; h=f//2
    nr=7+(not fused)
    rs1=Scatter(ids,per,*rest[:6]); rs2=Scatter(ids,per,*rest[6:12])
    rr=rest[12:]
    def own(s,c,put,w):
        cs=pl.ds(pl.multiple_of(c,w),w)
        put(0,f,dot(av[:,cs],(dgv,duv)[s][...],TN))
        put(f,f+h,dot(dyv[:,cs],actv[:,s*h:(s+1)*h],TN))
    ring=Ring(d,dm,own,None if fused else rr[7],rr[0],rr[1],rr[2],rr[3],rr[4],rr[5],rr[6],(0,h,f,f+h))
    loads=[pltpu.make_async_copy(s,x,lsem.at[i]) for i,(s,x) in enumerate(((a_ref,av),(dg_ref,dgv),(du_ref,duv),(dy_ref,dyv),(act_ref,actv)))]
    blk=lambda ref,b: rows_of(ref,b,0,per,per)
    locals_=[pltpu.make_async_copy(blk(s,b),parts.at[i%2],lsem.at[5+i]) for i,(s,b) in enumerate(((da_ref,far),(da_ref,t),(op_ref,far),(op_ref,t)))]
    for c in loads+locals_[:2]: c.start()
    greet_all([('tensor',mate),('tensor',far),('dp',ring.to[0]),('dp',ring.to[1])])
    pair1=[rs1.to_mate(1,blk(da_ref,diag)),rs1.to_mate(0,blk(da_ref,mate))]
    pair2=[rs2.to_mate(1,blk(op_ref,diag)),rs2.to_mate(0,blk(op_ref,mate))]
    for c in pair1: c.start()
    for c in loads: c.wait()
    ring.prepare()
    ring.start()
    share=lambda i,p: send(blk(full,t),blk(full,t),ss.at[i],rs.at[i],p)
    forward=lambda: send(blk(full,far),blk(full,far),ss.at[2],rs.at[2],mate)
    def e1():
        locals_[0].wait(); locals_[1].wait()
        rs1.pair(parts.at[0],parts.at[1])
        rs1.across().start()
        for c in pair2+locals_[2:]: c.start()
    def e2():
        gg_ref[...]=jnp.zeros_like(gg_ref)
        mine=blk(full,t)
        def rows(r,da):
            dh,gg=norm_bwd(hid_ref[r,:],g_ref[...],da)
            dh=dh+cot_ref[r,:].astype(F32)
            dhid_ref[r,:]=dh; gg_ref[...]+=gg
            mine[r,:]=dh.astype(BF)
        rs1.result(rows)
        share(0,far).start(); share(1,mate).start()
    def e3():
        locals_[2].wait(); locals_[3].wait()
        rs2.pair(parts.at[0],parts.at[1])
    def e4():
        share(0,far).wait_recv()
        forward().start()
        rs2.across().start()
        share(1,mate).wait_recv()
        pltpu.make_async_copy(blk(full,t),blk(dhf_o,t),osem.at[0]).start()
    tt=256
    def dout_tiles(lo,hi):
        def tile(i,_):
            rows=pl.ds(pl.multiple_of(i*tt,tt),tt)
            doutv[rows,:]=dot(full[rows,:],wo_ref[...],NT).astype(BF)
            pltpu.make_async_copy(doutv.at[rows],dout_o.at[rows],osem.at[4+i]).start()
            return 0
        lax.fori_loop(lo,hi,tile,0)
    def e5():
        forward().wait_recv()
        for i,b in ((1,mate),(2,far),(3,diag)):
            pltpu.make_async_copy(blk(full,b),blk(dhf_o,b),osem.at[i]).start()
    def e6():
        def rows(r,v): out_ref[r,:]=(hid_ref[r,:]+v).astype(BF)
        rs2.result(rows)
    nt_=n//tt
    def step(k,_):
        when_each(k,((1,e1),(3,e3),(5,e2)))
        ring.reduce_step(k,ownbuf)
        return 0
    lax.fori_loop(1,d,step,0)
    def emit(s,c):
        rows=pl.ds(pl.multiple_of(c*ring.rc,ring.rc),ring.rc)
        (dwg_ref,dwu_ref)[s][rows,:]=ring.g[s,rows,0:f]
        if fused: dwd_ref[s*h:(s+1)*h,rows]=ring.g[s,rows,f:f+h].T
    for s in range(2): emit(s,ring.chunk(s,d-1))
    def gstep(k,_):
        when_each(k,((2,e4),(3,e5),(4,lambda: dout_tiles(0,nt_//2)),(5,lambda: dout_tiles(nt_//2,nt_)),(6,e6)))
        ring.gather_step(k)
        for s in range(2): emit(s,ring.chunk(s,k-1))
        return 0
    lax.fori_loop(1,d,gstep,0)
    if not fused:
        for s in range(2):
            def tr(i,_):
                cs=pl.ds(pl.multiple_of(i*128,128),128)
                dwd_ref[s*h:(s+1)*h,cs]=ring.g[s,cs,f:f+h].T
                return 0
            lax.fori_loop(0,dm//128,tr,0)
    ring.drain(); rs1.drain(); rs2.drain()
    share(0,far).wait_send(); share(1,mate).wait_send(); forward().wait_send()
    for i,b in enumerate((t,mate,far,diag)): pltpu.make_async_copy(blk(full,b),blk(dhf_o,b),osem.at[i]).wait()
    def fin(i,_):
        rows=pl.ds(pl.multiple_of(i*tt,tt),tt)
        pltpu.make_async_copy(doutv.at[rows],dout_o.at[rows],osem.at[4+i]).wait()
        return 0
    lax.fori_loop(0,nt_,fin,0)

def post(hid,cot,gain,wo,a2,dy,act,dg,du,outp,dap,d,cid):
    per,dm=hid.shape; n=a2.shape[0]; f=act.shape[1]
    S=jax.ShapeDtypeStruct
    V=pl.BlockSpec(memory_space=pltpu.VMEM); A=pl.BlockSpec(memory_space=pl.ANY)
    fused=(dm//d)%128==0
    w=f+f//2
    D=pltpu.SemaphoreType.DMA
    return pl.pallas_call(functools.partial(post_kernel,d,fused),in_specs=[V]*4+[A]*7,out_specs=[V]*6+[A]*2,
        out_shape=[S((per,dm),BF),S((per,dm),F32),S((1,dm),F32),S((dm,f),BF),S((dm,f),BF),S((f,dm),BF),S((n,dm),BF),S((n,wo.shape[0]),BF)],
        scratch_shapes=[pltpu.VMEM((n,dm),BF),pltpu.VMEM((n,dm),BF)]+[pltpu.VMEM((n,f),BF)]*3+[pltpu.VMEM((n,dm),BF),pltpu.VMEM((n,wo.shape[0]),BF),pltpu.VMEM((2,per,dm),BF),
            pltpu.VMEM((2,dm//d,w),F32),D((9,)),D((4+n//256,)),D((3,)),D((3,))]+Scatter.scratch(per,dm)*2+Ring.scratch(d,dm,w,3),
        compiler_params=pltpu.CompilerParams(collective_id=cid,has_side_effects=True,vmem_limit_bytes=67043328),name='post')(hid,cot,gain,wo,a2,dy,act,dg,du,outp,dap)

def last_kernel(d,nt,fused,x_ref,dhid_ref,g_ref,gm_ref,gq_ref,gk_ref,wq_ref,wk_ref,wv_ref,dq_ref,dk_ref,dv_ref,a_ref,att_ref,dh_ref,
                dx_ref,dwq_ref,dwk_ref,dwv_ref,dwo_ref,ga_o,gm_o,gq_o,gk_o,
                dqv,dkv,dvv,av,attv,dhv,pbuf,farbuf,ownp,ownbuf,gbuf,grecv,lsem,gs,gr,*rest):
    ids=t,mate,far,diag=group()
    per,dm=x_ref.shape
    wq,wk,wv,wo=dqv.shape[1],dkv.shape[1],dvv.shape[1],attv.shape[1]
    sc=Scatter(ids,per,*rest[:6])
    rr=rest[6:]
    def own(s,c,put,w):
        cs=pl.ds(pl.multiple_of(c,w),w)
        if s==0:
            put(0,wq,dot(av[:,cs],dqv[...],TN)); put(wq,wq+wk,dot(av[:,cs],dkv[...],TN))
        else:
            put(0,wv,dot(av[:,cs],dvv[...],TN)); put(wv,wv+wo,dot(dhv[:,cs],attv[...],TN))
    u=(wq+wk)//3
    ring=Ring(d,dm,own,None if fused else rr[7],rr[0],rr[1],rr[2],rr[3],rr[4],rr[5],rr[6],(0,u,2*u,3*u))
    loads=[pltpu.make_async_copy(s,x,lsem.at[i]) for i,(s,x) in enumerate(((dq_ref,dqv),(dk_ref,dkv),(dv_ref,dvv),(a_ref,av),(att_ref,attv),(dh_ref,dhv)))]
    for c in loads: c.start()
    steps=[]
    for axis,n in (('tensor',nt),('dp',d)):
        b=1
        while b<n:
            steps.append((axis,b)); b*=2
    def partner(axis,b):
        me=lax.axis_index(axis)
        return me+b-2*b*lax.rem(me//b,2)
    greet_all([('tensor',mate),('tensor',far),('dp',ring.to[0]),('dp',ring.to[1])]+[(a,partner(a,b)) for a,b in steps])
    def part(b,ref,i):
        def tile(j,_):
            p=pl.multiple_of(j*128,128)
            rows=pl.ds(pl.multiple_of(b*per+j*128,128),128)
            v=dot(dqv[rows,:],wq_ref[...],NT)+dot(dkv[rows,:],wk_ref[...],NT)+dot(dvv[rows,:],wv_ref[...],NT)
            ref[i,pl.ds(p,128),:]=v.astype(ref.dtype)
            return 0
        lax.fori_loop(0,per//128,tile,0)
    for i in range(3): loads[i].wait()
    def both(i,_):
        part(diag+i*(mate-diag),pbuf,1-i)
        sc_send(1-i).start()
        return 0
    def sc_send(i): return send(pbuf.at[i],sc.rbuf.at[i],sc.ss.at[i],sc.rs.at[i],mate)
    lax.fori_loop(0,2,both,0)
    for i in range(3,6): loads[i].wait()
    ring.prepare()
    ring.start()
    def two(i,_):
        part(far+i*(t-far),farbuf,i)
        return 0
    lax.fori_loop(0,2,two,0)
    def e1():
        sc.pair(farbuf.at[0],farbuf.at[1])
        sc.across().start()
    def e2():
        gbuf[:,0:dm]=jnp.zeros((1,dm),F32)
        gbuf[:,dm:2*dm]=gm_ref[...]
        gbuf[:,2*dm:2*dm+HD]=gq_ref[...]
        gbuf[:,2*dm+HD:2*dm+2*HD]=gk_ref[...]
        def rows(r,e):
            dv,gg=norm_bwd(x_ref[r,:].astype(F32),g_ref[...],e)
            dx_ref[r,:]=dhid_ref[r,:]+dv
            gbuf[:,0:dm]+=gg
        sc.result(rows)
    def step(k,_):
        when_each(k,((1,e1),(d-1,e2)))
        ring.reduce_step(k,ownbuf)
        return 0
    lax.fori_loop(1,d,step,0)
    cps=[pltpu.make_async_remote_copy(src_ref=grecv.at[2*i+1],dst_ref=grecv.at[2*i],send_sem=gs.at[i],recv_sem=gr.at[i],device_id={a:partner(a,b)},device_id_type=MESH) for i,(a,b) in enumerate(steps)]
    def g_send(i):
        grecv[2*i+1]=gbuf[...]
        cps[i].start()
    def g_add(i):
        cps[i].wait_recv()
        gbuf[...]+=grecv[2*i]
    def turn(i):
        def f():
            if i>0: g_add(i-1)
            if i<len(steps): g_send(i)
        return f
    def emit(s,c):
        rows=pl.ds(pl.multiple_of(c*ring.rc,ring.rc),ring.rc)
        if s==0:
            dwq_ref[rows,:]=ring.g[0,rows,0:wq]; dwk_ref[rows,:]=ring.g[0,rows,wq:wq+wk]
        else:
            dwv_ref[rows,:]=ring.g[1,rows,0:wv]
            if fused: dwo_ref[:,rows]=ring.g[1,rows,wv:wv+wo].T
    for s in range(2): emit(s,ring.chunk(s,d-1))
    def gstep(k,_):
        when_each(k,[(i+1,turn(i)) for i in range(min(len(steps)+1,d-1))])
        ring.gather_step(k)
        for s in range(2): emit(s,ring.chunk(s,k-1))
        return 0
    lax.fori_loop(1,d,gstep,0)
    for i in range(d-1,len(steps)+1): turn(i)()
    if not fused:
        def tr(i,_):
            cs=pl.ds(pl.multiple_of(i*128,128),128)
            dwo_ref[:,cs]=ring.g[1,cs,wv:wv+wo].T
            return 0
        lax.fori_loop(0,dm//128,tr,0)
    ga_o[...]=gbuf[:,0:dm]; gm_o[...]=gbuf[:,dm:2*dm]; gq_o[...]=gbuf[:,2*dm:2*dm+HD]; gk_o[...]=gbuf[:,2*dm+HD:2*dm+2*HD]
    ring.drain(); sc_send(0).wait_send(); sc_send(1).wait_send(); sc.across().wait_send()
    for c in cps: c.wait_send()

def last(x,dhid,g,gm,gq,gk,wq,wk,wv,dq,dk,dv,a1,att,dhf,d,nt,cid):
    per,dm=x.shape; n=a1.shape[0]
    S=jax.ShapeDtypeStruct
    V=pl.BlockSpec(memory_space=pltpu.VMEM); A=pl.BlockSpec(memory_space=pl.ANY)
    fused=(dm//d)%128==0
    w=dq.shape[1]+dk.shape[1]
    assert dv.shape[1]+att.shape[1]==w
    D=pltpu.SemaphoreType.DMA
    ns=sum((s-1).bit_length() for s in (d,nt))
    row=lambda c: S((1,c),F32)
    return pl.pallas_call(functools.partial(last_kernel,d,nt,fused),in_specs=[V]*9+[A]*6,out_specs=[V]*9,
        out_shape=[S((per,dm),F32)]+[S((dm,v.shape[1]),BF) for v in (dq,dk,dv)]+[S((att.shape[1],dm),BF),row(dm),row(dm),row(HD),row(HD)],
        scratch_shapes=[pltpu.VMEM(v.shape,BF) for v in (dq,dk,dv,a1,att,dhf)]+[pltpu.VMEM((2,per,dm),BF),pltpu.VMEM((2,per,dm),F32),pltpu.VMEM((8,128),F32),
            pltpu.VMEM((2,dm//d,w),F32),pltpu.VMEM((1,2*dm+2*HD),F32),pltpu.VMEM((2*ns,1,2*dm+2*HD),F32),D((6,)),D((ns,)),D((ns,))]+Scatter.scratch(per,dm)+Ring.scratch(d,dm,w,3),
        compiler_params=pltpu.CompilerParams(collective_id=cid,has_side_effects=True,vmem_limit_bytes=62<<20),name='last')(x,dhid,g,gm,gq,gk,wq,wk,wv,dq,dk,dv,a1,att,dhf)


THETA=1000000.0
def gather(a): return lax.all_gather(a,'tensor',axis=0,tiled=True)

def local(nd,nt,tokens,w_query,w_key,w_value,w_out,w_gate,w_up,w_down,norm_attn,norm_mlp,norm_query,norm_key,cotangent,segments,positions):
    n=segments.shape[1]
    scale=HD**-0.5
    seg=segments.reshape(-1); pos=positions.reshape(-1)
    idx=jnp.arange(n,dtype=jnp.int32)
    start=idx-pos
    ends=jnp.sum((seg[None,:]<=jnp.arange(4,dtype=jnp.int32)[:,None]).astype(jnp.int32),1)
    end=jnp.sum(jnp.where(seg[None,:]==jnp.arange(4,dtype=jnp.int32)[:,None],ends[:,None],0),0)
    bq=512; bk=512
    lo=start[::bq]//bk
    freqs=THETA**(-jnp.arange(0,HD,2).astype(F32)/HD)
    freqs=jnp.concatenate([freqs,freqs])[None]
    posb=jnp.broadcast_to(pos.astype(F32)[:,None],(n,HD))
    row=lambda g: g.astype(F32)[None]
    g_attn,g_mlp,gq,gk=row(norm_attn),row(norm_mlp),row(norm_query),row(norm_key)
    a1,q,k,v,qraw,kraw,cos,sin=front(tokens,posb,freqs,g_attn,w_query,w_key,w_value,gq,gk,4,1)
    q,cot=lax.optimization_barrier((q,cotangent))
    dy=gather(cot)
    att,lse=attn_fwd(q,k,v,end[None],lo,bq,bk,scale)
    hid,a2,act,dg,du,outp,dap=middle(att,w_out,tokens,dy,w_gate,w_up,w_down,g_mlp,2,2)
    output,dhid,gm,dwg,dwu,dwd,dhf,dout=post(hid,cotangent,g_mlp,w_out,a2,dy,act,dg,du,outp,dap,nd,3)
    dq,dk,dv,dgq,dgk,dwg,dwu,dwd=attn_bwd(q,k,v,dout,att,lse,start[None],lo,qraw,kraw,cos,sin,gq,gk,(dwg,dwu,dwd),bq,bk,scale)
    d_tokens,dwq,dwk,dwv,dwo,ga,gm,gq,gk=last(tokens,dhid,g_attn,gm,dgq,dgk,w_query,w_key,w_value,dq,dk,dv,a1,att,dhf,nd,nt,4)
    up=lambda a: a.astype(F32)
    return (output,d_tokens,up(dwq),up(dwk),up(dwv),up(dwo),dwg,dwu,dwd,ga[0],gm[0],gq[0],gk[0])

def solution(mesh):
    nd,nt=mesh.shape['dp'],mesh.shape['tensor']
    row=P(('dp','tensor'),None); col=P(None,'tensor'); rw=P('tensor',None)
    return jax.shard_map(functools.partial(local,nd,nt),mesh=mesh,
        in_specs=(row,col,col,col,rw,col,col,rw,P(),P(),P(),P(),row,P('dp',None),P('dp',None)),
        out_specs=(row,row,col,col,col,rw,col,col,rw,P(),P(),P(),P()),check_vma=False)
```

```python
import functools, math
import numpy as np
import jax, jax.numpy as jnp
from jax import lax
from jax.sharding import PartitionSpec as P
from jax.experimental import pallas as pl
from jax.experimental.pallas import tpu as pltpu
HD=128
EPS=1e-6
F32=jnp.float32; BF=jnp.bfloat16
NT=(((1,),(1,)),((),()))
TN=(((0,),(0,)),((),()))
NN=(((1,),(0,)),((),()))
LOG2E=math.log2(math.e)
THETA=1000000.0
LONGEST=1024
FREQS=(THETA**(-np.arange(0,HD,2,dtype=np.float64)/HD)).astype(np.float32)
MESH=pl.DeviceIdType.MESH
D_=pltpu.SemaphoreType.DMA
S_=jax.ShapeDtypeStruct
V_=pl.BlockSpec(memory_space=pltpu.VMEM); A_=pl.BlockSpec(memory_space=pl.ANY)

def dot(a,b,dims=NN): return lax.dot_general(a,b,dims,preferred_element_type=F32)

def group():
    t=lax.axis_index('tensor')
    mate=t+1-2*lax.rem(t,2)
    return t,mate,lax.rem(t+2,4),lax.rem(mate+2,4)

def greet(peers):
    barrier=pltpu.get_barrier_semaphore()
    for axis,p in peers:
        pl.semaphore_signal(barrier,inc=1,device_id={axis:p},device_id_type=MESH)
    pl.semaphore_wait(barrier,len(peers))

def send(src,dst,ss,rs,peer,axis='tensor'):
    return pltpu.make_async_remote_copy(src_ref=src,dst_ref=dst,send_sem=ss,recv_sem=rs,device_id={axis:peer},device_id_type=MESH)

def span(i,step,mult=None): return pl.ds(pl.multiple_of(i*step,mult or step),step)

def rows_of(ref,b,j,r,per): return ref.at[pl.ds(pl.multiple_of(b*per+j*r,r),r)]

def each(n,f):
    def body(i,_):
        f(i)
        return 0
    lax.fori_loop(0,n,body,0)

def each_rows(n,f,step=64): each(n//step,lambda i: f(span(i,step)))

def when_each(k,table):
    for at,f in table: pl.when(k==at)(f)

def call(kernel,ins,outs,scratch,cid,name,out_specs,in_specs,limit=67043328):
    return pl.pallas_call(kernel,in_specs=in_specs,out_specs=out_specs,out_shape=outs,scratch_shapes=scratch,
        compiler_params=pltpu.CompilerParams(collective_id=cid,has_side_effects=True,vmem_limit_bytes=limit),name=name)(*ins)

def attn_fwd_kernel(bq,bk,ratio,scale,pos_ref,q_ref,k_ref,v_ref,prow_ref,o_ref,l_ref,vx_ref,acc_ref):
    i=pl.program_id(1)
    n=k_ref.shape[0]
    @pl.when(i==0)
    def _():
        vx_ref[:,:HD]=v_ref[...]
        vx_ref[:,HD:]=jnp.ones((n,HD),BF)
    q=q_ref[...]
    qs=jnp.concatenate([q[:,h*HD:(h+1)*HD] for h in range(ratio)],0)
    rows=lax.rem(lax.broadcasted_iota(jnp.int32,(ratio*bq,1),0),bq)+i*bq
    start=jnp.broadcast_to(prow_ref[...].astype(F32),(HD,bq)).T[:,0:1].astype(jnp.int32)
    start=rows-jnp.concatenate([start]*ratio,0)
    acc_ref[...]=jnp.zeros_like(acc_ref)
    c=scale*LOG2E
    def step(j,_):
        b=pl.multiple_of(j*bk,bk)
        s=dot(qs,k_ref[pl.ds(b,bk),:],NT)
        cols=lax.broadcasted_iota(jnp.int32,(1,bk),1)+b
        m=(rows>=cols)&(start<=cols)
        e=jnp.where(m,jnp.exp2(s*c),0.0).astype(BF)
        acc_ref[...]+=dot(e,vx_ref[pl.ds(b,bk),:])
        return 0
    lax.fori_loop((i*bq-pos_ref[i*bq])//bk,(i*bq+bq-1)//bk+1,step,0)
    a=acc_ref[...]
    l=a[:,HD:]
    o=(a[:,:HD]/l).astype(BF)
    lt=jnp.log2(l).T[0:1]
    for h in range(ratio):
        o_ref[:,h*HD:(h+1)*HD]=o[h*bq:(h+1)*bq]
        l_ref[0,h:h+1,:]=lt[:,h*bq:(h+1)*bq]

def attn_fwd(q,k,v,pos,bq,bk,scale):
    n,wq=q.shape; g=k.shape[1]//HD; ratio=wq//HD//g
    gs=pltpu.PrefetchScalarGridSpec(num_scalar_prefetch=1,grid=(g,n//bq),
        in_specs=[pl.BlockSpec((bq,ratio*HD),lambda g,i,p:(i,g)),
                  pl.BlockSpec((n,HD),lambda g,i,p:(0,g)),
                  pl.BlockSpec((n,HD),lambda g,i,p:(0,g)),
                  pl.BlockSpec((1,bq),lambda g,i,p:(0,i))],
        out_specs=[pl.BlockSpec((bq,ratio*HD),lambda g,i,p:(i,g)),
                   pl.BlockSpec((1,ratio,bq),lambda g,i,p:(g,0,i))],
        scratch_shapes=[pltpu.VMEM((n,2*HD),BF),pltpu.VMEM((ratio*bq,2*HD),F32)])
    return pl.pallas_call(functools.partial(attn_fwd_kernel,bq,bk,ratio,scale),grid_spec=gs,
        out_shape=[S_((n,wq),BF),S_((g,ratio,n),F32)],name='attn_fwd')(pos[0],q,k,v,pos)
def front_kernel(nc,x_ref,pos_ref,fr_ref,g_ref,wq_ref,wk_ref,wv_ref,gq_ref,gk_ref,
                 a_o,q_o,k_o,v_o,xh_o,r_o,cos_o,sin_o,
                 xf,a_s,q_s,k_s,v_s,xh_s,r_s,cost,sint,cosn,sinn,lsem,osem,ss,rs):
    t,mate,far,diag=group()
    per=x_ref.shape[0]; r=per//nc; n=xf.shape[0]; half=HD//2
    outs=[(a_s,a_o,0),(q_s,q_o,0),(k_s,k_o,0),(v_s,v_o,0),(xh_s,xh_o,1),(r_s,r_o,2)]
    own=pltpu.make_async_copy(x_ref,rows_of(xf,t,0,per,per),lsem)
    own.start()
    greet([('tensor',mate),('tensor',far)])
    across=lambda j: send(x_ref.at[span(j,r)],rows_of(xf,t,j,r,per),ss.at[0,j],rs.at[0,j],far)
    beside=lambda j: send(x_ref.at[span(j,r)],rows_of(xf,t,j,r,per),ss.at[1,j],rs.at[1,j],mate)
    onward=lambda j: send(rows_of(xf,far,j,r,per),rows_of(xf,far,j,r,per),ss.at[2,j],rs.at[2,j],mate)
    each(nc,lambda j: across(j).start())
    each(nc,lambda j: beside(j).start())
    gain=g_ref[...]; gq=gq_ref[...]; gk=gk_ref[...]
    tt=256
    def table(i):
        c=span(i,tt)
        ang=fr_ref[...]*pos_ref[:,c].astype(F32)
        co,si=jnp.cos(ang),jnp.sin(ang)
        ct=jnp.concatenate([co,co],0); st=jnp.concatenate([-si,si],0)
        cost[:,c]=ct; sint[:,c]=st
        cosn[c,:]=ct.T; sinn[c,:]=st.T
    each(n//tt,table)
    tabs=[pltpu.make_async_copy(cost,cos_o,osem.at[6,0]),pltpu.make_async_copy(sint,sin_o,osem.at[7,0])]
    for c in tabs: c.start()
    def out_copy(o,i):
        s,d,ax=outs[o]
        c=span(i,r)
        at=(c,(slice(None),c),(slice(None),slice(None),c))[ax]
        return pltpu.make_async_copy(s.at[at],d.at[at],osem.at[o,i])
    def tile(b,j):
        p=pl.multiple_of(b*per+j*r,r)
        rows=pl.ds(p,r)
        x=xf[rows,:].astype(F32)
        a=(x*lax.rsqrt(jnp.mean(x*x,-1,keepdims=True)+EPS)*gain).astype(BF)
        a_s[rows,:]=a
        v_s[rows,:]=dot(a,wv_ref[...]).astype(BF)
        cos=cosn[rows,:]; sin=sinn[rows,:]
        h0=0
        for w_ref,g,dst in ((wq_ref,gq,q_s),(wk_ref,gk,k_s)):
            raw=dot(a,w_ref[...])
            for h in range(raw.shape[1]//HD):
                rh=raw[:,h*HD:(h+1)*HD]
                u=rh*lax.rsqrt(jnp.mean(rh*rh,-1,keepdims=True)+EPS)*g
                dst[rows,h*HD:(h+1)*HD]=(u*cos+pltpu.roll(u,half,1)*sin).astype(BF)
                rt=rh.T
                rr=lax.rsqrt(jnp.mean(rt*rt,0,keepdims=True)+EPS)
                xh_s[(h0+h)*HD:(h0+h+1)*HD,rows]=(rt*rr).astype(BF)
                r_s[h0+h,:,rows]=rr
            h0+=raw.shape[1]//HD
        for o in range(6): out_copy(o,b*nc+j).start()
    own.wait()
    each(nc,lambda j: tile(t,j))
    each(nc,lambda j: beside(j).wait_recv())
    each(nc,lambda j: tile(mate,j))
    def body(j):
        across(j).wait_recv()
        onward(j).start()
        tile(far,j)
        onward(j).wait_recv()
        tile(diag,j)
    each(nc,body)
    def drain(j):
        across(j).wait_send(); beside(j).wait_send(); onward(j).wait_send()
    each(nc,drain)
    def flush(i):
        for o in range(6): out_copy(o,i).wait()
    each(n//r,flush)
    for c in tabs: c.wait()

def front(x,pos,freqs,gain,wq,wk,wv,gq,gk,nc,cid):
    n=4*x.shape[0]; d=x.shape[1]
    wide=wq.shape[1]+wk.shape[1]
    shapes=[((n,d),BF),((n,wq.shape[1]),BF),((n,wk.shape[1]),BF),((n,wv.shape[1]),BF),((wide,n),BF),((wide//HD,1,n),F32),((HD,n),F32),((HD,n),F32)]
    return call(functools.partial(front_kernel,nc),(x,pos,freqs,gain,wq,wk,wv,gq,gk),[S_(*s) for s in shapes],
        [pltpu.VMEM((n,d),BF)]+[pltpu.VMEM(*s) for s in shapes]+[pltpu.VMEM((n,HD),F32)]*2+[D_,D_((8,4*nc)),D_((3,nc)),D_((3,nc))],cid,'front',[A_]*8,[A_]+[V_]*8)
def ring_neighbours(d):
    me=lax.axis_index('dp')
    half=d//2
    odd=lax.rem(me,2); up=me//2
    pos=odd*(d-1-2*up)+up
    def at(p):
        hi=p//half
        return hi*(2*(d-1-p)+1)+(1-hi)*2*p
    return pos,at(lax.rem(pos+1,d)),at(lax.rem(pos+d-1,d))

class Ring:
    def __init__(self,d,sems,make=None):
        self.d,self.sems,self.make=d,sems,make
        self.pos,right,left=ring_neighbours(d)
        self.to=(right,left)
        self.units=[]
    def add(self,s,rc,mine,sbuf,recv,out): self.units.append((s,rc,mine,sbuf,recv,out))
    def chunk(self,s,k): return lax.rem(self.pos-k+2*self.d,self.d) if s==0 else lax.rem(self.pos+k,self.d)
    def rs(self,u,k,src):
        return send(src,self.units[u][4].at[k],self.sems[0].at[u,k],self.sems[1].at[u,k],self.to[self.units[u][0]],'dp')
    def ag(self,u,k,c):
        s,rc,_,_,_,out=self.units[u]
        ref=out.at[span(c,rc)]
        return send(ref,ref,self.sems[2].at[u,k],self.sems[3].at[u,k],self.to[s],'dp')
    def start(self):
        for u,(s,rc,mine,sbuf,recv,out) in enumerate(self.units):
            sbuf[...]=mine(0).astype(BF)
            self.rs(u,0,sbuf).start()
    def reduce_step(self,k):
        if self.make: self.make(k)
        for u,(s,rc,mine,sbuf,recv,out) in enumerate(self.units):
            self.rs(u,k-1,sbuf).wait_recv()
            val=(mine(k)+recv[k-1].astype(F32)).astype(BF)
            @pl.when(k<self.d-1)
            def _():
                recv[k-1]=val
                self.rs(u,k,recv.at[k-1]).start()
            @pl.when(k==self.d-1)
            def _():
                c=self.chunk(s,k)
                out[span(c,rc),:]=val
                self.ag(u,0,c).start()
    def gather_step(self,k):
        for u,(s,rc,mine,sbuf,recv,out) in enumerate(self.units):
            c=self.chunk(s,k-1)
            self.ag(u,k-1,c).wait_recv()
            @pl.when(k<self.d-1)
            def _(): self.ag(u,k,c).start()
    def any_step(self,m):
        pl.when(m<self.d)(lambda: self.reduce_step(m))
        pl.when(m>=self.d)(lambda: self.gather_step(m-self.d+1))
    def drain(self):
        def body(k):
            for u,(s,rc,mine,sbuf,recv,out) in enumerate(self.units):
                self.rs(u,k,sbuf).wait_send()
                self.ag(u,k,0).wait_send()
        each(self.d-1,body)

class Scatter:
    def __init__(self,ids,per,rbuf,fbuf,ybuf,acc,ss,rs):
        self.t,self.mate,self.far,self.diag=ids
        self.per=per; self.rbuf,self.fbuf,self.ybuf,self.acc,self.ss,self.rs=rbuf,fbuf,ybuf,acc,ss,rs
    @staticmethod
    def scratch(per,w): return [pltpu.VMEM((2,per,w),BF),pltpu.VMEM((per,w),BF),pltpu.VMEM((per,w),BF),pltpu.VMEM((per,w),F32),D_((3,)),D_((3,))]
    def to_mate(self,i,src): return send(src,self.rbuf.at[i],self.ss.at[i],self.rs.at[i],self.mate)
    def across(self): return send(self.fbuf,self.ybuf,self.ss.at[2],self.rs.at[2],self.far)
    def pair(self,far_part,own_part,base=None):
        self.pair_far(far_part)
        self.pair_own(own_part,base)
    def pair_far(self,far_part):
        self.to_mate(1,self.fbuf).wait_recv()
        def far_rows(r): self.fbuf[r,:]=(far_part[r,:].astype(F32)+self.rbuf[1,r,:].astype(F32)).astype(BF)
        each_rows(self.per,far_rows)
        self.across().start()
    def pair_own(self,own_part,base=None):
        self.to_mate(0,self.fbuf).wait_recv()
        def own_rows(r):
            v=own_part[r,:].astype(F32)+self.rbuf[0,r,:].astype(F32)
            self.acc[r,:]=v if base is None else v+base[r,:]
        each_rows(self.per,own_rows)
    def result(self,f):
        self.across().wait_recv()
        each_rows(self.per,lambda r: f(r,self.acc[r,:]+self.ybuf[r,:].astype(F32)))
    def drain(self):
        self.to_mate(0,self.fbuf).wait_send(); self.to_mate(1,self.fbuf).wait_send(); self.across().wait_send()

def norm_bwd(v,gain,e):
    r=lax.rsqrt(jnp.mean(v*v,-1,keepdims=True)+EPS)
    vh=v*r
    ge=e*gain
    return r*(ge-vh*jnp.mean(vh*ge,-1,keepdims=True)),jnp.sum(e*vh,0,keepdims=True)
def mid_kernel(nc,att_ref,wo_ref,x_ref,cot_ref,cof_ref,wg_ref,wu_ref,wd_ref,g_ref,
               hid_ref,a_o,act_o,dg_o,du_o,op_o,da_o,dy_o,
               attv,wov,dyv,wgv,wuv,wdv,full,act_s,dg_s,du_s,op_s,da_s,acc,pbuf,rbuf,fbuf,ybuf,lsem,osem,ss,rs,dsem):
    t,mate,far,diag=group()
    per=x_ref.shape[0]; r=per//nc; n=full.shape[0]
    loads=[pltpu.make_async_copy(s,d,lsem.at[i]) for i,(s,d) in enumerate(((att_ref,attv),(wo_ref,wov),(cot_ref,rows_of(dyv,t,0,per,per)),(wg_ref,wgv),(wu_ref,wuv),(wd_ref,wdv),(cof_ref,rows_of(dyv,far,0,per,per))))]
    for c in loads: c.start()
    greet([('tensor',mate),('tensor',far)])
    dys=[send(cot_ref,rows_of(dyv,t,0,per,per),dsem.at[0],dsem.at[1],mate),send(cof_ref,rows_of(dyv,far,0,per,per),dsem.at[2],dsem.at[3],mate)]
    outs=[(full,a_o),(act_s,act_o),(dg_s,dg_o),(du_s,du_o),(op_s,op_o),(da_s,da_o)]
    gain=g_ref[...]
    def proj(b,j):
        return dot(rows_of(attv,b,j,r,per)[...],wov[...])
    def to_mate(i,j):
        return send(pbuf.at[i,pl.ds(pl.multiple_of(j*r,r),r)],rbuf.at[i,pl.ds(pl.multiple_of(j*r,r),r)],ss.at[i,j],rs.at[i,j],mate)
    def to_far(j):
        rr=pl.ds(pl.multiple_of(j*r,r),r)
        return send(fbuf.at[rr],ybuf.at[rr],ss.at[2,j],rs.at[2,j],far)
    def share(j,i,peer):
        return send(rows_of(full,t,j,r,per),rows_of(full,t,j,r,per),ss.at[i,j],rs.at[i,j],peer)
    def forward(j):
        return send(rows_of(full,far,j,r,per),rows_of(full,far,j,r,per),ss.at[5,j],rs.at[5,j],mate)
    loads[0].wait(); loads[1].wait()
    def reduce(j,_):
        rr=pl.ds(pl.multiple_of(j*r,r),r)
        pbuf[1,rr,:]=proj(diag,j).astype(BF); to_mate(1,j).start()
        pbuf[0,rr,:]=proj(mate,j).astype(BF); to_mate(0,j).start()
        f=proj(far,j)
        to_mate(1,j).wait_recv()
        fbuf[rr,:]=(f+rbuf[1,rr,:].astype(F32)).astype(BF)
        to_far(j).start()
        @pl.when(j==0)
        def _():
            for c in dys: c.start()
        o=proj(t,j)
        to_mate(0,j).wait_recv()
        acc[rr,:]=o+rbuf[0,rr,:].astype(F32)+x_ref[rr,:].astype(F32)
        return 0
    lax.fori_loop(0,nc,reduce,0)
    for i in range(2,7): loads[i].wait()
    for c in dys: c.wait_recv()
    dyc=pltpu.make_async_copy(dyv,dy_o,lsem.at[7])
    dyc.start()
    def mlp_rows(b,j):
        rows=pl.ds(pl.multiple_of(b*per+j*r,r),r)
        a=full[rows,:]
        gate=dot(a,wgv[...]); up=dot(a,wuv[...])
        dact=dot(dyv[rows,:],wdv[...],NT)
        sig=1.0/(1.0+jnp.exp(-gate))
        sl=gate*sig
        act=(sl*up).astype(BF)
        act_s[rows,:]=act
        dg=(dact*up*(sig*(1.0+gate*(1.0-sig)))).astype(BF)
        du=(dact*sl).astype(BF)
        dg_s[rows,:]=dg; du_s[rows,:]=du
        op_s[rows,:]=dot(act,wdv[...]).astype(BF)
        da_s[rows,:]=(dot(dg,wgv[...],NT)+dot(du,wuv[...],NT)).astype(BF)
        for o,(s,d) in enumerate(outs):
            pltpu.make_async_copy(s.at[rows],d.at[rows],osem.at[o,b*nc+j]).start()
    def near(j,_):
        rr=pl.ds(pl.multiple_of(j*r,r),r)
        to_far(j).wait_recv()
        h=acc[rr,:]+ybuf[rr,:].astype(F32)
        hid_ref[rr,:]=h
        rows_of(full,t,j,r,per)[...]=(h*lax.rsqrt(jnp.mean(h*h,-1,keepdims=True)+EPS)*gain).astype(BF)
        share(j,3,far).start(); share(j,4,mate).start()
        def both(i,_):
            @pl.when(i==1)
            def _(): share(j,4,mate).wait_recv()
            mlp_rows(t+i*(mate-t),j)
            return 0
        lax.fori_loop(0,2,both,0)
        return 0
    lax.fori_loop(0,nc,near,0)
    def away(j,_):
        share(j,3,far).wait_recv()
        forward(j).start()
        def both(i,_):
            @pl.when(i==1)
            def _(): forward(j).wait_recv()
            mlp_rows(far+i*(diag-far),j)
            return 0
        lax.fori_loop(0,2,both,0)
        return 0
    lax.fori_loop(0,nc,away,0)
    def drain(j,_):
        to_mate(0,j).wait_send(); to_mate(1,j).wait_send(); to_far(j).wait_send()
        share(j,3,far).wait_send(); share(j,4,mate).wait_send(); forward(j).wait_send()
        return 0
    lax.fori_loop(0,nc,drain,0)
    def flush(i,_):
        rows=pl.ds(pl.multiple_of(i*r,r),r)
        for o,(s,d) in enumerate(outs):
            pltpu.make_async_copy(s.at[rows],d.at[rows],osem.at[o,i]).wait()
        return 0
    lax.fori_loop(0,n//r,flush,0)
    dyc.wait()
    for c in dys: c.wait_send()

def middle(att,wo,x,cot,cof,wg,wu,wd,gain,nc,cid):
    n=att.shape[0]; per,d=x.shape; f=wg.shape[1]
    rows=[((n,d),BF),((n,f),BF),((n,f),BF),((n,f),BF),((n,d),BF),((n,d),BF)]
    return call(functools.partial(mid_kernel,nc),(att,wo,x,cot,cof,wg,wu,wd,gain),[S_((per,d),F32)]+[S_(*s) for s in rows]+[S_((n,d),BF)],
        [pltpu.VMEM(s,BF) for s in (att.shape,wo.shape,(n,d),wg.shape,wu.shape,wd.shape)]+[pltpu.VMEM(*s) for s in rows]+
        [pltpu.VMEM((per,d),F32),pltpu.VMEM((2,per,d),BF),pltpu.VMEM((2,per,d),BF),pltpu.VMEM((per,d),BF),pltpu.VMEM((per,d),BF),
         D_((8,)),D_((6,4*nc)),D_((6,nc)),D_((6,nc)),D_((4,))],cid,'middle',[V_]+[A_]*7,[A_,A_,V_,A_,A_,A_,A_,A_,V_])
def post_kernel(d,fused,hid_ref,cot_ref,g_ref,wo_ref,a_ref,dy_ref,act_ref,dg_ref,du_ref,da_ref,att_ref,
                dhid_ref,gg_ref,dwg_ref,dwu_ref,dwd_ref,dwo_ref,dout_o,
                av,ac,dyv,actv,dgv,duv,attv,full,doutv,parts,ownbuf,sbuf,recv,lsem,osem,ss,rs,m0,m1,m2,m3,oacc,*rest):
    ids=t,mate,far,diag=group()
    per,dm=hid_ref.shape; n=full.shape[0]; f=dgv.shape[1]; rc=dm//d
    rs1=Scatter(ids,per,*rest[:6])
    whole=None if fused else rest[6]
    def make(k):
        if fused:
            for s in range(2): ownbuf[s]=dot(av[:,span(ring.chunk(s,k),rc)],(dgv,duv)[s][...],TN)
    ring=Ring(d,(m0,m1,m2,m3),make)
    nu=3
    w=f//nu
    for j in range(nu):
        for s,out in enumerate((dwg_ref,dwu_ref)):
            lo,hi=j*w,(j+1)*w
            def mine(k,s=s,lo=lo,hi=hi):
                if fused: return ownbuf[s,:,lo:hi]
                return whole[s,span(ring.chunk(s,k),rc),lo:hi].astype(F32)
            ring.add(s,rc,mine,sbuf.at[s,:,lo:hi],recv.at[s,:,:,lo:hi],out.at[:,lo:hi])
    c0=pl.multiple_of(ring.chunk(0,0)*rc,128) if fused else 0
    loads=[pltpu.make_async_copy(s,x,lsem.at[i]) for i,(s,x) in enumerate(((dg_ref,dgv),(a_ref.at[:,pl.ds(c0,128)],ac),(du_ref,duv),(a_ref,av),(dy_ref,dyv),(act_ref,actv),(att_ref,attv)))]
    blk=lambda ref,b: rows_of(ref,b,0,per,per)
    parts_=[pltpu.make_async_copy(blk(da_ref,b),parts.at[i],lsem.at[7+i]) for i,b in enumerate((far,t))]
    for c in loads[:4]+parts_+loads[4:]: c.start()
    greet([('tensor',mate),('tensor',far),('dp',ring.to[0]),('dp',ring.to[1])])
    rs1.to_mate(1,blk(da_ref,diag)).start(); rs1.to_mate(0,blk(da_ref,mate)).start()
    for c in loads[:3]: c.wait()
    if fused:
        for s in range(2): ownbuf[s]=dot(ac[...],(dgv,duv)[s][...],TN)
        ring.start()
        loads[3].wait()
    else:
        loads[3].wait()
        for s in range(2):
            def tile(i,s=s): whole[s,span(i,128),:]=dot(av[:,span(i,128)],(dgv,duv)[s][...],TN).astype(BF)
            each(dm//128,tile)
        ring.start()
    share=lambda i,p: send(blk(full,t),blk(full,t),ss.at[i],rs.at[i],p)
    onward=lambda: send(blk(full,far),blk(full,far),ss.at[2],rs.at[2],mate)
    def e1():
        for c in parts_: c.wait()
        rs1.pair(parts.at[0],parts.at[1])
    def e2():
        gg_ref[...]=jnp.zeros_like(gg_ref)
        mine=blk(full,t)
        def rows(r,da):
            dh,gg=norm_bwd(hid_ref[r,:],g_ref[...],da)
            dh=dh+cot_ref[r,:].astype(F32)
            dhid_ref[r,:]=dh; gg_ref[...]+=gg
            mine[r,:]=dh.astype(BF)
        rs1.result(rows)
        share(0,far).start(); share(1,mate).start()
    def down():
        for c in loads[4:6]: c.wait()
        def tile(i): dwd_ref[:,span(i,256)]=dot(actv[...],dyv[:,span(i,256)],TN).astype(BF)
        each(dm//256,tile)
    tt=256
    def dout_rows(b,last=False):
        def tile(i):
            rows=pl.ds(pl.multiple_of(b*per+i*tt,tt),tt)
            doutv[rows,:]=dot(full[rows,:],wo_ref[...],NT).astype(BF)
        each(per//tt,tile)
        rows=span(b,per)
        if last: pltpu.make_async_copy(doutv,dout_o,osem.at[0]).start()
        def out_tile(i):
            c=span(i,256)
            v=dot(attv[rows,:],full[rows,c],TN)
            if last: dwo_ref[:,c]=(oacc[:,c]+v).astype(BF)
            else: oacc[:,c]+=v
        each(dm//256,out_tile)
    def e3():
        loads[6].wait()
        oacc[...]=jnp.zeros_like(oacc)
        dout_rows(t)
        share(1,mate).wait_recv()
        dout_rows(mate)
    def e4():
        share(0,far).wait_recv()
        onward().start()
        dout_rows(far)
    def step(k):
        when_each(k,((1,e1),(d//2,down),(d-1,e2)))
        ring.reduce_step(k)
    lax.fori_loop(1,d,lambda k,_: (step(k),0)[1],0)
    def gstep(k):
        when_each(k,((2,e3),(d-2,e4)))
        ring.gather_step(k)
    lax.fori_loop(1,d,lambda k,_: (gstep(k),0)[1],0)
    onward().wait_recv()
    dout_rows(diag,True)
    ring.drain(); rs1.drain()
    share(0,far).wait_send(); share(1,mate).wait_send(); onward().wait_send()
    pltpu.make_async_copy(doutv,dout_o,osem.at[0]).wait()

def post(hid,cot,gain,wo,a2,dy,act,dg,du,dap,att,d,cid):
    per,dm=hid.shape; n=a2.shape[0]; f=act.shape[1]
    fused=(dm//d)%128==0
    M=pltpu.VMEM
    wo_=wo.shape[0]
    return call(functools.partial(post_kernel,d,fused),(hid,cot,gain,wo,a2,dy,act,dg,du,dap,att),
        [S_((per,dm),F32),S_((1,dm),F32),S_((dm,f),BF),S_((dm,f),BF),S_((f,dm),BF),S_((wo_,dm),BF),S_((n,wo_),BF)],
        [M((n,dm),BF),M((n,128),BF),M((n,dm),BF),M((n,f),BF),M((n,f),BF),M((n,f),BF),M((n,wo_),BF),M((n,dm),BF),M((n,wo_),BF),M((2,per,dm),BF),
         M((2,dm//d,f),F32),M((2,dm//d,f),BF),M((2,d-1,dm//d,f),BF),D_((9,)),D_((1,)),D_((3,)),D_((3,))]+[D_((6,d-1))]*4+[M((wo_,dm),F32)]+Scatter.scratch(per,dm)+([] if fused else [M((2,dm,f),BF)]),
        cid,'post',[V_]*6+[A_],[V_]*4+[A_]*7)
def rot_norm_bwd(dt,xh,r,gain,cos,sin):
    h=HD//2
    du=dt*cos-jnp.concatenate([dt[h:],dt[:h]],0)*sin
    ge=du*gain
    return r*(ge-xh*jnp.mean(xh*ge,0,keepdims=True)),du*xh

def tail_kernel(d,nt,fused,bq,bk,scale,x_ref,g_ref,gm_ref,gqc_ref,gkc_ref,wq_ref,wk_ref,wv_ref,pos_ref,lse_ref,r_ref,dwd_ref,dwo_ref,
                q_ref,k_ref,v_ref,do_ref,att_ref,xh_ref,cos_ref,sin_ref,a_ref,op_ref,hid_ref,dhid_ref,
                out_o,dx_ref,dwq_o,dwk_o,dwv_o,dwd_o,dwo_o,ga_o,gm_o,gq_o,gk_o,
                u1,kv,vv,attv,xhv,cosv,sinv,dj,dka,dva,dqa,qs,os_,kt,dd,gacc,gcol,ac,
                pbuf,farbuf,ownbuf,gbuf,grecv,b2d,r2d,b2o,r2o,b3,r3,lsem,gs,gr,p0,p1,p2,p3,t0,t1,t2,t3,*rest):
    ids=t,mate,far,diag=group()
    per,dm=x_ref.shape; n=u1.shape[0]
    wq,wk,wv,wo=attv.shape[1],kv.shape[1],vv.shape[1],dwo_ref.shape[0]
    rc=dm//d
    sc=Scatter(ids,per,*rest[:6]); so=Scatter(ids,per,*rest[6:12])
    whole=None if fused else rest[12]
    blk=lambda ref,b: rows_of(ref,b,0,per,per)
    loads=[pltpu.make_async_copy(s,x,lsem.at[i]) for i,(s,x) in enumerate(((q_ref,u1.at[:,0:wq]),(k_ref,kv),(v_ref,vv),(do_ref,u1.at[:,wq:2*wq]),(att_ref,attv),(xh_ref,xhv),(cos_ref,cosv),(sin_ref,sinv)))]
    first=Ring(d,(p0,p1,p2,p3))
    h=dm//2
    for lo in range(0,h,h//2):
        for src,b,rv,out in ((dwd_ref,b2d,r2d,dwd_o),(dwo_ref,b2o,r2o,dwo_o)):
            rr=src.shape[0]//d
            for s in range(2):
                cs=slice(s*h+lo,s*h+lo+h//2); bs=slice(lo,lo+h//2)
                first.add(s,rr,lambda k,s=s,src=src,rr=rr,cs=cs: src[span(first.chunk(s,k),rr),cs].astype(F32),b.at[s,:,bs],rv.at[s,:,:,bs],out.at[:,cs])
    def make(k):
        if fused:
            c=first.chunk(0,k); e=first.chunk(1,k)
            ownbuf[0]=dot(u1[:,span(c,rc)],dj[:,0:wq],TN)
            ownbuf[1]=dot(u1[:,span(e,rc)],dj[:,wq:2*wq],TN)
    second=Ring(d,(t0,t1,t2,t3),make)
    for lo in range(0,wq,wk):
        for s in range(2):
            out=dwq_o.at[:,lo:lo+wk] if s==0 else (dwk_o,dwv_o)[lo//wk]
            def mine(k,s=s,lo=lo):
                if fused: return ownbuf[s,:,lo:lo+wk]
                return whole[s,span(second.chunk(s,k),rc),lo:lo+wk].astype(F32)
            second.add(s,rc,mine,b3.at[s,:,lo:lo+wk],r3.at[s,:,:,lo:lo+wk],out)
    c0=pl.multiple_of(first.chunk(0,0)*rc,128) if fused else 0
    later=[pltpu.make_async_copy(a_ref.at[:,pl.ds(c0,128)],ac,lsem.at[8]),pltpu.make_async_copy(dhid_ref,dx_ref,lsem.at[9]),
           pltpu.make_async_copy(blk(op_ref,far),pbuf.at[0],lsem.at[10]),pltpu.make_async_copy(blk(op_ref,t),pbuf.at[1],lsem.at[11]),pltpu.make_async_copy(hid_ref,so.acc,lsem.at[12])]
    for c in loads+later: c.start()
    steps=[]
    for axis,m in (('tensor',nt),('dp',d)):
        b=1
        while b<m:
            steps.append((axis,b)); b*=2
    def partner(axis,b):
        me=lax.axis_index(axis)
        return me+b-2*b*lax.rem(me//b,2)
    greet([('tensor',mate),('tensor',far),('dp',first.to[0]),('dp',first.to[1])]+[(a,partner(a,b)) for a,b in steps])
    first.start()
    so.to_mate(1,blk(op_ref,diag)).start(); so.to_mate(0,blk(op_ref,mate)).start()
    def pair_out():
        for c in later[2:]: c.wait()
        so.pair(pbuf.at[0],pbuf.at[1],so.acc)
    def finish_out():
        def rows(r,v): out_o[r,:]=v.astype(BF)
        so.result(rows)
    gcol[0]=jnp.broadcast_to(gqc_ref[...],(HD,HD)); gcol[1]=jnp.broadcast_to(gkc_ref[...],(HD,HD))
    gacc[...]=jnp.zeros_like(gacc)
    for c in loads: c.wait()
    groups=wk//HD; ratio=wq//wk; nb=n//bq; jb=bq//bk
    c2=scale*LOG2E
    total=2*(d-1)
    back=-(-LONGEST//bk)
    first_key=lambda i: jnp.maximum(jb*i-back,0)
    sizes=[jb*(i+1)-max(jb*i-back,0) for i in range(nb)]
    per_group=sum(sizes)
    full=[i for i in range(nb) if jb*i<=back]
    iters=groups*per_group
    def before(i):
        u=jnp.minimum(i,len(full))
        return jb*u*(u+1)//2+(i-u)*(jb+back)
    hooks=iters
    def hook(it):
        when_each(it,((2,pair_out),(iters-1,finish_out)))
        for z in range(-(-total//iters)):
            m=(it*total+z*total//iters)//iters+1 if total<=iters else it*total//iters+1+z
            ready=(it+1)*total//iters>=m
            if total<=iters: ready=ready&((it*total)//iters<m)
            pl.when(ready)(lambda: first.any_step(m))
    def lane_tiles(dt,head,gi,cols,put):
        for z in range(dt.shape[1]//HD):
            cs=pl.ds(pl.multiple_of(cols+z*HD,HD),HD)
            dx,gg=rot_norm_bwd(dt[:,z*HD:(z+1)*HD]*scale,xhv[span(head,HD),cs].astype(F32),r_ref[head,:,cs],gcol[gi],cosv[:,cs],sinv[:,cs])
            gacc[gi]+=gg
            put(cs,dx.T.astype(BF))
    def one_group(g):
        gl=pl.multiple_of(g*HD,HD)
        kcols=pl.ds(gl,HD)
        def prep(i):
            kt[:,span(i,bq)]=kv[span(i,bq),kcols].T
            dka[span(i,bq),:]=jnp.zeros((bq,HD),F32); dva[span(i,bq),:]=jnp.zeros((bq,HD),F32)
        each(nb,prep)
        qcol=[pl.ds(pl.multiple_of(g*ratio*HD+x*HD,HD),HD) for x in range(ratio)]
        dcol=[pl.ds(pl.multiple_of(wq+g*ratio*HD+x*HD,HD),HD) for x in range(ratio)]
        def q_block(i):
            rows=span(i,bq)
            colq=lax.broadcasted_iota(jnp.int32,(1,bq),1)+i*bq
            st=colq-pos_ref[:,rows]
            for x in range(ratio):
                at=slice(x*bq,(x+1)*bq)
                qx=u1[rows,qcol[x]]; ox=u1[rows,dcol[x]]
                qs[at,:]=qx; os_[at,:]=ox
                pr=ox.astype(F32)*attv[rows,qcol[x]].astype(F32)
                hi=pr.astype(BF); lo=(pr-hi.astype(F32)).astype(BF)
                one=jnp.ones((8,HD),BF)
                dd[:,at]=dot(one,hi,NT)+dot(one,lo,NT)
                dd[0:1,ratio*bq+x*bq:ratio*bq+(x+1)*bq]=lse_ref[g*ratio+x,:,rows]
            dqa[...]=jnp.zeros_like(dqa)
            two=lambda v: jnp.concatenate([v]*ratio,1)
            cols,sts=two(colq),two(st)
            inner=dd[0:1,0:ratio*bq]; ls=dd[0:1,ratio*bq:]
            def key_block(j):
                b=span(j,bk)
                kb=kv[b,kcols]
                s=dot(kb,qs[...],NT)
                keys=lax.broadcasted_iota(jnp.int32,(bk,1),0)+j*bk
                p=jnp.where((cols>=keys)&(sts<=keys),jnp.exp2(s*c2-ls),0.0)
                ds=(p*(dot(vv[b,kcols],os_[...],NT)-inner)).astype(BF)
                dva[b,:]+=dot(p.astype(BF),os_[...])
                dka[b,:]+=dot(ds,qs[...])
                dqa[...]+=dot(kt[:,b],ds)
                hook(g*per_group+before(i)+j-j0)
                return 0
            j0=first_key(i)
            lax.fori_loop(j0,(i+1)*jb,lambda j,_: key_block(j),0)
            for x in range(ratio):
                def put(cs,v,x=x): dj[cs,qcol[x]]=v
                lane_tiles(dqa[:,x*bq:(x+1)*bq],g*ratio+x,0,i*bq,put)
        each(nb,q_block)
        def fin(i):
            rows=span(i,bq)
            dj[rows,pl.ds(pl.multiple_of(wq+wk+gl,HD),HD)]=dva[rows,:].astype(BF)
            def put(cs,v): dj[cs,pl.ds(pl.multiple_of(wq+gl,HD),HD)]=v
            lane_tiles(dka[rows,:].T,wq//HD+g,1,i*bq,put)
        each(nb,fin)
    each(groups,one_group)
    al=pltpu.make_async_copy(a_ref,u1,lsem.at[13])
    al.start()
    later[0].wait(); later[1].wait()
    if fused:
        ownbuf[0]=dot(ac[...],dj[:,0:wq],TN); ownbuf[1]=dot(ac[...],dj[:,wq:2*wq],TN)
    else:
        al.wait()
        for s in range(2):
            def tile(i,s=s): whole[s,span(i,128),:]=dot(u1[:,span(i,128)],dj[:,s*wq:(s+1)*wq],TN).astype(BF)
            each(dm//128,tile)
    second.start()
    if fused: al.wait()
    tp=256
    def part(b,ref,i):
        def tile(j):
            rows=pl.ds(pl.multiple_of(b*per+j*tp,tp),tp)
            v=dot(dj[rows,0:wq],wq_ref[...],NT)+dot(dj[rows,wq:wq+wk],wk_ref[...],NT)+dot(dj[rows,wq+wk:2*wq],wv_ref[...],NT)
            ref[i,span(j,tp),:]=v.astype(BF)
        each(per//tp,tile)
    part(diag,pbuf,1)
    sc.to_mate(1,pbuf.at[1]).start()
    part(far,farbuf,0)
    sc.pair_far(farbuf.at[0])
    part(mate,pbuf,0)
    sc.to_mate(0,pbuf.at[0]).start()
    part(t,farbuf,1)
    def e1(): sc.pair_own(farbuf.at[1])
    def e2():
        gbuf[:,0:dm]=jnp.zeros((1,dm),F32)
        gbuf[:,dm:2*dm]=gm_ref[...]
        gbuf[:,2*dm:2*dm+HD]=jnp.sum(gacc[0].T,0,keepdims=True)
        gbuf[:,2*dm+HD:2*dm+2*HD]=jnp.sum(gacc[1].T,0,keepdims=True)
        def rows(r,e):
            dv,gg=norm_bwd(x_ref[r,:].astype(F32),g_ref[...],e)
            dx_ref[r,:]+=dv
            gbuf[:,0:dm]+=gg
        sc.result(rows)
    def step(k):
        pl.when(k==1)(e1)
        second.reduce_step(k)
    lax.fori_loop(1,d,lambda k,_: (step(k),0)[1],0)
    cps=[send(grecv.at[2*i+1],grecv.at[2*i],gs.at[i],gr.at[i],partner(a,b),a) for i,(a,b) in enumerate(steps)]
    def turn(i):
        def f():
            if i==0: e2()
            else:
                cps[i-1].wait_recv()
                gbuf[...]+=grecv[2*i-2]
            if i<len(steps):
                grecv[2*i+1]=gbuf[...]
                cps[i].start()
        return f
    def gstep(k):
        when_each(k,[(i+2,turn(i)) for i in range(min(len(steps)+1,d-2))])
        second.gather_step(k)
    lax.fori_loop(1,d,lambda k,_: (gstep(k),0)[1],0)
    for i in range(d-2,len(steps)+1): turn(i)()
    ga_o[...]=gbuf[:,0:dm]; gm_o[...]=gbuf[:,dm:2*dm]; gq_o[...]=gbuf[:,2*dm:2*dm+HD]; gk_o[...]=gbuf[:,2*dm+HD:2*dm+2*HD]
    first.drain(); second.drain(); sc.drain(); so.drain()
    for c in cps: c.wait_send()

def tail(x,g,gm,gqc,gkc,wq,wk,wv,pos,lse,r,dwd,dwo,q,k,v,do,att,xh,cos,sin,a1,op,hid,dhid,d,nt,bq,bk,scale,cid):
    per,dm=x.shape; n=a1.shape[0]
    nq,nk,nv=q.shape[1],k.shape[1],v.shape[1]
    assert nq==nk+nv
    fused=(dm//d)%128==0
    M=pltpu.VMEM
    ns=sum((s-1).bit_length() for s in (d,nt))
    ratio=nq//nk; rc=dm//d; h=dm//2
    row=lambda c: S_((1,c),F32)
    rd,ro=dwd.shape[0]//d,dwo.shape[0]//d
    ins=(x,g,gm,gqc,gkc,wq,wk,wv,pos,lse,r,dwd,dwo,q,k,v,do,att,xh,cos,sin,a1,op,hid,dhid)
    return call(functools.partial(tail_kernel,d,nt,fused,bq,bk,scale),ins,
        [S_((per,dm),BF),S_((per,dm),F32),S_((dm,nq),BF),S_((dm,nk),BF),S_((dm,nv),BF),S_(dwd.shape,BF),S_(dwo.shape,BF),row(dm),row(dm),row(HD),row(HD)],
        [M((n,2*nq),BF),M((n,nk),BF),M((n,nv),BF),M((n,nq),BF),M(xh.shape,BF),M(cos.shape,F32),M(sin.shape,F32),M((n,2*nq),BF),M((n,HD),F32),M((n,HD),F32),
         M((HD,ratio*bq),F32),M((ratio*bq,HD),BF),M((ratio*bq,HD),BF),M((HD,n),BF),M((8,2*ratio*bq),F32),M((2,HD,HD),F32),M((2,HD,HD),F32),M((n,128),BF),
         M((2,per,dm),BF),M((2,per,dm),BF),M((2,rc,nq),F32),M((1,2*dm+2*HD),F32),M((2*ns,1,2*dm+2*HD),F32),
         M((2,rd,h),BF),M((2,d-1,rd,h),BF),M((2,ro,h),BF),M((2,d-1,ro,h),BF),M((2,rc,nq),BF),M((2,d-1,rc,nq),BF),
         D_((14,)),D_((ns,)),D_((ns,))]+[D_((8,d-1))]*4+[D_((4,d-1))]*4+Scatter.scratch(per,dm)*2+([] if fused else [M((2,dm,nq),BF)]),
        cid,'tail',[V_]*11,[V_]*13+[A_]*12)
def widen_kernel(*refs):
    n=len(refs)//2
    for a,b in zip(refs[:n],refs[n:]): b[...]=a[...].astype(F32)

def widen(arrays,steps=4):
    specs=[pl.BlockSpec((a.shape[0]//steps,a.shape[1]),lambda i:(i,0)) for a in arrays]
    return pl.pallas_call(widen_kernel,grid=(steps,),in_specs=specs,out_specs=specs,out_shape=[S_(a.shape,F32) for a in arrays],name='widen')(*arrays)

def local(nd,nt,tokens,w_query,w_key,w_value,w_out,w_gate,w_up,w_down,norm_attn,norm_mlp,norm_query,norm_key,cotangent,segments,positions):
    scale=HD**-0.5
    row=lambda g: g.astype(F32)[None]
    col=lambda g: g.astype(F32)[:,None]
    g_attn,g_mlp=row(norm_attn),row(norm_mlp)
    a1,q,k,v,xh,r,cos,sin=front(tokens,positions,jnp.asarray(FREQS[:,None]),g_attn,w_query,w_key,w_value,row(norm_query),row(norm_key),4,1)
    q,cot=lax.optimization_barrier((q,cotangent))
    cof=lax.ppermute(cot,'tensor',[(i,(i+2)%nt) for i in range(nt)])
    att,lse=attn_fwd(q,k,v,positions,512,256,scale)
    att,cof=lax.optimization_barrier((att,cof))
    hid,a2,act,dg,du,outp,dap,dy=middle(att,w_out,tokens,cotangent,cof,w_gate,w_up,w_down,g_mlp,2,2)
    dhid,gm,dwg,dwu,dwd,dwo,dout=post(hid,cotangent,g_mlp,w_out,a2,dy,act,dg,du,dap,att,nd,3)
    n=q.shape[0]
    output,d_tokens,dwq,dwk,dwv,dwd,dwo,ga,gm,gq,gk=tail(tokens,g_attn,gm,col(norm_query),col(norm_key),w_query,w_key,w_value,positions,lse.reshape(-1,1,n),r,dwd,dwo,
        q,k,v,dout,att,xh,cos,sin,a1,outp,hid,dhid,nd,nt,512,256,scale,4)
    dwq,dwk,dwv,dwo,dwg,dwu,dwd=widen((dwq,dwk,dwv,dwo,dwg,dwu,dwd))
    return (output,d_tokens,dwq,dwk,dwv,dwo,dwg,dwu,dwd,ga[0],gm[0],gq[0],gk[0])

def solution(mesh):
    nd,nt=mesh.shape['dp'],mesh.shape['tensor']
    row=P(('dp','tensor'),None); col=P(None,'tensor'); rw=P('tensor',None)
    return jax.shard_map(functools.partial(local,nd,nt),mesh=mesh,
        in_specs=(row,col,col,col,rw,col,col,rw,P(),P(),P(),P(),row,P('dp',None),P('dp',None)),
        out_specs=(row,row,col,col,col,rw,col,col,rw,P(),P(),P(),P()),check_vma=False)
```

```python
import functools, math
import numpy as np
import jax, jax.numpy as jnp
from jax import lax
from jax.sharding import PartitionSpec as P
from jax.experimental import pallas as pl
from jax.experimental.pallas import tpu as pltpu
HD=128
EPS=1e-6
F32=jnp.float32; BF=jnp.bfloat16
NT=(((1,),(1,)),((),()))
TN=(((0,),(0,)),((),()))
NN=(((1,),(0,)),((),()))
LOG2E=math.log2(math.e)
THETA=1000000.0
LONGEST=1024
FREQS=(THETA**(-np.arange(0,HD,2,dtype=np.float64)/HD)).astype(np.float32)
MESH=pl.DeviceIdType.MESH
D_=pltpu.SemaphoreType.DMA
S_=jax.ShapeDtypeStruct
V_=pl.BlockSpec(memory_space=pltpu.VMEM); A_=pl.BlockSpec(memory_space=pl.ANY)

def dot(a,b,dims=NN): return lax.dot_general(a,b,dims,preferred_element_type=F32)

def vec(ref): return ref[...].astype(F32).reshape(1,-1)

def group():
    t=lax.axis_index('tensor')
    mate=t+1-2*lax.rem(t,2)
    return t,mate,lax.rem(t+2,4),lax.rem(mate+2,4)

def greet(peers):
    barrier=pltpu.get_barrier_semaphore()
    for axis,p in peers:
        pl.semaphore_signal(barrier,inc=1,device_id={axis:p},device_id_type=MESH)
    pl.semaphore_wait(barrier,len(peers))

def send(src,dst,ss,rs,peer,axis='tensor'):
    return pltpu.make_async_remote_copy(src_ref=src,dst_ref=dst,send_sem=ss,recv_sem=rs,device_id={axis:peer},device_id_type=MESH)

def span(i,step,mult=None): return pl.ds(pl.multiple_of(i*step,mult or step),step)

def rows_of(ref,b,j,r,per): return ref.at[pl.ds(pl.multiple_of(b*per+j*r,r),r)]

def each(n,f):
    def body(i,_):
        f(i)
        return 0
    lax.fori_loop(0,n,body,0)

def each_rows(n,f,step=64): each(n//step,lambda i: f(span(i,step)))

def when_each(k,table):
    for at,f in table: pl.when(k==at)(f)

def call(kernel,ins,outs,scratch,cid,name,out_specs,in_specs,limit=67043328):
    return pl.pallas_call(kernel,in_specs=in_specs,out_specs=out_specs,out_shape=outs,scratch_shapes=scratch,
        compiler_params=pltpu.CompilerParams(collective_id=cid,has_side_effects=True,vmem_limit_bytes=limit),name=name)(*ins)

def attn_fwd_kernel(bq,bk,ratio,scale,pos_ref,q_ref,k_ref,v_ref,prow_ref,o_ref,l_ref,vx_ref,acc_ref):
    i=pl.program_id(1)
    n=k_ref.shape[0]
    @pl.when(i==0)
    def _():
        vx_ref[:,:HD]=v_ref[...]
        vx_ref[:,HD:]=jnp.ones((n,HD),BF)
    q=q_ref[...]
    qs=jnp.concatenate([q[:,h*HD:(h+1)*HD] for h in range(ratio)],0)
    rows=lax.rem(lax.broadcasted_iota(jnp.int32,(ratio*bq,1),0),bq)+i*bq
    start=jnp.broadcast_to(prow_ref[...].astype(F32),(HD,bq)).T[:,0:1].astype(jnp.int32)
    start=rows-jnp.concatenate([start]*ratio,0)
    acc_ref[...]=jnp.zeros_like(acc_ref)
    c=scale*LOG2E
    def step(j,_):
        b=pl.multiple_of(j*bk,bk)
        s=dot(qs,k_ref[pl.ds(b,bk),:],NT)
        cols=lax.broadcasted_iota(jnp.int32,(1,bk),1)+b
        m=(rows>=cols)&(start<=cols)
        e=jnp.where(m,jnp.exp2(s*c),0.0).astype(BF)
        acc_ref[...]+=dot(e,vx_ref[pl.ds(b,bk),:])
        return 0
    lax.fori_loop((i*bq-pos_ref[i*bq])//bk,(i*bq+bq-1)//bk+1,step,0)
    a=acc_ref[...]
    l=a[:,HD:]
    o=(a[:,:HD]/l).astype(BF)
    lt=jnp.log2(l).T[0:1]
    for h in range(ratio):
        o_ref[:,h*HD:(h+1)*HD]=o[h*bq:(h+1)*bq]
        l_ref[h]=lt[:,h*bq:(h+1)*bq]

def attn_fwd(q,k,v,pos,bq,bk,scale):
    n,wq=q.shape; g=k.shape[1]//HD; ratio=wq//HD//g
    gs=pltpu.PrefetchScalarGridSpec(num_scalar_prefetch=1,grid=(g,n//bq),
        in_specs=[pl.BlockSpec((bq,ratio*HD),lambda g,i,p:(i,g)),
                  pl.BlockSpec((n,HD),lambda g,i,p:(0,g)),
                  pl.BlockSpec((n,HD),lambda g,i,p:(0,g)),
                  pl.BlockSpec((1,bq),lambda g,i,p:(0,i))],
        out_specs=[pl.BlockSpec((bq,ratio*HD),lambda g,i,p:(i,g)),
                   pl.BlockSpec((ratio,1,bq),lambda g,i,p:(g,0,i))],
        scratch_shapes=[pltpu.VMEM((n,2*HD),BF),pltpu.VMEM((ratio*bq,2*HD),F32)])
    return pl.pallas_call(functools.partial(attn_fwd_kernel,bq,bk,ratio,scale),grid_spec=gs,
        out_shape=[S_((n,wq),BF),S_((g*ratio,1,n),F32)],name='attn_fwd')(pos[0],q,k,v,pos)
def front_kernel(nc,x_ref,cot_ref,pos_ref,fr_ref,g_ref,gq_ref,gk_ref,wq_ref,wk_ref,wv_ref,
                 a_o,q_o,k_o,v_o,xh_o,r_o,cos_o,sin_o,early_o,late_o,
                 xf,a_s,q_s,k_s,v_s,xh_s,r_s,cost,sint,cosn,sinn,lsem,osem,ss,rs,es):
    t,mate,far,diag=group()
    per=x_ref.shape[0]; r=per//nc; n=xf.shape[0]; half=HD//2
    outs=[(a_s,a_o,0),(q_s,q_o,0),(k_s,k_o,0),(v_s,v_o,0),(xh_s,xh_o,1),(r_s,r_o,2)]
    own=pltpu.make_async_copy(x_ref,rows_of(xf,t,0,per,per),lsem)
    own.start()
    greet([('tensor',mate),('tensor',far)])
    across=lambda j: send(x_ref.at[span(j,r)],rows_of(xf,t,j,r,per),ss.at[0,j],rs.at[0,j],far)
    beside=lambda j: send(x_ref.at[span(j,r)],rows_of(xf,t,j,r,per),ss.at[1,j],rs.at[1,j],mate)
    onward=lambda j: send(rows_of(xf,far,j,r,per),rows_of(xf,far,j,r,per),ss.at[2,j],rs.at[2,j],mate)
    each(nc,lambda j: across(j).start())
    each(nc,lambda j: beside(j).start())
    early=send(cot_ref.at[0:early_o.shape[0]],early_o,es.at[0],es.at[1],far)
    keep=pltpu.make_async_copy(cot_ref.at[early_o.shape[0]:per],late_o,es.at[2])
    keep.start()
    gain,gq,gk=vec(g_ref),vec(gq_ref),vec(gk_ref)
    tt=256
    def table(i):
        c=span(i,tt)
        ang=fr_ref[...]*pos_ref[:,c].astype(F32)
        co,si=jnp.cos(ang),jnp.sin(ang)
        ct=jnp.concatenate([co,co],0); st=jnp.concatenate([-si,si],0)
        cost[:,c]=ct; sint[:,c]=st
        cosn[c,:]=ct.T; sinn[c,:]=st.T
    each(n//tt,table)
    tabs=[pltpu.make_async_copy(cost,cos_o,osem.at[6,0]),pltpu.make_async_copy(sint,sin_o,osem.at[7,0])]
    for c in tabs: c.start()
    def out_copy(o,i):
        s,d,ax=outs[o]
        c=span(i,r)
        at=(c,(slice(None),c),(slice(None),slice(None),c))[ax]
        return pltpu.make_async_copy(s.at[at],d.at[at],osem.at[o,i])
    def tile(b,j):
        p=pl.multiple_of(b*per+j*r,r)
        rows=pl.ds(p,r)
        x=xf[rows,:].astype(F32)
        a=(x*lax.rsqrt(jnp.mean(x*x,-1,keepdims=True)+EPS)*gain).astype(BF)
        a_s[rows,:]=a
        v_s[rows,:]=dot(a,wv_ref[...]).astype(BF)
        cos=cosn[rows,:]; sin=sinn[rows,:]
        h0=0
        for w_ref,g,dst in ((wq_ref,gq,q_s),(wk_ref,gk,k_s)):
            raw=dot(a,w_ref[...])
            for h in range(raw.shape[1]//HD):
                rh=raw[:,h*HD:(h+1)*HD]
                u=rh*lax.rsqrt(jnp.mean(rh*rh,-1,keepdims=True)+EPS)*g
                dst[rows,h*HD:(h+1)*HD]=(u*cos+pltpu.roll(u,half,1)*sin).astype(BF)
                rt=rh.T
                rr=lax.rsqrt(jnp.mean(rt*rt,0,keepdims=True)+EPS)
                xh_s[(h0+h)*HD:(h0+h+1)*HD,rows]=(rt*rr).astype(BF)
                r_s[h0+h,:,rows]=rr
            h0+=raw.shape[1]//HD
        for o in range(6): out_copy(o,b*nc+j).start()
    own.wait()
    each(nc,lambda j: tile(t,j))
    each(nc,lambda j: beside(j).wait_recv())
    each(nc,lambda j: tile(mate,j))
    def body(j):
        across(j).wait_recv()
        pl.when(j==nc-1)(lambda: early.start())
        onward(j).start()
        tile(far,j)
        onward(j).wait_recv()
        tile(diag,j)
    each(nc,body)
    def drain(j):
        across(j).wait_send(); beside(j).wait_send(); onward(j).wait_send()
    each(nc,drain)
    def flush(i):
        for o in range(6): out_copy(o,i).wait()
    each(n//r,flush)
    for c in tabs: c.wait()
    early.wait()
    keep.wait()

def front(x,cot,pos,freqs,gain,gq,gk,wq,wk,wv,first,nc,cid):
    n=4*x.shape[0]; d=x.shape[1]
    wide=wq.shape[1]+wk.shape[1]
    shapes=[((n,d),BF),((n,wq.shape[1]),BF),((n,wk.shape[1]),BF),((n,wv.shape[1]),BF),((wide,n),BF),((wide//HD,1,n),F32),((HD,n),F32),((HD,n),F32)]
    return call(functools.partial(front_kernel,nc),(x,cot,pos,freqs,gain,gq,gk,wq,wk,wv),[S_(*s) for s in shapes]+[S_((first,d),BF),S_((x.shape[0]-first,d),BF)],
        [pltpu.VMEM((n,d),BF)]+[pltpu.VMEM(*s) for s in shapes]+[pltpu.VMEM((n,HD),F32)]*2+[D_,D_((8,4*nc)),D_((3,nc)),D_((3,nc)),D_((3,))],cid,'front',[A_]*10,[A_]*2+[V_]*8)
def ring_neighbours(d):
    me=lax.axis_index('dp')
    half=d//2
    odd=lax.rem(me,2); up=me//2
    pos=odd*(d-1-2*up)+up
    def at(p):
        hi=p//half
        return hi*(2*(d-1-p)+1)+(1-hi)*2*p
    return pos,at(lax.rem(pos+1,d)),at(lax.rem(pos+d-1,d))

class Ring:
    def __init__(self,d,sems,make=None):
        self.d,self.sems,self.make=d,sems,make
        self.pos,right,left=ring_neighbours(d)
        self.to=(right,left)
        self.units=[]
    def add(self,s,rc,mine,sbuf,recv,out): self.units.append((s,rc,mine,sbuf,recv,out))
    def chunk(self,s,k): return lax.rem(self.pos-k+2*self.d,self.d) if s==0 else lax.rem(self.pos+k,self.d)
    def rs(self,u,k,src):
        return send(src,self.units[u][4].at[k],self.sems[0].at[u,k],self.sems[1].at[u,k],self.to[self.units[u][0]],'dp')
    def ag(self,u,k,c):
        s,rc,_,_,_,out=self.units[u]
        ref=out.at[span(c,rc)]
        return send(ref,ref,self.sems[2].at[u,k],self.sems[3].at[u,k],self.to[s],'dp')
    def start(self):
        for u,(s,rc,mine,sbuf,recv,out) in enumerate(self.units):
            sbuf[...]=mine(0).astype(BF)
            self.rs(u,0,sbuf).start()
    def reduce_step(self,k):
        if self.make: self.make(k)
        for u,(s,rc,mine,sbuf,recv,out) in enumerate(self.units):
            self.rs(u,k-1,sbuf).wait_recv()
            val=(mine(k)+recv[k-1].astype(F32)).astype(BF)
            @pl.when(k<self.d-1)
            def _():
                recv[k-1]=val
                self.rs(u,k,recv.at[k-1]).start()
            @pl.when(k==self.d-1)
            def _():
                c=self.chunk(s,k)
                out[span(c,rc),:]=val
                self.ag(u,0,c).start()
    def gather_step(self,k):
        for u,(s,rc,mine,sbuf,recv,out) in enumerate(self.units):
            c=self.chunk(s,k-1)
            self.ag(u,k-1,c).wait_recv()
            @pl.when(k<self.d-1)
            def _(): self.ag(u,k,c).start()
    def any_step(self,m):
        pl.when(m<self.d)(lambda: self.reduce_step(m))
        pl.when(m>=self.d)(lambda: self.gather_step(m-self.d+1))
    def drain(self):
        def body(k):
            for u,(s,rc,mine,sbuf,recv,out) in enumerate(self.units):
                self.rs(u,k,sbuf).wait_send()
                self.ag(u,k,0).wait_send()
        each(self.d-1,body)

class Scatter:
    def __init__(self,ids,per,rbuf,fbuf,ybuf,acc,ss,rs):
        self.t,self.mate,self.far,self.diag=ids
        self.per=per; self.rbuf,self.fbuf,self.ybuf,self.acc,self.ss,self.rs=rbuf,fbuf,ybuf,acc,ss,rs
    @staticmethod
    def scratch(per,w): return [pltpu.VMEM((2,per,w),BF),pltpu.VMEM((per,w),BF),pltpu.VMEM((per,w),BF),pltpu.VMEM((per,w),F32),D_((3,)),D_((3,))]
    def to_mate(self,i,src): return send(src,self.rbuf.at[i],self.ss.at[i],self.rs.at[i],self.mate)
    def across(self): return send(self.fbuf,self.ybuf,self.ss.at[2],self.rs.at[2],self.far)
    def pair(self,far_part,own_part,base=None):
        self.pair_far(far_part)
        self.pair_own(own_part,base)
    def pair_far(self,far_part):
        self.to_mate(1,self.fbuf).wait_recv()
        def far_rows(r): self.fbuf[r,:]=(far_part[r,:].astype(F32)+self.rbuf[1,r,:].astype(F32)).astype(BF)
        each_rows(self.per,far_rows)
        self.across().start()
    def pair_own(self,own_part,base=None):
        self.to_mate(0,self.fbuf).wait_recv()
        def own_rows(r):
            v=own_part[r,:].astype(F32)+self.rbuf[0,r,:].astype(F32)
            self.acc[r,:]=v if base is None else v+base[r,:]
        each_rows(self.per,own_rows)
    def result(self,f):
        self.across().wait_recv()
        each_rows(self.per,lambda r: f(r,self.acc[r,:]+self.ybuf[r,:].astype(F32)))
    def drain(self):
        self.to_mate(0,self.fbuf).wait_send(); self.to_mate(1,self.fbuf).wait_send(); self.across().wait_send()

def norm_bwd(v,gain,e):
    r=lax.rsqrt(jnp.mean(v*v,-1,keepdims=True)+EPS)
    vh=v*r
    ge=e*gain
    return r*(ge-vh*jnp.mean(vh*ge,-1,keepdims=True)),jnp.sum(e*vh,0,keepdims=True)
def mid_kernel(nc,att_ref,wo_ref,x_ref,cot_ref,early_ref,late_ref,wg_ref,wu_ref,wd_ref,g_ref,
               hid_ref,a_o,act_o,dg_o,du_o,op_o,da_o,dy_o,
               attv,wov,dyv,wgv,wuv,wdv,full,act_s,dg_s,du_s,op_s,da_s,acc,pbuf,rbuf,fbuf,ybuf,lsem,osem,ss,rs,dsem):
    t,mate,far,diag=group()
    per=x_ref.shape[0]; r=per//nc; n=full.shape[0]
    ne=early_ref.shape[0]
    loads=[pltpu.make_async_copy(s,d,lsem.at[i]) for i,(s,d) in enumerate(((att_ref,attv),(wo_ref,wov),(cot_ref,rows_of(dyv,t,0,per,per)),(wg_ref,wgv),(wu_ref,wuv),(wd_ref,wdv),(early_ref,dyv.at[pl.ds(pl.multiple_of(far*per,per),ne)]),(late_ref,dyv.at[pl.ds(pl.multiple_of(far*per+ne,ne),per-ne)])))]
    for c in loads: c.start()
    greet([('tensor',mate),('tensor',far)])
    dys=[send(cot_ref,rows_of(dyv,t,0,per,per),dsem.at[0],dsem.at[1],mate),send(early_ref,dyv.at[pl.ds(pl.multiple_of(far*per,per),ne)],dsem.at[2],dsem.at[3],mate),send(late_ref,dyv.at[pl.ds(pl.multiple_of(far*per+ne,ne),per-ne)],dsem.at[4],dsem.at[5],mate)]
    outs=[(full,a_o),(act_s,act_o),(dg_s,dg_o),(du_s,du_o),(op_s,op_o),(da_s,da_o)]
    gain=vec(g_ref)
    def proj(b,j):
        return dot(rows_of(attv,b,j,r,per)[...],wov[...])
    def to_mate(i,j):
        return send(pbuf.at[i,pl.ds(pl.multiple_of(j*r,r),r)],rbuf.at[i,pl.ds(pl.multiple_of(j*r,r),r)],ss.at[i,j],rs.at[i,j],mate)
    def to_far(j):
        rr=pl.ds(pl.multiple_of(j*r,r),r)
        return send(fbuf.at[rr],ybuf.at[rr],ss.at[2,j],rs.at[2,j],far)
    def share(j,i,peer):
        return send(rows_of(full,t,j,r,per),rows_of(full,t,j,r,per),ss.at[i,j],rs.at[i,j],peer)
    def forward(j):
        return send(rows_of(full,far,j,r,per),rows_of(full,far,j,r,per),ss.at[5,j],rs.at[5,j],mate)
    loads[0].wait(); loads[1].wait()
    def reduce(j,_):
        rr=pl.ds(pl.multiple_of(j*r,r),r)
        pbuf[1,rr,:]=proj(diag,j).astype(BF); to_mate(1,j).start()
        pbuf[0,rr,:]=proj(mate,j).astype(BF); to_mate(0,j).start()
        f=proj(far,j)
        to_mate(1,j).wait_recv()
        fbuf[rr,:]=(f+rbuf[1,rr,:].astype(F32)).astype(BF)
        to_far(j).start()
        @pl.when(j==0)
        def _():
            for c in dys: c.start()
        o=proj(t,j)
        to_mate(0,j).wait_recv()
        acc[rr,:]=o+rbuf[0,rr,:].astype(F32)+x_ref[rr,:].astype(F32)
        return 0
    lax.fori_loop(0,nc,reduce,0)
    for i in range(2,8): loads[i].wait()
    for c in dys: c.wait_recv()
    dyc=pltpu.make_async_copy(dyv,dy_o,lsem.at[8])
    dyc.start()
    def mlp_rows(b,j):
        rows=pl.ds(pl.multiple_of(b*per+j*r,r),r)
        a=full[rows,:]
        gate=dot(a,wgv[...]); up=dot(a,wuv[...])
        dact=dot(dyv[rows,:],wdv[...],NT)
        sig=1.0/(1.0+jnp.exp(-gate))
        sl=gate*sig
        act=(sl*up).astype(BF)
        act_s[rows,:]=act
        dg=(dact*up*(sig*(1.0+gate*(1.0-sig)))).astype(BF)
        du=(dact*sl).astype(BF)
        dg_s[rows,:]=dg; du_s[rows,:]=du
        op_s[rows,:]=dot(act,wdv[...]).astype(BF)
        da_s[rows,:]=(dot(dg,wgv[...],NT)+dot(du,wuv[...],NT)).astype(BF)
        for o,(s,d) in enumerate(outs):
            pltpu.make_async_copy(s.at[rows],d.at[rows],osem.at[o,b*nc+j]).start()
    def near(j,_):
        rr=pl.ds(pl.multiple_of(j*r,r),r)
        to_far(j).wait_recv()
        h=acc[rr,:]+ybuf[rr,:].astype(F32)
        hid_ref[rr,:]=h
        rows_of(full,t,j,r,per)[...]=(h*lax.rsqrt(jnp.mean(h*h,-1,keepdims=True)+EPS)*gain).astype(BF)
        share(j,3,far).start(); share(j,4,mate).start()
        def both(i,_):
            @pl.when(i==1)
            def _(): share(j,4,mate).wait_recv()
            mlp_rows(t+i*(mate-t),j)
            return 0
        lax.fori_loop(0,2,both,0)
        return 0
    lax.fori_loop(0,nc,near,0)
    def away(j,_):
        share(j,3,far).wait_recv()
        forward(j).start()
        def both(i,_):
            @pl.when(i==1)
            def _(): forward(j).wait_recv()
            mlp_rows(far+i*(diag-far),j)
            return 0
        lax.fori_loop(0,2,both,0)
        return 0
    lax.fori_loop(0,nc,away,0)
    def drain(j,_):
        to_mate(0,j).wait_send(); to_mate(1,j).wait_send(); to_far(j).wait_send()
        share(j,3,far).wait_send(); share(j,4,mate).wait_send(); forward(j).wait_send()
        return 0
    lax.fori_loop(0,nc,drain,0)
    def flush(i,_):
        rows=pl.ds(pl.multiple_of(i*r,r),r)
        for o,(s,d) in enumerate(outs):
            pltpu.make_async_copy(s.at[rows],d.at[rows],osem.at[o,i]).wait()
        return 0
    lax.fori_loop(0,n//r,flush,0)
    dyc.wait()
    for c in dys: c.wait_send()

def middle(att,wo,x,cot,early,late,wg,wu,wd,gain,nc,cid):
    n=att.shape[0]; per,d=x.shape; f=wg.shape[1]
    rows=[((n,d),BF),((n,f),BF),((n,f),BF),((n,f),BF),((n,d),BF),((n,d),BF)]
    return call(functools.partial(mid_kernel,nc),(att,wo,x,cot,early,late,wg,wu,wd,gain),[S_((per,d),F32)]+[S_(*s) for s in rows]+[S_((n,d),BF)],
        [pltpu.VMEM(s,BF) for s in (att.shape,wo.shape,(n,d),wg.shape,wu.shape,wd.shape)]+[pltpu.VMEM(*s) for s in rows]+
        [pltpu.VMEM((per,d),F32),pltpu.VMEM((2,per,d),BF),pltpu.VMEM((2,per,d),BF),pltpu.VMEM((per,d),BF),pltpu.VMEM((per,d),BF),
         D_((9,)),D_((6,4*nc)),D_((6,nc)),D_((6,nc)),D_((6,))],cid,'middle',[V_]+[A_]*7,[A_,A_,V_,A_,A_,A_,A_,A_,A_,V_])
def post_kernel(d,fused,hid_ref,cot_ref,g_ref,wo_ref,a_ref,dy_ref,act_ref,dg_ref,du_ref,da_ref,att_ref,
                dhid_ref,gg_ref,dwg_ref,dwu_ref,dwd_ref,dwo_ref,dout_o,
                av,ac,dyv,actv,dgv,duv,attv,full,doutv,parts,ownbuf,sbuf,recv,lsem,osem,ss,rs,m0,m1,m2,m3,oacc,*rest):
    ids=t,mate,far,diag=group()
    per,dm=hid_ref.shape; n=full.shape[0]; f=dgv.shape[1]; rc=dm//d
    rs1=Scatter(ids,per,*rest[:6])
    whole=None if fused else rest[6]
    def make(k):
        if fused:
            for s in range(2): ownbuf[s]=dot(av[:,span(ring.chunk(s,k),rc)],(dgv,duv)[s][...],TN)
    ring=Ring(d,(m0,m1,m2,m3),make)
    nu=3
    w=f//nu
    for j in range(nu):
        for s,out in enumerate((dwg_ref,dwu_ref)):
            lo,hi=j*w,(j+1)*w
            def mine(k,s=s,lo=lo,hi=hi):
                if fused: return ownbuf[s,:,lo:hi]
                return whole[s,span(ring.chunk(s,k),rc),lo:hi].astype(F32)
            ring.add(s,rc,mine,sbuf.at[s,:,lo:hi],recv.at[s,:,:,lo:hi],out.at[:,lo:hi])
    c0=pl.multiple_of(ring.chunk(0,0)*rc,128) if fused else 0
    loads=[pltpu.make_async_copy(s,x,lsem.at[i]) for i,(s,x) in enumerate(((dg_ref,dgv),(a_ref.at[:,pl.ds(c0,128)],ac),(du_ref,duv),(a_ref,av),(dy_ref,dyv),(act_ref,actv),(att_ref,attv)))]
    blk=lambda ref,b: rows_of(ref,b,0,per,per)
    parts_=[pltpu.make_async_copy(blk(da_ref,b),parts.at[i],lsem.at[7+i]) for i,b in enumerate((far,t))]
    for c in loads[:4]+parts_+loads[4:]: c.start()
    greet([('tensor',mate),('tensor',far),('dp',ring.to[0]),('dp',ring.to[1])])
    rs1.to_mate(1,blk(da_ref,diag)).start(); rs1.to_mate(0,blk(da_ref,mate)).start()
    for c in loads[:3]: c.wait()
    if fused:
        for s in range(2): ownbuf[s]=dot(ac[...],(dgv,duv)[s][...],TN)
        ring.start()
        loads[3].wait()
    else:
        loads[3].wait()
        for s in range(2):
            def tile(i,s=s): whole[s,span(i,128),:]=dot(av[:,span(i,128)],(dgv,duv)[s][...],TN).astype(BF)
            each(dm//128,tile)
        ring.start()
    share=lambda i,p: send(blk(full,t),blk(full,t),ss.at[i],rs.at[i],p)
    onward=lambda: send(blk(full,far),blk(full,far),ss.at[2],rs.at[2],mate)
    def e1():
        for c in parts_: c.wait()
        rs1.pair(parts.at[0],parts.at[1])
    def e2():
        gg_ref[...]=jnp.zeros_like(gg_ref)
        mine=blk(full,t)
        gain=vec(g_ref)
        def rows(r,da):
            dh,gg=norm_bwd(hid_ref[r,:],gain,da)
            dh=dh+cot_ref[r,:].astype(F32)
            dhid_ref[r,:]=dh; gg_ref[...]+=gg
            mine[r,:]=dh.astype(BF)
        rs1.result(rows)
        share(0,far).start(); share(1,mate).start()
    def down(i):
        dwd_ref[:,span(i,256)]=dot(actv[...],dyv[:,span(i,256)],TN).astype(BF)
    nd_=dm//256
    tt=256
    def dout_rows(b,last=False):
        def tile(i):
            rows=pl.ds(pl.multiple_of(b*per+i*tt,tt),tt)
            doutv[rows,:]=dot(full[rows,:],wo_ref[...],NT).astype(BF)
        each(per//tt,tile)
        if last: pltpu.make_async_copy(doutv,dout_o,osem.at[0]).start()
    def out_rows(b,last=False):
        rows=span(b,per)
        def out_tile(i):
            c=span(i,256)
            v=dot(attv[rows,:],full[rows,c],TN)
            if last: dwo_ref[:,c]=(oacc[:,c]+v).astype(BF)
            else: oacc[:,c]+=v
        each(dm//256,out_tile)
    def e3():
        loads[6].wait()
        oacc[...]=jnp.zeros_like(oacc)
        dout_rows(t)
    def e4():
        share(1,mate).wait_recv()
        dout_rows(mate)
    def e5():
        share(0,far).wait_recv()
        onward().start()
        dout_rows(far)
    def step(k):
        pl.when(k==1)(e1)
        @pl.when(k==2)
        def _():
            for c in loads[4:6]: c.wait()
        pl.when((k>=2)&(k<2+nd_))(lambda: down(k-2))
        pl.when(k==d-1)(e2)
        ring.reduce_step(k)
    lax.fori_loop(1,d,lambda k,_: (step(k),0)[1],0)
    def gstep(k):
        ring.gather_step(k)
        when_each(k,((1,e3),(2,lambda: out_rows(t)),(3,e4),(4,lambda: out_rows(mate)),(d-2,e5),(d-1,lambda: out_rows(far))))
    lax.fori_loop(1,d,lambda k,_: (gstep(k),0)[1],0)
    onward().wait_recv()
    dout_rows(diag,True)
    out_rows(diag,True)
    ring.drain(); rs1.drain()
    share(0,far).wait_send(); share(1,mate).wait_send(); onward().wait_send()
    pltpu.make_async_copy(doutv,dout_o,osem.at[0]).wait()

def post(hid,cot,gain,wo,a2,dy,act,dg,du,dap,att,d,cid):
    per,dm=hid.shape; n=a2.shape[0]; f=act.shape[1]
    fused=(dm//d)%128==0
    M=pltpu.VMEM
    wo_=wo.shape[0]
    return call(functools.partial(post_kernel,d,fused),(hid,cot,gain,wo,a2,dy,act,dg,du,dap,att),
        [S_((per,dm),F32),S_((1,dm),F32),S_((dm,f),BF),S_((dm,f),BF),S_((f,dm),BF),S_((wo_,dm),BF),S_((n,wo_),BF)],
        [M((n,dm),BF),M((n,128),BF),M((n,dm),BF),M((n,f),BF),M((n,f),BF),M((n,f),BF),M((n,wo_),BF),M((n,dm),BF),M((n,wo_),BF),M((2,per,dm),BF),
         M((2,dm//d,f),F32),M((2,dm//d,f),BF),M((2,d-1,dm//d,f),BF),D_((9,)),D_((1,)),D_((3,)),D_((3,))]+[D_((6,d-1))]*4+[M((wo_,dm),F32)]+Scatter.scratch(per,dm)+([] if fused else [M((2,dm,f),BF)]),
        cid,'post',[V_]*6+[A_],[V_]*4+[A_]*7)
def rot_norm_bwd(dt,xh,r,gain,cos,sin):
    h=HD//2
    du=dt*cos-jnp.concatenate([dt[h:],dt[:h]],0)*sin
    ge=du*gain
    return r*(ge-xh*jnp.mean(xh*ge,0,keepdims=True)),du*xh

def tail_kernel(d,nt,fused,bq,bk,scale,x_ref,g_ref,gq_ref,gk_ref,gm_ref,wq_ref,wk_ref,wv_ref,pos_ref,lse_ref,r_ref,dwd_ref,dwo_ref,
                q_ref,k_ref,v_ref,do_ref,att_ref,xh_ref,cos_ref,sin_ref,a_ref,op_ref,hid_ref,dhid_ref,
                out_o,dx_ref,dwq_o,dwk_o,dwv_o,dwd_o,dwo_o,ga_o,gm_o,gq_o,gk_o,
                u1,kv,vv,attv,xhv,cosv,sinv,dj,dka,dva,dqa,qs,os_,kt,dd,gacc,gcol,ac,
                pbuf,farbuf,ownbuf,gbuf,grecv,b2d,r2d,b2o,r2o,b3,r3,lsem,gs,gr,*sems):
    ids=t,mate,far,diag=group()
    per,dm=x_ref.shape; n=u1.shape[0]
    p,(t0,t1,t2,t3),rest=sems[:8],sems[8:12],sems[12:]
    wq,wk,wv,wo=attv.shape[1],kv.shape[1],vv.shape[1],dwo_ref.shape[0]
    rc=dm//d
    sc=Scatter(ids,per,*rest[:6]); so=Scatter(ids,per,*rest[6:12])
    whole=None if fused else rest[12]
    blk=lambda ref,b: rows_of(ref,b,0,per,per)
    loads=[pltpu.make_async_copy(s,x,lsem.at[i]) for i,(s,x) in enumerate(((q_ref,u1.at[:,0:wq]),(k_ref,kv),(v_ref,vv),(do_ref,u1.at[:,wq:2*wq]),(att_ref,attv),(xh_ref,xhv),(cos_ref,cosv),(sin_ref,sinv)))]
    h=dm//2; w1=h//2
    firsts=[Ring(d,p[0:4]),Ring(d,p[4:8])]
    for z,ring in enumerate(firsts):
        for src,b,rv,out in ((dwd_ref,b2d,r2d,dwd_o),(dwo_ref,b2o,r2o,dwo_o)):
            rr=src.shape[0]//d
            for s in range(2):
                cs=slice(s*h+z*w1,s*h+(z+1)*w1); bs=slice(z*w1,(z+1)*w1)
                ring.add(s,rr,lambda k,s=s,src=src,rr=rr,cs=cs,ring=ring: src[span(ring.chunk(s,k),rr),cs].astype(F32),b.at[s,:,bs],rv.at[s,:,:,bs],out.at[:,cs])
    first=firsts[0]
    def make(k):
        if fused:
            c=first.chunk(0,k); e=first.chunk(1,k)
            ownbuf[0]=dot(u1[:,span(c,rc)],dj[:,0:wq],TN)
            ownbuf[1]=dot(u1[:,span(e,rc)],dj[:,wq:2*wq],TN)
    second=Ring(d,(t0,t1,t2,t3),make)
    w2=128
    for lo in range(0,wq,w2):
        for s in range(2):
            out=dwq_o.at[:,lo:lo+w2] if s==0 else (dwk_o.at[:,lo:lo+w2] if lo<wk else dwv_o.at[:,lo-wk:lo-wk+w2])
            def mine(k,s=s,lo=lo):
                if fused: return ownbuf[s,:,lo:lo+w2]
                return whole[s,span(second.chunk(s,k),rc),lo:lo+w2].astype(F32)
            second.add(s,rc,mine,b3.at[s,:,lo:lo+w2],r3.at[s,:,:,lo:lo+w2],out)
    c0=pl.multiple_of(first.chunk(0,0)*rc,128) if fused else 0
    later=[pltpu.make_async_copy(a_ref.at[:,pl.ds(c0,128)],ac,lsem.at[8]),pltpu.make_async_copy(dhid_ref,dx_ref,lsem.at[9]),
           pltpu.make_async_copy(blk(op_ref,far),pbuf.at[0],lsem.at[10]),pltpu.make_async_copy(blk(op_ref,t),pbuf.at[1],lsem.at[11]),pltpu.make_async_copy(hid_ref,so.acc,lsem.at[12])]
    for c in loads+later: c.start()
    steps=[]
    for axis,m in (('tensor',nt),('dp',d)):
        b=1
        while b<m:
            steps.append((axis,b)); b*=2
    def partner(axis,b):
        me=lax.axis_index(axis)
        return me+b-2*b*lax.rem(me//b,2)
    greet([('tensor',mate),('tensor',far),('dp',first.to[0]),('dp',first.to[1])]+[(a,partner(a,b)) for a,b in steps])
    for ring in firsts: ring.start()
    so.to_mate(1,blk(op_ref,diag)).start(); so.to_mate(0,blk(op_ref,mate)).start()
    def pair_out():
        for c in later[2:]: c.wait()
        so.pair(pbuf.at[0],pbuf.at[1],so.acc)
    def finish_out():
        def rows(r,v): out_o[r,:]=v.astype(BF)
        so.result(rows)
    for i,ref in enumerate((gq_ref,gk_ref)): gcol[i]=jnp.broadcast_to(vec(ref),(HD,HD)).T
    gacc[...]=jnp.zeros_like(gacc)
    for c in loads[:5]: c.wait()
    groups=wk//HD; ratio=wq//wk; nb=n//bq; jb=bq//bk
    c2=scale*LOG2E
    total=4*(d-1)
    back=-(-LONGEST//bk)
    first_key=lambda i: jnp.maximum(jb*i-back,0)
    sizes=[jb*(i+1)-max(jb*i-back,0) for i in range(nb)]
    per_group=sum(sizes)
    full=[i for i in range(nb) if jb*i<=back]
    iters=groups*(per_group+nb*ratio)
    def before(i):
        u=jnp.minimum(i,len(full))
        return jb*u*(u+1)//2+(i-u)*(jb+back)
    hooks=iters
    def hook(it):
        when_each(it,((2,pair_out),(iters-1,finish_out)))
        for z in range(-(-total//iters)):
            m=it*total//iters+1+z
            for y in range(2): pl.when((m<=(it+1)*total//iters)&(lax.rem(m,2)==1-y))(lambda y=y: firsts[y].any_step((m+1)//2))
    def lane_tiles(dt,head,gi,cols,put):
        for z in range(dt.shape[1]//HD):
            cs=pl.ds(pl.multiple_of(cols+z*HD,HD),HD)
            dx,gg=rot_norm_bwd(dt[:,z*HD:(z+1)*HD]*scale,xhv[span(head,HD),cs].astype(F32),r_ref[head,:,cs],gcol[gi],cosv[:,cs],sinv[:,cs])
            gacc[gi]+=gg
            put(cs,dx.T.astype(BF))
    def one_group(g):
        gl=pl.multiple_of(g*HD,HD)
        kcols=pl.ds(gl,HD)
        def prep(i):
            kt[:,span(i,bq)]=kv[span(i,bq),kcols].T
            dka[span(i,bq),:]=jnp.zeros((bq,HD),F32); dva[span(i,bq),:]=jnp.zeros((bq,HD),F32)
        each(nb,prep)
        qcol=[pl.ds(pl.multiple_of(g*ratio*HD+x*HD,HD),HD) for x in range(ratio)]
        dcol=[pl.ds(pl.multiple_of(wq+g*ratio*HD+x*HD,HD),HD) for x in range(ratio)]
        def q_block(i):
            rows=span(i,bq)
            colq=lax.broadcasted_iota(jnp.int32,(1,bq),1)+i*bq
            st=colq-pos_ref[:,rows]
            for x in range(ratio):
                at=slice(x*bq,(x+1)*bq)
                qx=u1[rows,qcol[x]]; ox=u1[rows,dcol[x]]
                qs[at,:]=qx; os_[at,:]=ox
                pr=ox.astype(F32)*attv[rows,qcol[x]].astype(F32)
                hi=pr.astype(BF); lo=(pr-hi.astype(F32)).astype(BF)
                one=jnp.ones((8,HD),BF)
                dd[:,at]=dot(one,hi,NT)+dot(one,lo,NT)
                dd[0:1,ratio*bq+x*bq:ratio*bq+(x+1)*bq]=lse_ref[g*ratio+x,:,rows]
            dqa[...]=jnp.zeros_like(dqa)
            two=lambda v: jnp.concatenate([v]*ratio,1)
            cols,sts=two(colq),two(st)
            inner=dd[0:1,0:ratio*bq]; ls=dd[0:1,ratio*bq:]
            def key_block(j):
                b=span(j,bk)
                kb=kv[b,kcols]
                s=dot(kb,qs[...],NT)
                keys=lax.broadcasted_iota(jnp.int32,(bk,1),0)+j*bk
                p=jnp.where((cols>=keys)&(sts<=keys),jnp.exp2(s*c2-ls),0.0)
                ds=(p*(dot(vv[b,kcols],os_[...],NT)-inner)).astype(BF)
                dva[b,:]+=dot(p.astype(BF),os_[...])
                dka[b,:]+=dot(ds,qs[...])
                dqa[...]+=dot(kt[:,b],ds)
            def finish(x):
                if x==0:
                    @pl.when((g==0)&(i==0))
                    def _():
                        for c in loads[5:]: c.wait()
                def put(cs,v,x=x): dj[cs,qcol[x]]=v
                lane_tiles(dqa[:,x*bq:(x+1)*bq],g*ratio+x,0,i*bq,put)
            j0,j1=first_key(i),(i+1)*jb
            def slot(j,_):
                pl.when(j<j1)(lambda: key_block(j))
                for x in range(ratio): pl.when(j==j1+x)(lambda x=x: finish(x))
                hook(g*(per_group+nb*ratio)+before(i)+i*ratio+j-j0)
                return 0
            lax.fori_loop(j0,j1+ratio,slot,0)
        each(nb,q_block)
        def fin(i):
            rows=span(i,bq)
            dj[rows,pl.ds(pl.multiple_of(wq+wk+gl,HD),HD)]=dva[rows,:].astype(BF)
            def put(cs,v): dj[cs,pl.ds(pl.multiple_of(wq+gl,HD),HD)]=v
            lane_tiles(dka[rows,:].T,wq//HD+g,1,i*bq,put)
        each(nb,fin)
    each(groups,one_group)
    al=pltpu.make_async_copy(a_ref,u1,lsem.at[13])
    al.start()
    later[0].wait(); later[1].wait()
    if fused:
        ownbuf[0]=dot(ac[...],dj[:,0:wq],TN); ownbuf[1]=dot(ac[...],dj[:,wq:2*wq],TN)
    else:
        al.wait()
        for s in range(2):
            def tile(i,s=s): whole[s,span(i,128),:]=dot(u1[:,span(i,128)],dj[:,s*wq:(s+1)*wq],TN).astype(BF)
            each(dm//128,tile)
    second.start()
    if fused: al.wait()
    tp=256
    def part(b,ref,i):
        def tile(j):
            rows=pl.ds(pl.multiple_of(b*per+j*tp,tp),tp)
            v=dot(dj[rows,0:wq],wq_ref[...],NT)+dot(dj[rows,wq:wq+wk],wk_ref[...],NT)+dot(dj[rows,wq+wk:2*wq],wv_ref[...],NT)
            ref[i,span(j,tp),:]=v.astype(BF)
        each(per//tp,tile)
    part(diag,pbuf,1)
    sc.to_mate(1,pbuf.at[1]).start()
    part(far,farbuf,0)
    sc.pair_far(farbuf.at[0])
    def e0():
        part(mate,pbuf,0)
        sc.to_mate(0,pbuf.at[0]).start()
    def e1():
        part(t,farbuf,1)
        sc.pair_own(farbuf.at[1])
    def e2():
        gain=vec(g_ref)
        gbuf[:,0:dm]=jnp.zeros((1,dm),F32)
        gbuf[:,dm:2*dm]=gm_ref[...]
        gbuf[:,2*dm:2*dm+HD]=jnp.sum(gacc[0].T,0,keepdims=True)
        gbuf[:,2*dm+HD:2*dm+2*HD]=jnp.sum(gacc[1].T,0,keepdims=True)
        def rows(r,e):
            dv,gg=norm_bwd(x_ref[r,:].astype(F32),gain,e)
            dx_ref[r,:]+=dv
            gbuf[:,0:dm]+=gg
        sc.result(rows)
    def step(k):
        second.reduce_step(k)
        when_each(k,((1,e0),(2,e1)))
    lax.fori_loop(1,d,lambda k,_: (step(k),0)[1],0)
    cps=[send(grecv.at[2*i+1],grecv.at[2*i],gs.at[i],gr.at[i],partner(a,b),a) for i,(a,b) in enumerate(steps)]
    def turn(i):
        def f():
            if i==0: e2()
            else:
                cps[i-1].wait_recv()
                gbuf[...]+=grecv[2*i-2]
            if i<len(steps):
                grecv[2*i+1]=gbuf[...]
                cps[i].start()
        return f
    def gstep(k):
        when_each(k,[(i+2,turn(i)) for i in range(min(len(steps)+1,d-2))])
        second.gather_step(k)
    lax.fori_loop(1,d,lambda k,_: (gstep(k),0)[1],0)
    for i in range(d-2,len(steps)+1): turn(i)()
    ga_o[...]=gbuf[:,0:dm]; gm_o[...]=gbuf[:,dm:2*dm]; gq_o[...]=gbuf[:,2*dm:2*dm+HD]; gk_o[...]=gbuf[:,2*dm+HD:2*dm+2*HD]
    for ring in firsts: ring.drain()
    second.drain(); sc.drain(); so.drain()
    for c in cps: c.wait_send()

def tail(x,g,gq,gk,gm,wq,wk,wv,pos,lse,r,dwd,dwo,q,k,v,do,att,xh,cos,sin,a1,op,hid,dhid,d,nt,bq,bk,scale,cid):
    per,dm=x.shape; n=a1.shape[0]
    nq,nk,nv=q.shape[1],k.shape[1],v.shape[1]
    assert nq==nk+nv
    fused=(dm//d)%128==0
    M=pltpu.VMEM
    ns=sum((s-1).bit_length() for s in (d,nt))
    ratio=nq//nk; rc=dm//d; h=dm//2
    row=lambda c: S_((1,c),F32)
    rd,ro=dwd.shape[0]//d,dwo.shape[0]//d
    ins=(x,g,gq,gk,gm,wq,wk,wv,pos,lse,r,dwd,dwo,q,k,v,do,att,xh,cos,sin,a1,op,hid,dhid)
    return call(functools.partial(tail_kernel,d,nt,fused,bq,bk,scale),ins,
        [S_((per,dm),BF),S_((per,dm),F32),S_((dm,nq),BF),S_((dm,nk),BF),S_((dm,nv),BF),S_(dwd.shape,BF),S_(dwo.shape,BF),row(dm),row(dm),row(HD),row(HD)],
        [M((n,2*nq),BF),M((n,nk),BF),M((n,nv),BF),M((n,nq),BF),M(xh.shape,BF),M(cos.shape,F32),M(sin.shape,F32),M((n,2*nq),BF),M((n,HD),F32),M((n,HD),F32),
         M((HD,ratio*bq),F32),M((ratio*bq,HD),BF),M((ratio*bq,HD),BF),M((HD,n),BF),M((8,2*ratio*bq),F32),M((2,HD,HD),F32),M((2,HD,HD),F32),M((n,128),BF),
         M((2,per,dm),BF),M((2,per,dm),BF),M((2,rc,nq),F32),M((1,2*dm+2*HD),F32),M((2*ns,1,2*dm+2*HD),F32),
         M((2,rd,h),BF),M((2,d-1,rd,h),BF),M((2,ro,h),BF),M((2,d-1,ro,h),BF),M((2,rc,nq),BF),M((2,d-1,rc,nq),BF),
         D_((14,)),D_((ns,)),D_((ns,))]+[D_((4,d-1))]*8+[D_((2*nq//128,d-1))]*4+Scatter.scratch(per,dm)*2+([] if fused else [M((2,dm,nq),BF)]),
        cid,'tail',[V_]*11,[V_]*13+[A_]*12)
def widen_kernel(*refs):
    n=len(refs)//2
    for a,b in zip(refs[:n],refs[n:]): b[...]=a[...].astype(b.dtype)

def widen(arrays,plain,steps=4):
    specs=[pl.BlockSpec((a.shape[0]//steps,a.shape[1]),lambda i:(i,0)) for a in arrays+plain]
    return pl.pallas_call(widen_kernel,grid=(steps,),in_specs=specs,out_specs=specs,out_shape=[S_(a.shape,F32) for a in arrays]+[S_(a.shape,a.dtype) for a in plain],name='widen')(*arrays,*plain)

def local(nd,nt,tokens,w_query,w_key,w_value,w_out,w_gate,w_up,w_down,norm_attn,norm_mlp,norm_query,norm_key,cotangent,segments,positions):
    scale=HD**-0.5
    ne=cotangent.shape[0]//4
    a1,q,k,v,xh,r,cos,sin,early,late=front(tokens,cotangent,positions,jnp.asarray(FREQS[:,None]),norm_attn,norm_query,norm_key,w_query,w_key,w_value,ne,4,1)
    late=lax.ppermute(late,'tensor',[(i,(i+2)%nt) for i in range(nt)])
    att,lse=attn_fwd(q,k,v,positions,512,512,scale)
    att,late=lax.optimization_barrier((att,late))
    hid,a2,act,dg,du,outp,dap,dy=middle(att,w_out,tokens,cotangent,early,late,w_gate,w_up,w_down,norm_mlp,2,2)
    dhid,gm,dwg,dwu,dwd,dwo,dout=post(hid,cotangent,norm_mlp,w_out,a2,dy,act,dg,du,dap,att,nd,3)
    output,d_tokens,dwq,dwk,dwv,dwd,dwo,ga,gm,gq,gk=tail(tokens,norm_attn,norm_query,norm_key,gm,w_query,w_key,w_value,positions,lse,r,dwd,dwo,
        q,k,v,dout,att,xh,cos,sin,a1,outp,hid,dhid,nd,nt,512,256,scale,4)
    dwq,dwk,dwv,dwo,dwg,dwu,dwd,output,d_tokens=widen((dwq,dwk,dwv,dwo,dwg,dwu,dwd),(output,d_tokens))
    return (output,d_tokens,dwq,dwk,dwv,dwo,dwg,dwu,dwd,ga[0],gm[0],gq[0],gk[0])

def solution(mesh):
    nd,nt=mesh.shape['dp'],mesh.shape['tensor']
    row=P(('dp','tensor'),None); col=P(None,'tensor'); rw=P('tensor',None)
    return jax.shard_map(functools.partial(local,nd,nt),mesh=mesh,
        in_specs=(row,col,col,col,rw,col,col,rw,P(),P(),P(),P(),row,P('dp',None),P('dp',None)),
        out_specs=(row,row,col,col,col,rw,col,col,rw,P(),P(),P(),P()),check_vma=False)
```

```python
import functools, math
import numpy as np
import jax, jax.numpy as jnp
from jax import lax
from jax.sharding import PartitionSpec as P
from jax.experimental import pallas as pl
from jax.experimental.pallas import tpu as pltpu
HD=128
EPS=1e-6
F32=jnp.float32; BF=jnp.bfloat16
NT=(((1,),(1,)),((),()))
TN=(((0,),(0,)),((),()))
NN=(((1,),(0,)),((),()))
LOG2E=math.log2(math.e)
THETA=1000000.0
LONGEST=1024
FREQS=(THETA**(-np.arange(0,HD,2,dtype=np.float64)/HD)).astype(np.float32)
MESH=pl.DeviceIdType.MESH
D_=pltpu.SemaphoreType.DMA
S_=jax.ShapeDtypeStruct
V_=pl.BlockSpec(memory_space=pltpu.VMEM); A_=pl.BlockSpec(memory_space=pl.ANY)

def dot(a,b,dims=NN): return lax.dot_general(a,b,dims,preferred_element_type=F32)

def vec(ref): return ref[...].astype(F32).reshape(1,-1)

def group():
    t=lax.axis_index('tensor')
    mate=t+1-2*lax.rem(t,2)
    return t,mate,lax.rem(t+2,4),lax.rem(mate+2,4)

def greet(peers):
    barrier=pltpu.get_barrier_semaphore()
    for axis,p in peers:
        pl.semaphore_signal(barrier,inc=1,device_id={axis:p},device_id_type=MESH)
    pl.semaphore_wait(barrier,len(peers))

def send(src,dst,ss,rs,peer,axis='tensor'):
    return pltpu.make_async_remote_copy(src_ref=src,dst_ref=dst,send_sem=ss,recv_sem=rs,device_id={axis:peer},device_id_type=MESH)

def span(i,step,mult=None): return pl.ds(pl.multiple_of(i*step,mult or step),step)

def rows_of(ref,b,j,r,per): return ref.at[pl.ds(pl.multiple_of(b*per+j*r,r),r)]

def each(n,f):
    def body(i,_):
        f(i)
        return 0
    lax.fori_loop(0,n,body,0)

def each_rows(n,f,step=64): each(n//step,lambda i: f(span(i,step)))

def when_each(k,table):
    for at,f in table: pl.when(k==at)(f)

def call(kernel,ins,outs,scratch,cid,name,out_specs,in_specs,limit=67043328):
    return pl.pallas_call(kernel,in_specs=in_specs,out_specs=out_specs,out_shape=outs,scratch_shapes=scratch,
        compiler_params=pltpu.CompilerParams(collective_id=cid,has_side_effects=True,vmem_limit_bytes=limit),name=name)(*ins)

def attn_fwd_kernel(bq,bk,ratio,scale,pos_ref,q_ref,k_ref,v_ref,prow_ref,o_ref,l_ref,vx_ref,acc_ref):
    i=pl.program_id(1)
    n=k_ref.shape[0]
    @pl.when(i==0)
    def _():
        vx_ref[:,:HD]=v_ref[...]
        vx_ref[:,HD:]=jnp.ones((n,HD),BF)
    q=q_ref[...]
    qs=jnp.concatenate([q[:,h*HD:(h+1)*HD] for h in range(ratio)],0)
    rows=lax.rem(lax.broadcasted_iota(jnp.int32,(ratio*bq,1),0),bq)+i*bq
    start=jnp.broadcast_to(prow_ref[...].astype(F32),(HD,bq)).T[:,0:1].astype(jnp.int32)
    start=rows-jnp.concatenate([start]*ratio,0)
    acc_ref[...]=jnp.zeros_like(acc_ref)
    c=scale*LOG2E
    def step(j,_):
        b=pl.multiple_of(j*bk,bk)
        s=dot(qs,k_ref[pl.ds(b,bk),:],NT)
        cols=lax.broadcasted_iota(jnp.int32,(1,bk),1)+b
        m=(rows>=cols)&(start<=cols)
        e=jnp.where(m,jnp.exp2(s*c),0.0).astype(BF)
        acc_ref[...]+=dot(e,vx_ref[pl.ds(b,bk),:])
        return 0
    lax.fori_loop((i*bq-pos_ref[i*bq])//bk,(i*bq+bq-1)//bk+1,step,0)
    a=acc_ref[...]
    l=a[:,HD:]
    o=(a[:,:HD]/l).astype(BF)
    lt=jnp.log2(l).T[0:1]
    for h in range(ratio):
        o_ref[:,h*HD:(h+1)*HD]=o[h*bq:(h+1)*bq]
        l_ref[h]=lt[:,h*bq:(h+1)*bq]

def attn_fwd(q,k,v,pos,bq,bk,scale):
    n,wq=q.shape; g=k.shape[1]//HD; ratio=wq//HD//g
    gs=pltpu.PrefetchScalarGridSpec(num_scalar_prefetch=1,grid=(g,n//bq),
        in_specs=[pl.BlockSpec((bq,ratio*HD),lambda g,i,p:(i,g)),
                  pl.BlockSpec((n,HD),lambda g,i,p:(0,g)),
                  pl.BlockSpec((n,HD),lambda g,i,p:(0,g)),
                  pl.BlockSpec((1,bq),lambda g,i,p:(0,i))],
        out_specs=[pl.BlockSpec((bq,ratio*HD),lambda g,i,p:(i,g)),
                   pl.BlockSpec((ratio,1,bq),lambda g,i,p:(g,0,i))],
        scratch_shapes=[pltpu.VMEM((n,2*HD),BF),pltpu.VMEM((ratio*bq,2*HD),F32)])
    return pl.pallas_call(functools.partial(attn_fwd_kernel,bq,bk,ratio,scale),grid_spec=gs,
        out_shape=[S_((n,wq),BF),S_((g*ratio,1,n),F32)],name='attn_fwd')(pos[0],q,k,v,pos)
def front_kernel(nc,x_ref,cot_ref,pos_ref,fr_ref,g_ref,gq_ref,gk_ref,wq_ref,wk_ref,wv_ref,
                 a_o,q_o,k_o,v_o,xh_o,r_o,cos_o,sin_o,early_o,late_o,
                 xf,a_s,q_s,k_s,v_s,xh_s,r_s,cost,sint,cosn,sinn,lsem,osem,ss,rs,es):
    t,mate,far,diag=group()
    per=x_ref.shape[0]; r=per//nc; n=xf.shape[0]; half=HD//2
    outs=[(a_s,a_o,0),(q_s,q_o,0),(k_s,k_o,0),(v_s,v_o,0),(xh_s,xh_o,1),(r_s,r_o,2)]
    own=pltpu.make_async_copy(x_ref,rows_of(xf,t,0,per,per),lsem)
    own.start()
    greet([('tensor',mate),('tensor',far)])
    across=lambda j: send(x_ref.at[span(j,r)],rows_of(xf,t,j,r,per),ss.at[0,j],rs.at[0,j],far)
    beside=lambda j: send(x_ref.at[span(j,r)],rows_of(xf,t,j,r,per),ss.at[1,j],rs.at[1,j],mate)
    onward=lambda j: send(rows_of(xf,far,j,r,per),rows_of(xf,far,j,r,per),ss.at[2,j],rs.at[2,j],mate)
    each(nc,lambda j: across(j).start())
    each(nc,lambda j: beside(j).start())
    early=send(cot_ref.at[0:early_o.shape[0]],early_o,es.at[0],es.at[1],far)
    keep=pltpu.make_async_copy(cot_ref.at[early_o.shape[0]:per],late_o,es.at[2])
    keep.start()
    gain,gq,gk=vec(g_ref),vec(gq_ref),vec(gk_ref)
    tt=256
    def table(i):
        c=span(i,tt)
        ang=fr_ref[...]*pos_ref[:,c].astype(F32)
        co,si=jnp.cos(ang),jnp.sin(ang)
        ct=jnp.concatenate([co,co],0); st=jnp.concatenate([-si,si],0)
        cost[:,c]=ct; sint[:,c]=st
        cosn[c,:]=ct.T; sinn[c,:]=st.T
    each(n//tt,table)
    tabs=[pltpu.make_async_copy(cost,cos_o,osem.at[6,0]),pltpu.make_async_copy(sint,sin_o,osem.at[7,0])]
    for c in tabs: c.start()
    def out_copy(o,i):
        s,d,ax=outs[o]
        c=span(i,r)
        at=(c,(slice(None),c),(slice(None),slice(None),c))[ax]
        return pltpu.make_async_copy(s.at[at],d.at[at],osem.at[o,i])
    def tile(b,j):
        p=pl.multiple_of(b*per+j*r,r)
        rows=pl.ds(p,r)
        x=xf[rows,:].astype(F32)
        a=(x*lax.rsqrt(jnp.mean(x*x,-1,keepdims=True)+EPS)*gain).astype(BF)
        a_s[rows,:]=a
        v_s[rows,:]=dot(a,wv_ref[...]).astype(BF)
        cos=cosn[rows,:]; sin=sinn[rows,:]
        h0=0
        for w_ref,g,dst in ((wq_ref,gq,q_s),(wk_ref,gk,k_s)):
            raw=dot(a,w_ref[...])
            for h in range(raw.shape[1]//HD):
                rh=raw[:,h*HD:(h+1)*HD]
                u=rh*lax.rsqrt(jnp.mean(rh*rh,-1,keepdims=True)+EPS)*g
                dst[rows,h*HD:(h+1)*HD]=(u*cos+pltpu.roll(u,half,1)*sin).astype(BF)
                rt=rh.T
                rr=lax.rsqrt(jnp.mean(rt*rt,0,keepdims=True)+EPS)
                xh_s[(h0+h)*HD:(h0+h+1)*HD,rows]=(rt*rr).astype(BF)
                r_s[h0+h,:,rows]=rr
            h0+=raw.shape[1]//HD
        for o in range(6): out_copy(o,b*nc+j).start()
    own.wait()
    each(nc,lambda j: tile(t,j))
    each(nc,lambda j: beside(j).wait_recv())
    each(nc,lambda j: tile(mate,j))
    def body(j):
        across(j).wait_recv()
        pl.when(j==nc-1)(lambda: early.start())
        onward(j).start()
        tile(far,j)
        onward(j).wait_recv()
        tile(diag,j)
    each(nc,body)
    def drain(j):
        across(j).wait_send(); beside(j).wait_send(); onward(j).wait_send()
    each(nc,drain)
    def flush(i):
        for o in range(6): out_copy(o,i).wait()
    each(n//r,flush)
    for c in tabs: c.wait()
    early.wait()
    keep.wait()

def front(x,cot,pos,freqs,gain,gq,gk,wq,wk,wv,first,nc,cid):
    n=4*x.shape[0]; d=x.shape[1]
    wide=wq.shape[1]+wk.shape[1]
    shapes=[((n,d),BF),((n,wq.shape[1]),BF),((n,wk.shape[1]),BF),((n,wv.shape[1]),BF),((wide,n),BF),((wide//HD,1,n),F32),((HD,n),F32),((HD,n),F32)]
    return call(functools.partial(front_kernel,nc),(x,cot,pos,freqs,gain,gq,gk,wq,wk,wv),[S_(*s) for s in shapes]+[S_((first,d),BF),S_((x.shape[0]-first,d),BF)],
        [pltpu.VMEM((n,d),BF)]+[pltpu.VMEM(*s) for s in shapes]+[pltpu.VMEM((n,HD),F32)]*2+[D_,D_((8,4*nc)),D_((3,nc)),D_((3,nc)),D_((3,))],cid,'front',[A_]*10,[A_]*2+[V_]*8)
def ring_neighbours(d):
    me=lax.axis_index('dp')
    half=d//2
    odd=lax.rem(me,2); up=me//2
    pos=odd*(d-1-2*up)+up
    def at(p):
        hi=p//half
        return hi*(2*(d-1-p)+1)+(1-hi)*2*p
    return pos,at(lax.rem(pos+1,d)),at(lax.rem(pos+d-1,d))

class Ring:
    def __init__(self,d,sems,make=None):
        self.d,self.sems,self.make=d,sems,make
        self.pos,right,left=ring_neighbours(d)
        self.to=(right,left)
        self.units=[]
    def add(self,s,rc,mine,sbuf,recv,out): self.units.append((s,rc,mine,sbuf,recv,out))
    def chunk(self,s,k): return lax.rem(self.pos-k+2*self.d,self.d) if s==0 else lax.rem(self.pos+k,self.d)
    def rs(self,u,k,src):
        return send(src,self.units[u][4].at[k],self.sems[0].at[u,k],self.sems[1].at[u,k],self.to[self.units[u][0]],'dp')
    def ag(self,u,k,c):
        s,rc,_,_,_,out=self.units[u]
        ref=out.at[span(c,rc)]
        return send(ref,ref,self.sems[2].at[u,k],self.sems[3].at[u,k],self.to[s],'dp')
    def start(self):
        for u,(s,rc,mine,sbuf,recv,out) in enumerate(self.units):
            sbuf[...]=mine(0).astype(BF)
            self.rs(u,0,sbuf).start()
    def reduce_step(self,k):
        for u,(s,rc,mine,sbuf,recv,out) in enumerate(self.units):
            self.rs(u,k-1,sbuf).wait_recv()
            val=(mine(k)+recv[k-1].astype(F32)).astype(BF)
            @pl.when(k<self.d-1)
            def _():
                recv[k-1]=val
                self.rs(u,k,recv.at[k-1]).start()
            @pl.when(k==self.d-1)
            def _():
                c=self.chunk(s,k)
                out[span(c,rc),:]=val
                self.ag(u,0,c).start()
        if self.make: pl.when(k<self.d-1)(lambda: self.make(k+1))
    def gather_step(self,k):
        for u,(s,rc,mine,sbuf,recv,out) in enumerate(self.units):
            c=self.chunk(s,k-1)
            self.ag(u,k-1,c).wait_recv()
            @pl.when(k<self.d-1)
            def _(): self.ag(u,k,c).start()
    def any_step(self,m):
        pl.when(m<self.d)(lambda: self.reduce_step(m))
        pl.when(m>=self.d)(lambda: self.gather_step(m-self.d+1))
    def drain(self):
        def body(k):
            for u,(s,rc,mine,sbuf,recv,out) in enumerate(self.units):
                self.rs(u,k,sbuf).wait_send()
                self.ag(u,k,0).wait_send()
        each(self.d-1,body)

class Scatter:
    def __init__(self,ids,per,rbuf,fbuf,ybuf,acc,ss,rs):
        self.t,self.mate,self.far,self.diag=ids
        self.per=per; self.rbuf,self.fbuf,self.ybuf,self.acc,self.ss,self.rs=rbuf,fbuf,ybuf,acc,ss,rs
    @staticmethod
    def scratch(per,w): return [pltpu.VMEM((2,per,w),BF),pltpu.VMEM((per,w),BF),pltpu.VMEM((per,w),BF),pltpu.VMEM((per,w),F32),D_((3,)),D_((3,))]
    def to_mate(self,i,src): return send(src,self.rbuf.at[i],self.ss.at[i],self.rs.at[i],self.mate)
    def across(self): return send(self.fbuf,self.ybuf,self.ss.at[2],self.rs.at[2],self.far)
    def pair(self,far_part,own_part,base=None):
        self.pair_far(far_part)
        self.pair_own(own_part,base)
    def pair_far(self,far_part):
        self.to_mate(1,self.fbuf).wait_recv()
        def far_rows(r): self.fbuf[r,:]=(far_part[r,:].astype(F32)+self.rbuf[1,r,:].astype(F32)).astype(BF)
        each_rows(self.per,far_rows)
        self.across().start()
    def pair_own(self,own_part,base=None):
        self.to_mate(0,self.fbuf).wait_recv()
        def own_rows(r):
            v=own_part[r,:].astype(F32)+self.rbuf[0,r,:].astype(F32)
            self.acc[r,:]=v if base is None else v+base[r,:]
        each_rows(self.per,own_rows)
    def result(self,f):
        self.across().wait_recv()
        each_rows(self.per,lambda r: f(r,self.acc[r,:]+self.ybuf[r,:].astype(F32)))
    def drain(self):
        self.to_mate(0,self.fbuf).wait_send(); self.to_mate(1,self.fbuf).wait_send(); self.across().wait_send()

def norm_bwd(v,gain,e):
    r=lax.rsqrt(jnp.mean(v*v,-1,keepdims=True)+EPS)
    vh=v*r
    ge=e*gain
    return r*(ge-vh*jnp.mean(vh*ge,-1,keepdims=True)),jnp.sum(e*vh,0,keepdims=True)
def mid_kernel(nc,att_ref,wo_ref,x_ref,cot_ref,early_ref,late_ref,wg_ref,wu_ref,wd_ref,g_ref,
               hid_ref,a_o,act_o,dg_o,du_o,op_o,da_o,dy_o,
               attv,wov,dyv,wgv,wuv,wdv,full,act_s,dg_s,du_s,op_s,da_s,acc,pbuf,rbuf,fbuf,ybuf,lsem,osem,ss,rs,dsem):
    t,mate,far,diag=group()
    per=x_ref.shape[0]; r=per//nc; n=full.shape[0]
    ne=early_ref.shape[0]
    loads=[pltpu.make_async_copy(s,d,lsem.at[i]) for i,(s,d) in enumerate(((att_ref,attv),(wo_ref,wov),(cot_ref,rows_of(dyv,t,0,per,per)),(wg_ref,wgv),(wu_ref,wuv),(wd_ref,wdv),(early_ref,dyv.at[pl.ds(pl.multiple_of(far*per,per),ne)]),(late_ref,dyv.at[pl.ds(pl.multiple_of(far*per+ne,ne),per-ne)])))]
    for c in loads: c.start()
    greet([('tensor',mate),('tensor',far)])
    dys=[send(cot_ref,rows_of(dyv,t,0,per,per),dsem.at[0],dsem.at[1],mate),send(early_ref,dyv.at[pl.ds(pl.multiple_of(far*per,per),ne)],dsem.at[2],dsem.at[3],mate),send(late_ref,dyv.at[pl.ds(pl.multiple_of(far*per+ne,ne),per-ne)],dsem.at[4],dsem.at[5],mate)]
    outs=[(full,a_o),(act_s,act_o),(dg_s,dg_o),(du_s,du_o),(op_s,op_o),(da_s,da_o)]
    gain=vec(g_ref)
    def proj(b,j):
        return dot(rows_of(attv,b,j,r,per)[...],wov[...])
    def to_mate(i,j):
        return send(pbuf.at[i,pl.ds(pl.multiple_of(j*r,r),r)],rbuf.at[i,pl.ds(pl.multiple_of(j*r,r),r)],ss.at[i,j],rs.at[i,j],mate)
    def to_far(j):
        rr=pl.ds(pl.multiple_of(j*r,r),r)
        return send(fbuf.at[rr],ybuf.at[rr],ss.at[2,j],rs.at[2,j],far)
    def share(j,i,peer):
        return send(rows_of(full,t,j,r,per),rows_of(full,t,j,r,per),ss.at[i,j],rs.at[i,j],peer)
    def forward(j):
        return send(rows_of(full,far,j,r,per),rows_of(full,far,j,r,per),ss.at[5,j],rs.at[5,j],mate)
    loads[0].wait(); loads[1].wait()
    def reduce(j,_):
        rr=pl.ds(pl.multiple_of(j*r,r),r)
        pbuf[1,rr,:]=proj(diag,j).astype(BF); to_mate(1,j).start()
        pbuf[0,rr,:]=proj(mate,j).astype(BF); to_mate(0,j).start()
        f=proj(far,j)
        to_mate(1,j).wait_recv()
        fbuf[rr,:]=(f+rbuf[1,rr,:].astype(F32)).astype(BF)
        to_far(j).start()
        @pl.when(j==0)
        def _():
            for c in dys: c.start()
        o=proj(t,j)
        to_mate(0,j).wait_recv()
        acc[rr,:]=o+rbuf[0,rr,:].astype(F32)+x_ref[rr,:].astype(F32)
        return 0
    lax.fori_loop(0,nc,reduce,0)
    for i in range(2,8): loads[i].wait()
    for c in dys: c.wait_recv()
    dyc=pltpu.make_async_copy(dyv,dy_o,lsem.at[8])
    dyc.start()
    def mlp_rows(b,j):
        rows=pl.ds(pl.multiple_of(b*per+j*r,r),r)
        a=full[rows,:]
        gate=dot(a,wgv[...]); up=dot(a,wuv[...])
        dact=dot(dyv[rows,:],wdv[...],NT)
        sig=1.0/(1.0+jnp.exp(-gate))
        sl=gate*sig
        act=(sl*up).astype(BF)
        act_s[rows,:]=act
        dg=(dact*up*(sig*(1.0+gate*(1.0-sig)))).astype(BF)
        du=(dact*sl).astype(BF)
        dg_s[rows,:]=dg; du_s[rows,:]=du
        op_s[rows,:]=dot(act,wdv[...]).astype(BF)
        da_s[rows,:]=(dot(dg,wgv[...],NT)+dot(du,wuv[...],NT)).astype(BF)
        for o,(s,d) in enumerate(outs):
            pltpu.make_async_copy(s.at[rows],d.at[rows],osem.at[o,b*nc+j]).start()
    def near(j,_):
        rr=pl.ds(pl.multiple_of(j*r,r),r)
        to_far(j).wait_recv()
        h=acc[rr,:]+ybuf[rr,:].astype(F32)
        hid_ref[rr,:]=h
        rows_of(full,t,j,r,per)[...]=(h*lax.rsqrt(jnp.mean(h*h,-1,keepdims=True)+EPS)*gain).astype(BF)
        share(j,3,far).start(); share(j,4,mate).start()
        def both(i,_):
            @pl.when(i==1)
            def _(): share(j,4,mate).wait_recv()
            mlp_rows(t+i*(mate-t),j)
            return 0
        lax.fori_loop(0,2,both,0)
        return 0
    lax.fori_loop(0,nc,near,0)
    def away(j,_):
        share(j,3,far).wait_recv()
        forward(j).start()
        def both(i,_):
            @pl.when(i==1)
            def _(): forward(j).wait_recv()
            mlp_rows(far+i*(diag-far),j)
            return 0
        lax.fori_loop(0,2,both,0)
        return 0
    lax.fori_loop(0,nc,away,0)
    def drain(j,_):
        to_mate(0,j).wait_send(); to_mate(1,j).wait_send(); to_far(j).wait_send()
        share(j,3,far).wait_send(); share(j,4,mate).wait_send(); forward(j).wait_send()
        return 0
    lax.fori_loop(0,nc,drain,0)
    def flush(i,_):
        rows=pl.ds(pl.multiple_of(i*r,r),r)
        for o,(s,d) in enumerate(outs):
            pltpu.make_async_copy(s.at[rows],d.at[rows],osem.at[o,i]).wait()
        return 0
    lax.fori_loop(0,n//r,flush,0)
    dyc.wait()
    for c in dys: c.wait_send()

def middle(att,wo,x,cot,early,late,wg,wu,wd,gain,nc,cid):
    n=att.shape[0]; per,d=x.shape; f=wg.shape[1]
    rows=[((n,d),BF),((n,f),BF),((n,f),BF),((n,f),BF),((n,d),BF),((n,d),BF)]
    return call(functools.partial(mid_kernel,nc),(att,wo,x,cot,early,late,wg,wu,wd,gain),[S_((per,d),F32)]+[S_(*s) for s in rows]+[S_((n,d),BF)],
        [pltpu.VMEM(s,BF) for s in (att.shape,wo.shape,(n,d),wg.shape,wu.shape,wd.shape)]+[pltpu.VMEM(*s) for s in rows]+
        [pltpu.VMEM((per,d),F32),pltpu.VMEM((2,per,d),BF),pltpu.VMEM((2,per,d),BF),pltpu.VMEM((per,d),BF),pltpu.VMEM((per,d),BF),
         D_((9,)),D_((6,4*nc)),D_((6,nc)),D_((6,nc)),D_((6,))],cid,'middle',[V_]+[A_]*7,[A_,A_,V_,A_,A_,A_,A_,A_,A_,V_])
def post_kernel(d,fused,hid_ref,cot_ref,g_ref,wo_ref,a_ref,dy_ref,act_ref,dg_ref,du_ref,da_ref,att_ref,
                dhid_o,gg_ref,dwg_ref,dwu_ref,both_ref,dout_o,
                av,ac,dyv,actv,dgv,duv,attv,full,doutv,parts,ownbuf,sbuf,recv,dhid_ref,lsem,osem,ss,rs,m0,m1,m2,m3,oacc,*rest):
    ids=t,mate,far,diag=group()
    per,dm=hid_ref.shape; n=full.shape[0]; f=dgv.shape[1]; rc=dm//d
    rs1=Scatter(ids,per,*rest[:6])
    whole=None if fused else rest[6]
    def make(k):
        if fused:
            for s in range(2): ownbuf[s]=dot(av[:,span(ring.chunk(s,k),rc)],(dgv,duv)[s][...],TN)
    ring=Ring(d,(m0,m1,m2,m3),make)
    nu=3
    w=f//nu
    for j in range(nu):
        for s,out in enumerate((dwg_ref,dwu_ref)):
            lo,hi=j*w,(j+1)*w
            def mine(k,s=s,lo=lo,hi=hi):
                if fused: return ownbuf[s,:,lo:hi]
                return whole[s,span(ring.chunk(s,k),rc),lo:hi].astype(F32)
            ring.add(s,rc,mine,sbuf.at[s,:,lo:hi],recv.at[s,:,:,lo:hi],out.at[:,lo:hi])
    c0=pl.multiple_of(ring.chunk(0,0)*rc,128) if fused else 0
    loads=[pltpu.make_async_copy(s,x,lsem.at[i]) for i,(s,x) in enumerate(((dg_ref,dgv),(a_ref.at[:,pl.ds(c0,128)],ac),(du_ref,duv),(a_ref,av),(dy_ref,dyv),(act_ref,actv),(att_ref,attv)))]
    blk=lambda ref,b: rows_of(ref,b,0,per,per)
    parts_=[pltpu.make_async_copy(blk(da_ref,b),parts.at[i],lsem.at[7+i]) for i,b in enumerate((far,t))]
    for c in loads[:4]+parts_+loads[4:]: c.start()
    greet([('tensor',mate),('tensor',far),('dp',ring.to[0]),('dp',ring.to[1])])
    rs1.to_mate(1,blk(da_ref,diag)).start(); rs1.to_mate(0,blk(da_ref,mate)).start()
    for c in loads[:3]: c.wait()
    if fused:
        for s in range(2): ownbuf[s]=dot(ac[...],(dgv,duv)[s][...],TN)
        ring.start()
        loads[3].wait()
        make(1)
    else:
        loads[3].wait()
        for s in range(2):
            def tile(i,s=s): whole[s,span(i,128),:]=dot(av[:,span(i,128)],(dgv,duv)[s][...],TN).astype(BF)
            each(dm//128,tile)
        ring.start()
    share=lambda i,p: send(blk(full,t),blk(full,t),ss.at[i],rs.at[i],p)
    onward=lambda: send(blk(full,far),blk(full,far),ss.at[2],rs.at[2],mate)
    def e1():
        for c in parts_: c.wait()
        rs1.pair(parts.at[0],parts.at[1])
    def e2():
        gg_ref[...]=jnp.zeros_like(gg_ref)
        mine=blk(full,t)
        gain=vec(g_ref)
        def rows(r,da):
            dh,gg=norm_bwd(hid_ref[r,:],gain,da)
            dh=dh+cot_ref[r,:].astype(F32)
            dhid_ref[r,:]=dh; gg_ref[...]+=gg
            mine[r,:]=dh.astype(BF)
        rs1.result(rows)
        pltpu.make_async_copy(dhid_ref,dhid_o,osem.at[1]).start()
        share(0,far).start(); share(1,mate).start()
    rd,ro=f//d,wo_ref.shape[0]//d
    def put_rows(first,r,c,v):
        for j in range(d): both_ref[j*(rd+ro)+first:j*(rd+ro)+first+r,c]=v[j*r:(j+1)*r].astype(BF)
    def down(i):
        put_rows(0,rd,span(i,256),dot(actv[...],dyv[:,span(i,256)],TN))
    nd_=dm//256
    tt=256
    def dout_rows(b,last=False):
        def tile(i):
            rows=pl.ds(pl.multiple_of(b*per+i*tt,tt),tt)
            doutv[rows,:]=dot(full[rows,:],wo_ref[...],NT).astype(BF)
        each(per//tt,tile)
        if last: pltpu.make_async_copy(doutv,dout_o,osem.at[0]).start()
    def out_rows(b,last=False):
        rows=span(b,per)
        def out_tile(i):
            c=span(i,256)
            v=dot(attv[rows,:],full[rows,c],TN)
            if last: put_rows(rd,ro,c,oacc[:,c]+v)
            else: oacc[:,c]+=v
        each(dm//256,out_tile)
    def e3():
        loads[6].wait()
        oacc[...]=jnp.zeros_like(oacc)
        dout_rows(t)
    def e4():
        share(1,mate).wait_recv()
        dout_rows(mate)
    def e5():
        share(0,far).wait_recv()
        onward().start()
        dout_rows(far)
    def step(k):
        when_each(k,((1,e1),(d-1,e2)))
        ring.reduce_step(k)
        @pl.when(k==2)
        def _():
            for c in loads[4:6]: c.wait()
        pl.when((k>=2)&(k<2+nd_))(lambda: down(k-2))
    lax.fori_loop(1,d,lambda k,_: (step(k),0)[1],0)
    def gstep(k):
        ring.gather_step(k)
        when_each(k,((1,e3),(2,lambda: out_rows(t)),(3,e4),(4,lambda: out_rows(mate)),(d-3,e5),(d-2,lambda: out_rows(far))))
    lax.fori_loop(1,d,lambda k,_: (gstep(k),0)[1],0)
    onward().wait_recv()
    dout_rows(diag,True)
    out_rows(diag,True)
    ring.drain(); rs1.drain()
    share(0,far).wait_send(); share(1,mate).wait_send(); onward().wait_send()
    pltpu.make_async_copy(doutv,dout_o,osem.at[0]).wait()
    pltpu.make_async_copy(dhid_ref,dhid_o,osem.at[1]).wait()

def post(hid,cot,gain,wo,a2,dy,act,dg,du,dap,att,d,cid):
    per,dm=hid.shape; n=a2.shape[0]; f=act.shape[1]
    fused=(dm//d)%128==0
    M=pltpu.VMEM
    wo_=wo.shape[0]
    return call(functools.partial(post_kernel,d,fused),(hid,cot,gain,wo,a2,dy,act,dg,du,dap,att),
        [S_((per,dm),F32),S_((1,dm),F32),S_((dm,f),BF),S_((dm,f),BF),S_((f+wo_,dm),BF),S_((n,wo_),BF)],
        [M((n,dm),BF),M((n,128),BF),M((n,dm),BF),M((n,f),BF),M((n,f),BF),M((n,f),BF),M((n,wo_),BF),M((n,dm),BF),M((n,wo_),BF),M((2,per,dm),BF),
         M((2,dm//d,f),F32),M((2,dm//d,f),BF),M((2,d-1,dm//d,f),BF),M((per,dm),F32),D_((9,)),D_((2,)),D_((3,)),D_((3,))]+[D_((6,d-1))]*4+[M((wo_,dm),F32)]+Scatter.scratch(per,dm)+([] if fused else [M((2,dm,f),BF)]),
        cid,'post',[A_]+[V_]*4+[A_],[V_]*4+[A_]*7)
def rot_norm_bwd(dt,xh,r,gain,cos,sin):
    h=HD//2
    du=dt*cos-jnp.concatenate([dt[h:],dt[:h]],0)*sin
    ge=du*gain
    return r*(ge-xh*jnp.mean(xh*ge,0,keepdims=True)),du*xh

def tail_kernel(d,nt,nr,fused,bq,bk,scale,x_ref,g_ref,gq_ref,gk_ref,gm_ref,wq_ref,wk_ref,wv_ref,pos_ref,lse_ref,r_ref,both_ref,
                q_ref,k_ref,v_ref,do_ref,att_ref,xh_ref,cos_ref,sin_ref,a_ref,op_ref,hid_ref,dhid_ref,
                out_o,dx_ref,dwq_o,dwk_o,dwv_o,both_o,ga_o,gm_o,gq_o,gk_o,
                u1,kv,vv,attv,xhv,cosv,sinv,dj,dka,dva,dqa,qs,os_,kt,dd,gacc,gcol,ac,
                pbuf,farbuf,ownbuf,gbuf,grecv,bothv,outv,b2,r2,b3,r3,lsem,gs,gr,*sems):
    ids=t,mate,far,diag=group()
    per,dm=x_ref.shape; n=u1.shape[0]
    p,(t0,t1,t2,t3),rest=sems[0],sems[1:5],sems[5:]
    wq,wk,wv,wo=attv.shape[1],kv.shape[1],vv.shape[1],attv.shape[1]
    rc=dm//d
    sc=Scatter(ids,per,*rest[:6]); so=Scatter(ids,per,*rest[6:12])
    whole=None if fused else rest[12]
    blk=lambda ref,b: rows_of(ref,b,0,per,per)
    loads=[pltpu.make_async_copy(s,x,lsem.at[i]) for i,(s,x) in enumerate(((q_ref,u1.at[:,0:wq]),(k_ref,kv),(v_ref,vv),(do_ref,u1.at[:,wq:2*wq]),(att_ref,attv),(xh_ref,xhv),(cos_ref,cosv),(sin_ref,sinv)))]
    h=dm//2; w1=h//nr
    rr=both_ref.shape[0]//d
    def first_ring(y):
        ring=Ring(d,[p.at[i,y] for i in range(4)])
        for s in range(2):
            cs=pl.ds(pl.multiple_of(s*h+y*w1,w1),w1); bs=pl.ds(pl.multiple_of(y*w1,w1),w1)
            ring.add(s,rr,lambda k,s=s,cs=cs,ring=ring: both_ref[span(ring.chunk(s,k),rr),cs].astype(F32),b2.at[s,:,bs],r2.at[s,:,:,bs],bothv.at[:,cs])
        return ring
    first=first_ring(0)
    def make(k):
        if fused:
            c=first.chunk(0,k); e=first.chunk(1,k)
            ownbuf[0]=dot(u1[:,span(c,rc)],dj[:,0:wq],TN)
            ownbuf[1]=dot(u1[:,span(e,rc)],dj[:,wq:2*wq],TN)
    second=Ring(d,(t0,t1,t2,t3),make)
    w2=128
    for lo in range(0,wq,w2):
        for s in range(2):
            out=dwq_o.at[:,lo:lo+w2] if s==0 else (dwk_o.at[:,lo:lo+w2] if lo<wk else dwv_o.at[:,lo-wk:lo-wk+w2])
            def mine(k,s=s,lo=lo):
                if fused: return ownbuf[s,:,lo:lo+w2]
                return whole[s,span(second.chunk(s,k),rc),lo:lo+w2].astype(F32)
            second.add(s,rc,mine,b3.at[s,:,lo:lo+w2],r3.at[s,:,:,lo:lo+w2],out)
    c0=pl.multiple_of(first.chunk(0,0)*rc,128) if fused else 0
    later=[pltpu.make_async_copy(a_ref.at[:,pl.ds(c0,128)],ac,lsem.at[8]),pltpu.make_async_copy(dhid_ref,dx_ref,lsem.at[9]),
           pltpu.make_async_copy(blk(op_ref,far),pbuf.at[0],lsem.at[10]),pltpu.make_async_copy(blk(op_ref,t),pbuf.at[1],lsem.at[11]),pltpu.make_async_copy(hid_ref,so.acc,lsem.at[12])]
    for c in loads+later: c.start()
    steps=[]
    for axis,m in (('tensor',nt),('dp',d)):
        b=1
        while b<m:
            steps.append((axis,b)); b*=2
    def partner(axis,b):
        me=lax.axis_index(axis)
        return me+b-2*b*lax.rem(me//b,2)
    greet([('tensor',mate),('tensor',far),('dp',first.to[0]),('dp',first.to[1])]+[(a,partner(a,b)) for a,b in steps])
    each(nr,lambda y: first_ring(y).start())
    so.to_mate(1,blk(op_ref,diag)).start(); so.to_mate(0,blk(op_ref,mate)).start()
    def pair_out():
        for c in later[2:]: c.wait()
        so.pair(pbuf.at[0],pbuf.at[1],so.acc)
    def finish_out():
        def rows(r,v): outv[r,:]=v.astype(BF)
        so.result(rows)
    for i,ref in enumerate((gq_ref,gk_ref)): gcol[i]=jnp.broadcast_to(vec(ref),(HD,HD)).T
    gacc[...]=jnp.zeros_like(gacc)
    for c in loads[:5]: c.wait()
    groups=wk//HD; ratio=wq//wk; nb=n//bq; jb=bq//bk
    c2=scale*LOG2E
    total=2*nr*(d-1)
    assert bq==2*bk and LONGEST%bk==0
    back=LONGEST//bk
    first_key=lambda i: jnp.maximum(jb*i-back,0)
    sizes=[jb*(i+1)-max(jb*i-back,0) for i in range(nb)]
    per_group=sum(sizes)
    full=[i for i in range(nb) if jb*i<=back]
    iters=groups*(per_group+nb*ratio)
    def before(i):
        u=jnp.minimum(i,len(full))
        return jb*u*(u+1)//2+(i-u)*(jb+back)
    hooks=iters
    def hook(it):
        when_each(it,((2,pair_out),(iters-1,finish_out)))
        for z in range(-(-total//iters)):
            m=it*total//iters+1+z
            pl.when(m<=(it+1)*total//iters)(lambda: first_ring(lax.rem(m-1,nr)).any_step((m-1)//nr+1))
    def lane_tiles(dt,head,gi,cols,put):
        for z in range(dt.shape[1]//HD):
            cs=pl.ds(pl.multiple_of(cols+z*HD,HD),HD)
            dx,gg=rot_norm_bwd(dt[:,z*HD:(z+1)*HD]*scale,xhv[span(head,HD),cs].astype(F32),r_ref[head,:,cs],gcol[gi],cosv[:,cs],sinv[:,cs])
            gacc[gi]+=gg
            put(cs,dx.T.astype(BF))
    def one_group(g):
        gl=pl.multiple_of(g*HD,HD)
        kcols=pl.ds(gl,HD)
        def prep(i):
            kt[:,span(i,bq)]=kv[span(i,bq),kcols].T
            dka[span(i,bq),:]=jnp.zeros((bq,HD),F32); dva[span(i,bq),:]=jnp.zeros((bq,HD),F32)
        each(nb,prep)
        qcol=[pl.ds(pl.multiple_of(g*ratio*HD+x*HD,HD),HD) for x in range(ratio)]
        dcol=[pl.ds(pl.multiple_of(wq+g*ratio*HD+x*HD,HD),HD) for x in range(ratio)]
        def q_block(i):
            rows=span(i,bq)
            hb=bq//2
            wide=ratio*bq
            cq=[lax.broadcasted_iota(jnp.int32,(1,hb),1)+i*bq+y*hb for y in range(2)]
            cols=jnp.concatenate([cq[y] for y in range(2) for x in range(ratio)],1)
            sts=cols-jnp.concatenate([pos_ref[:,pl.ds(pl.multiple_of(i*bq+y*hb,hb),hb)] for y in range(2) for x in range(ratio)],1)
            one=jnp.ones((8,HD),BF)
            for y in range(2):
                for x in range(ratio):
                    at=slice((y*ratio+x)*hb,(y*ratio+x+1)*hb)
                    rh=pl.ds(pl.multiple_of(i*bq+y*hb,hb),hb)
                    qx=u1[rh,qcol[x]]; ox=u1[rh,dcol[x]]
                    qs[at,:]=qx; os_[at,:]=ox
                    pr=ox.astype(F32)*attv[rh,qcol[x]].astype(F32)
                    hi=pr.astype(BF); lo=(pr-hi.astype(F32)).astype(BF)
                    dd[:,at]=dot(one,hi,NT)+dot(one,lo,NT)
                    dd[0:1,wide+at.start:wide+at.stop]=lse_ref[g*ratio+x,:,rh]
            dqa[...]=jnp.zeros_like(dqa)
            def key_block(j,lo,hi,causal):
                b=span(j,bk)
                kb=kv[b,kcols]
                cs=slice(lo,hi)
                s=dot(kb,qs[cs,:],NT)
                keys=lax.broadcasted_iota(jnp.int32,(bk,1),0)+j*bk
                m=sts[:,cs]<=keys
                if causal: m=m&(cols[:,cs]>=keys)
                p=jnp.where(m,jnp.exp2(s*c2-dd[0:1,wide+lo:wide+hi]),0.0)
                ds=(p*(dot(vv[b,kcols],os_[cs,:],NT)-dd[0:1,cs])).astype(BF)
                dva[b,:]+=dot(p.astype(BF),os_[cs,:])
                dka[b,:]+=dot(ds,qs[cs,:])
                dqa[:,cs]+=dot(kt[:,b],ds)
            def finish(x):
                if x==0:
                    @pl.when((g==0)&(i==0))
                    def _():
                        for c in loads[5:]: c.wait()
                def put(cs,v,x=x): dj[cs,qcol[x]]=v
                lane_tiles(jnp.concatenate([dqa[:,(y*ratio+x)*hb:(y*ratio+x+1)*hb] for y in range(2)],1),g*ratio+x,0,i*bq,put)
            j0,j1=first_key(i),(i+1)*jb
            def slot(j,_):
                far_back=(jb*i>=back)&(j==jb*i-back)
                pl.when(far_back)(lambda: key_block(j,0,wide//2,False))
                pl.when((j<jb*i)&jnp.logical_not(far_back))(lambda: key_block(j,0,wide,False))
                pl.when(j==jb*i)(lambda: key_block(j,0,wide,True))
                pl.when(j==jb*i+1)(lambda: key_block(j,wide//2,wide,True))
                for x in range(ratio): pl.when(j==j1+x)(lambda x=x: finish(x))
                hook(g*(per_group+nb*ratio)+before(i)+i*ratio+j-j0)
                return 0
            lax.fori_loop(j0,j1+ratio,slot,0)
        each(nb,q_block)
        def fin(i):
            rows=span(i,bq)
            dj[rows,pl.ds(pl.multiple_of(wq+wk+gl,HD),HD)]=dva[rows,:].astype(BF)
            def put(cs,v): dj[cs,pl.ds(pl.multiple_of(wq+gl,HD),HD)]=v
            lane_tiles(dka[rows,:].T,wq//HD+g,1,i*bq,put)
        each(nb,fin)
    each(groups,one_group)
    saves=[pltpu.make_async_copy(bothv,both_o,lsem.at[14]),pltpu.make_async_copy(outv,out_o,lsem.at[15])]
    for c in saves: c.start()
    al=pltpu.make_async_copy(a_ref,u1,lsem.at[13])
    al.start()
    later[0].wait(); later[1].wait()
    if fused:
        ownbuf[0]=dot(ac[...],dj[:,0:wq],TN); ownbuf[1]=dot(ac[...],dj[:,wq:2*wq],TN)
    else:
        al.wait()
        for s in range(2):
            def tile(i,s=s): whole[s,span(i,128),:]=dot(u1[:,span(i,128)],dj[:,s*wq:(s+1)*wq],TN).astype(BF)
            each(dm//128,tile)
    second.start()
    if fused:
        al.wait()
        make(1)
    tp=256
    def part(b,ref,i):
        def tile(j):
            rows=pl.ds(pl.multiple_of(b*per+j*tp,tp),tp)
            v=dot(dj[rows,0:wq],wq_ref[...],NT)+dot(dj[rows,wq:wq+wk],wk_ref[...],NT)+dot(dj[rows,wq+wk:2*wq],wv_ref[...],NT)
            ref[i,span(j,tp),:]=v.astype(BF)
        each(per//tp,tile)
    part(diag,pbuf,1)
    sc.to_mate(1,pbuf.at[1]).start()
    part(far,farbuf,0)
    sc.pair_far(farbuf.at[0])
    def e0():
        part(mate,pbuf,0)
        sc.to_mate(0,pbuf.at[0]).start()
    def e1():
        part(t,farbuf,1)
        sc.pair_own(farbuf.at[1])
    def e2():
        gain=vec(g_ref)
        gbuf[:,0:dm]=jnp.zeros((1,dm),F32)
        gbuf[:,dm:2*dm]=gm_ref[...]
        gbuf[:,2*dm:2*dm+HD]=jnp.sum(gacc[0].T,0,keepdims=True)
        gbuf[:,2*dm+HD:2*dm+2*HD]=jnp.sum(gacc[1].T,0,keepdims=True)
        def rows(r,e):
            dv,gg=norm_bwd(x_ref[r,:].astype(F32),gain,e)
            dx_ref[r,:]+=dv
            gbuf[:,0:dm]+=gg
        sc.result(rows)
    def step(k):
        second.reduce_step(k)
        when_each(k,((1,e0),(2,e1)))
    lax.fori_loop(1,d,lambda k,_: (step(k),0)[1],0)
    cps=[send(grecv.at[2*i+1],grecv.at[2*i],gs.at[i],gr.at[i],partner(a,b),a) for i,(a,b) in enumerate(steps)]
    def turn(i):
        def f():
            if i==0: e2()
            else:
                cps[i-1].wait_recv()
                gbuf[...]+=grecv[2*i-2]
            if i<len(steps):
                grecv[2*i+1]=gbuf[...]
                cps[i].start()
        return f
    def gstep(k):
        when_each(k,[(i+2,turn(i)) for i in range(min(len(steps)+1,d-2))])
        second.gather_step(k)
    lax.fori_loop(1,d,lambda k,_: (gstep(k),0)[1],0)
    for i in range(d-2,len(steps)+1): turn(i)()
    ga_o[...]=gbuf[:,0:dm]; gm_o[...]=gbuf[:,dm:2*dm]; gq_o[...]=gbuf[:,2*dm:2*dm+HD]; gk_o[...]=gbuf[:,2*dm+HD:2*dm+2*HD]
    each(nr,lambda y: first_ring(y).drain())
    second.drain(); sc.drain(); so.drain()
    for c in cps: c.wait_send()
    for c in saves: c.wait()

def tail(x,g,gq,gk,gm,wq,wk,wv,pos,lse,r,both,q,k,v,do,att,xh,cos,sin,a1,op,hid,dhid,d,nt,bq,bk,scale,cid):
    per,dm=x.shape; n=a1.shape[0]
    nq,nk,nv=q.shape[1],k.shape[1],v.shape[1]
    assert nq==nk+nv
    fused=(dm//d)%128==0
    M=pltpu.VMEM
    ns=sum((s-1).bit_length() for s in (d,nt))
    ratio=nq//nk; rc=dm//d; h=dm//2
    row=lambda c: S_((1,c),F32)
    rr=both.shape[0]//d; nr=4
    ins=(x,g,gq,gk,gm,wq,wk,wv,pos,lse,r,both,q,k,v,do,att,xh,cos,sin,a1,op,hid,dhid)
    return call(functools.partial(tail_kernel,d,nt,nr,fused,bq,bk,scale),ins,
        [S_((per,dm),BF),S_((per,dm),F32),S_((dm,nq),BF),S_((dm,nk),BF),S_((dm,nv),BF),S_(both.shape,BF),row(dm),row(dm),row(HD),row(HD)],
        [M((n,2*nq),BF),M((n,nk),BF),M((n,nv),BF),M((n,nq),BF),M(xh.shape,BF),M(cos.shape,F32),M(sin.shape,F32),M((n,2*nq),BF),M((n,HD),F32),M((n,HD),F32),
         M((HD,ratio*bq),F32),M((ratio*bq,HD),BF),M((ratio*bq,HD),BF),M((HD,n),BF),M((8,2*ratio*bq),F32),M((2,HD,HD),F32),M((2,HD,HD),F32),M((n,128),BF),
         M((2,per,dm),BF),M((2,per,dm),BF),M((2,rc,nq),F32),M((1,2*dm+2*HD),F32),M((2*ns,1,2*dm+2*HD),F32),
         M(both.shape,BF),M((per,dm),BF),M((2,rr,h),BF),M((2,d-1,rr,h),BF),M((2,rc,nq),BF),M((2,d-1,rc,nq),BF),
         D_((16,)),D_((ns,)),D_((ns,))]+[D_((4,nr,2,d-1))]+[D_((2*nq//128,d-1))]*4+Scatter.scratch(per,dm)*2+([] if fused else [M((2,dm,nq),BF)]),
        cid,'tail',[A_]+[V_]*4+[A_]+[V_]*4,[V_]*12+[A_]*12)
def widen_kernel(split,ng,*refs):
    n=(len(refs)-1)//2
    for a,b in zip(refs[:n-ng-1],refs[n:]): b[...]=a[...].astype(b.dtype)
    both=refs[n-ng-1]; down,out=refs[2*n-ng-1:2*n-ng+1]
    for a,b in zip(refs[n-ng:n],refs[-ng:]): b[...]=a[...].reshape(-1)
    down[...]=both[0:split,:].astype(F32); out[...]=both[split:,:].astype(F32)

def widen(arrays,plain,both,gains,rows,steps):
    spec=lambda n,w: pl.BlockSpec((n//steps,w),lambda i:(i,0))
    w=both.shape[1]
    ins=[spec(*a.shape) for a in arrays+plain]
    return pl.pallas_call(functools.partial(widen_kernel,rows//steps,len(gains)),grid=(steps,),in_specs=ins+[spec(*both.shape)]+[V_]*len(gains),out_specs=ins+[spec(rows,w),spec(both.shape[0]-rows,w)]+[V_]*len(gains),
        out_shape=[S_(a.shape,F32) for a in arrays]+[S_(a.shape,a.dtype) for a in plain]+[S_((rows,w),F32),S_((both.shape[0]-rows,w),F32)]+[S_((g.shape[1],),F32) for g in gains],name='widen')(*arrays,*plain,both,*gains)

def local(nd,nt,tokens,w_query,w_key,w_value,w_out,w_gate,w_up,w_down,norm_attn,norm_mlp,norm_query,norm_key,cotangent,segments,positions):
    scale=HD**-0.5
    ne=cotangent.shape[0]//4
    a1,q,k,v,xh,r,cos,sin,early,late=front(tokens,cotangent,positions,jnp.asarray(FREQS[:,None]),norm_attn,norm_query,norm_key,w_query,w_key,w_value,ne,4,1)
    late=lax.ppermute(late,'tensor',[(i,(i+2)%nt) for i in range(nt)])
    att,lse=attn_fwd(q,k,v,positions,512,512,scale)
    att,late=lax.optimization_barrier((att,late))
    hid,a2,act,dg,du,outp,dap,dy=middle(att,w_out,tokens,cotangent,early,late,w_gate,w_up,w_down,norm_mlp,2,2)
    dhid,gm,dwg,dwu,both,dout=post(hid,cotangent,norm_mlp,w_out,a2,dy,act,dg,du,dap,att,nd,3)
    output,d_tokens,dwq,dwk,dwv,both,ga,gm,gq,gk=tail(tokens,norm_attn,norm_query,norm_key,gm,w_query,w_key,w_value,positions,lse,r,both,
        q,k,v,dout,att,xh,cos,sin,a1,outp,hid,dhid,nd,nt,512,256,scale,4)
    dwq,dwk,dwv,dwg,dwu,output,d_tokens,dwd,dwo,ga,gm,gq,gk=widen((dwq,dwk,dwv,dwg,dwu),(output,d_tokens),both,(ga,gm,gq,gk),w_down.shape[0],nd)
    return (output,d_tokens,dwq,dwk,dwv,dwo,dwg,dwu,dwd,ga,gm,gq,gk)

def solution(mesh):
    nd,nt=mesh.shape['dp'],mesh.shape['tensor']
    row=P(('dp','tensor'),None); col=P(None,'tensor'); rw=P('tensor',None)
    return jax.shard_map(functools.partial(local,nd,nt),mesh=mesh,
        in_specs=(row,col,col,col,rw,col,col,rw,P(),P(),P(),P(),row,P('dp',None),P('dp',None)),
        out_specs=(row,row,col,col,col,rw,col,col,rw,P(),P(),P(),P()),check_vma=False)
```

```python
import functools, math
import numpy as np
import jax, jax.numpy as jnp
from jax import lax
from jax.sharding import PartitionSpec as P
from jax.experimental import pallas as pl
from jax.experimental.pallas import tpu as pltpu
HD=128
EPS=1e-6
F32=jnp.float32; BF=jnp.bfloat16
NT=(((1,),(1,)),((),()))
TN=(((0,),(0,)),((),()))
NN=(((1,),(0,)),((),()))
LOG2E=math.log2(math.e)
THETA=1000000.0
LONGEST=1024
FREQS=(THETA**(-np.arange(0,HD,2,dtype=np.float64)/HD)).astype(np.float32)
MESH=pl.DeviceIdType.MESH
D_=pltpu.SemaphoreType.DMA
S_=jax.ShapeDtypeStruct
V_=pl.BlockSpec(memory_space=pltpu.VMEM); A_=pl.BlockSpec(memory_space=pl.ANY)

def dot(a,b,dims=NN): return lax.dot_general(a,b,dims,preferred_element_type=F32)

def vec(ref): return ref[...].astype(F32).reshape(1,-1)

def group():
    t=lax.axis_index('tensor')
    mate=t+1-2*lax.rem(t,2)
    return t,mate,lax.rem(t+2,4),lax.rem(mate+2,4)

def greet(peers):
    barrier=pltpu.get_barrier_semaphore()
    for axis,p in peers:
        pl.semaphore_signal(barrier,inc=1,device_id={axis:p},device_id_type=MESH)
    pl.semaphore_wait(barrier,len(peers))

def send(src,dst,ss,rs,peer,axis='tensor'):
    return pltpu.make_async_remote_copy(src_ref=src,dst_ref=dst,send_sem=ss,recv_sem=rs,device_id={axis:peer},device_id_type=MESH)

def span(i,step,mult=None): return pl.ds(pl.multiple_of(i*step,mult or step),step)

def rows_of(ref,b,j,r,per): return ref.at[pl.ds(pl.multiple_of(b*per+j*r,r),r)]

def each(n,f):
    def body(i,_):
        f(i)
        return 0
    lax.fori_loop(0,n,body,0)

def each_rows(n,f,step=64): each(n//step,lambda i: f(span(i,step)))

def when_each(k,table):
    for at,f in table: pl.when(k==at)(f)

def call(kernel,ins,outs,scratch,cid,name,out_specs,in_specs,limit=67043328):
    return pl.pallas_call(kernel,in_specs=in_specs,out_specs=out_specs,out_shape=outs,scratch_shapes=scratch,
        compiler_params=pltpu.CompilerParams(collective_id=cid,has_side_effects=True,vmem_limit_bytes=limit),name=name)(*ins)

def attn_fwd_kernel(bq,bk,ratio,scale,pos_ref,q_ref,k_ref,v_ref,prow_ref,o_ref,l_ref,vx_ref,acc_ref):
    i=pl.program_id(1)
    n=k_ref.shape[0]
    @pl.when(i==0)
    def _():
        vx_ref[:,:HD]=v_ref[...]
        vx_ref[:,HD:]=jnp.ones((n,HD),BF)
    q=q_ref[...]
    qs=jnp.concatenate([q[:,h*HD:(h+1)*HD] for h in range(ratio)],0)
    rows=lax.rem(lax.broadcasted_iota(jnp.int32,(ratio*bq,1),0),bq)+i*bq
    start=jnp.broadcast_to(prow_ref[...].astype(F32),(HD,bq)).T[:,0:1].astype(jnp.int32)
    start=rows-jnp.concatenate([start]*ratio,0)
    acc_ref[...]=jnp.zeros_like(acc_ref)
    c=scale*LOG2E
    def step(j,_):
        b=pl.multiple_of(j*bk,bk)
        s=dot(qs,k_ref[pl.ds(b,bk),:],NT)
        cols=lax.broadcasted_iota(jnp.int32,(1,bk),1)+b
        m=(rows>=cols)&(start<=cols)
        e=jnp.where(m,jnp.exp2(s*c),0.0).astype(BF)
        acc_ref[...]+=dot(e,vx_ref[pl.ds(b,bk),:])
        return 0
    lax.fori_loop((i*bq-pos_ref[i*bq])//bk,(i*bq+bq-1)//bk+1,step,0)
    a=acc_ref[...]
    l=a[:,HD:]
    o=(a[:,:HD]/l).astype(BF)
    lt=jnp.log2(l).T[0:1]
    for h in range(ratio):
        o_ref[:,h*HD:(h+1)*HD]=o[h*bq:(h+1)*bq]
        l_ref[h]=lt[:,h*bq:(h+1)*bq]

def attn_fwd(q,k,v,pos,bq,bk,scale):
    n,wq=q.shape; g=k.shape[1]//HD; ratio=wq//HD//g
    gs=pltpu.PrefetchScalarGridSpec(num_scalar_prefetch=1,grid=(g,n//bq),
        in_specs=[pl.BlockSpec((bq,ratio*HD),lambda g,i,p:(i,g)),
                  pl.BlockSpec((n,HD),lambda g,i,p:(0,g)),
                  pl.BlockSpec((n,HD),lambda g,i,p:(0,g)),
                  pl.BlockSpec((1,bq),lambda g,i,p:(0,i))],
        out_specs=[pl.BlockSpec((bq,ratio*HD),lambda g,i,p:(i,g)),
                   pl.BlockSpec((ratio,1,bq),lambda g,i,p:(g,0,i))],
        scratch_shapes=[pltpu.VMEM((n,2*HD),BF),pltpu.VMEM((ratio*bq,2*HD),F32)])
    return pl.pallas_call(functools.partial(attn_fwd_kernel,bq,bk,ratio,scale),grid_spec=gs,
        out_shape=[S_((n,wq),BF),S_((g*ratio,1,n),F32)],name='attn_fwd')(pos[0],q,k,v,pos)
def front_kernel(nc,x_ref,cot_ref,pos_ref,fr_ref,g_ref,gq_ref,gk_ref,wq_in,wk_in,wv_in,
                 a_o,q_o,k_o,v_o,xh_o,r_o,cos_o,sin_o,early_o,late_o,
                 xf,a_s,q_s,k_s,v_s,xh_s,r_s,cost,sint,cosn,sinn,wq_ref,wk_ref,wv_ref,lsem,osem,ss,rs,es):
    t,mate,far,diag=group()
    per=x_ref.shape[0]; r=per//nc; n=xf.shape[0]; half=HD//2
    outs=[(a_s,a_o,0),(q_s,q_o,0),(k_s,k_o,0),(v_s,v_o,0),(xh_s,xh_o,1),(r_s,r_o,2)]
    own=pltpu.make_async_copy(x_ref,rows_of(xf,t,0,per,per),lsem)
    own.start()
    weights=[pltpu.make_async_copy(a,b,es.at[3+i]) for i,(a,b) in enumerate(((wq_in,wq_ref),(wk_in,wk_ref),(wv_in,wv_ref)))]
    for c in weights: c.start()
    greet([('tensor',mate),('tensor',far)])
    across=lambda j: send(x_ref.at[span(j,r)],rows_of(xf,t,j,r,per),ss.at[0,j],rs.at[0,j],far)
    beside=lambda j: send(x_ref.at[span(j,r)],rows_of(xf,t,j,r,per),ss.at[1,j],rs.at[1,j],mate)
    onward=lambda j: send(rows_of(xf,far,j,r,per),rows_of(xf,far,j,r,per),ss.at[2,j],rs.at[2,j],mate)
    each(nc,lambda j: across(j).start())
    each(nc,lambda j: beside(j).start())
    early=send(cot_ref.at[0:early_o.shape[0]],early_o,es.at[0],es.at[1],far)
    keep=pltpu.make_async_copy(cot_ref.at[early_o.shape[0]:per],late_o,es.at[2])
    keep.start()
    gain,gq,gk=vec(g_ref),vec(gq_ref),vec(gk_ref)
    tt=256
    def table(i):
        c=span(i,tt)
        ang=fr_ref[...]*pos_ref[:,c].astype(F32)
        co,si=jnp.cos(ang),jnp.sin(ang)
        ct=jnp.concatenate([co,co],0); st=jnp.concatenate([-si,si],0)
        cost[:,c]=ct; sint[:,c]=st
        cosn[c,:]=ct.T; sinn[c,:]=st.T
    each(n//tt,table)
    tabs=[pltpu.make_async_copy(cost,cos_o,osem.at[6,0]),pltpu.make_async_copy(sint,sin_o,osem.at[7,0])]
    for c in tabs: c.start()
    def out_copy(o,i):
        s,d,ax=outs[o]
        c=span(i,r)
        at=(c,(slice(None),c),(slice(None),slice(None),c))[ax]
        return pltpu.make_async_copy(s.at[at],d.at[at],osem.at[o,i])
    def tile(b,j):
        p=pl.multiple_of(b*per+j*r,r)
        rows=pl.ds(p,r)
        x=xf[rows,:].astype(F32)
        a=(x*lax.rsqrt(jnp.mean(x*x,-1,keepdims=True)+EPS)*gain).astype(BF)
        a_s[rows,:]=a
        v_s[rows,:]=dot(a,wv_ref[...]).astype(BF)
        cos=cosn[rows,:]; sin=sinn[rows,:]
        h0=0
        for w_ref,g,dst in ((wq_ref,gq,q_s),(wk_ref,gk,k_s)):
            raw=dot(a,w_ref[...])
            for h in range(raw.shape[1]//HD):
                rh=raw[:,h*HD:(h+1)*HD]
                u=rh*lax.rsqrt(jnp.mean(rh*rh,-1,keepdims=True)+EPS)*g
                dst[rows,h*HD:(h+1)*HD]=(u*cos+pltpu.roll(u,half,1)*sin).astype(BF)
                rt=rh.T
                rr=lax.rsqrt(jnp.mean(rt*rt,0,keepdims=True)+EPS)
                xh_s[(h0+h)*HD:(h0+h+1)*HD,rows]=(rt*rr).astype(BF)
                r_s[h0+h,:,rows]=rr
            h0+=raw.shape[1]//HD
        for o in range(6): out_copy(o,b*nc+j).start()
    for c in [own]+weights: c.wait()
    each(nc,lambda j: tile(t,j))
    each(nc,lambda j: beside(j).wait_recv())
    each(nc,lambda j: tile(mate,j))
    def body(j):
        across(j).wait_recv()
        pl.when(j==nc-1)(lambda: early.start())
        onward(j).start()
        tile(far,j)
        onward(j).wait_recv()
        tile(diag,j)
    each(nc,body)
    def drain(j):
        across(j).wait_send(); beside(j).wait_send(); onward(j).wait_send()
    each(nc,drain)
    def flush(i):
        for o in range(6): out_copy(o,i).wait()
    each(n//r,flush)
    for c in tabs: c.wait()
    early.wait()
    keep.wait()

def front(x,cot,pos,freqs,gain,gq,gk,wq,wk,wv,first,nc,cid):
    n=4*x.shape[0]; d=x.shape[1]
    wide=wq.shape[1]+wk.shape[1]
    shapes=[((n,d),BF),((n,wq.shape[1]),BF),((n,wk.shape[1]),BF),((n,wv.shape[1]),BF),((wide,n),BF),((wide//HD,1,n),F32),((HD,n),F32),((HD,n),F32)]
    return call(functools.partial(front_kernel,nc),(x,cot,pos,freqs,gain,gq,gk,wq,wk,wv),[S_(*s) for s in shapes]+[S_((first,d),BF),S_((x.shape[0]-first,d),BF)],
        [pltpu.VMEM((n,d),BF)]+[pltpu.VMEM(*s) for s in shapes]+[pltpu.VMEM((n,HD),F32)]*2+[pltpu.VMEM(w.shape,BF) for w in (wq,wk,wv)]+[D_,D_((8,4*nc)),D_((3,nc)),D_((3,nc)),D_((6,))],cid,'front',[A_]*10,[A_]*2+[V_]*5+[A_]*3)
def ring_neighbours(d):
    me=lax.axis_index('dp')
    half=d//2
    odd=lax.rem(me,2); up=me//2
    pos=odd*(d-1-2*up)+up
    def at(p):
        hi=p//half
        return hi*(2*(d-1-p)+1)+(1-hi)*2*p
    return pos,at(lax.rem(pos+1,d)),at(lax.rem(pos+d-1,d))

class Ring:
    def __init__(self,d,sems,make=None):
        self.d,self.sems,self.make=d,sems,make
        self.pos,right,left=ring_neighbours(d)
        self.to=(right,left)
        self.units=[]
    def add(self,s,rc,mine,sbuf,recv,out): self.units.append((s,rc,mine,sbuf,recv,out))
    def chunk(self,s,k): return lax.rem(self.pos-k+2*self.d,self.d) if s==0 else lax.rem(self.pos+k,self.d)
    def rs(self,u,k,src):
        return send(src,self.units[u][4].at[k],self.sems[0].at[u,k],self.sems[1].at[u,k],self.to[self.units[u][0]],'dp')
    def ag(self,u,k,c):
        s,rc,_,_,_,out=self.units[u]
        ref=out.at[span(c,rc)]
        return send(ref,ref,self.sems[2].at[u,k],self.sems[3].at[u,k],self.to[s],'dp')
    def start(self):
        for u,(s,rc,mine,sbuf,recv,out) in enumerate(self.units):
            sbuf[...]=mine(0).astype(BF)
            self.rs(u,0,sbuf).start()
    def reduce_step(self,k):
        for u,(s,rc,mine,sbuf,recv,out) in enumerate(self.units):
            self.rs(u,k-1,sbuf).wait_recv()
            val=(mine(k)+recv[k-1].astype(F32)).astype(BF)
            @pl.when(k<self.d-1)
            def _():
                recv[k-1]=val
                self.rs(u,k,recv.at[k-1]).start()
            @pl.when(k==self.d-1)
            def _():
                c=self.chunk(s,k)
                out[span(c,rc),:]=val
                self.ag(u,0,c).start()
        if self.make: pl.when(k<self.d-1)(lambda: self.make(k+1))
    def gather_step(self,k):
        for u,(s,rc,mine,sbuf,recv,out) in enumerate(self.units):
            c=self.chunk(s,k-1)
            self.ag(u,k-1,c).wait_recv()
            @pl.when(k<self.d-1)
            def _(): self.ag(u,k,c).start()
    def any_step(self,m):
        pl.when(m<self.d)(lambda: self.reduce_step(m))
        pl.when(m>=self.d)(lambda: self.gather_step(m-self.d+1))
    def drain(self):
        def body(k):
            for u,(s,rc,mine,sbuf,recv,out) in enumerate(self.units):
                self.rs(u,k,sbuf).wait_send()
                self.ag(u,k,0).wait_send()
        each(self.d-1,body)

class Scatter:
    def __init__(self,ids,per,rbuf,fbuf,ybuf,acc,ss,rs):
        self.t,self.mate,self.far,self.diag=ids
        self.per=per; self.rbuf,self.fbuf,self.ybuf,self.acc,self.ss,self.rs=rbuf,fbuf,ybuf,acc,ss,rs
    @staticmethod
    def scratch(per,w): return [pltpu.VMEM((2,per,w),BF),pltpu.VMEM((per,w),BF),pltpu.VMEM((per,w),BF),pltpu.VMEM((per,w),F32),D_((3,)),D_((3,))]
    def to_mate(self,i,src): return send(src,self.rbuf.at[i],self.ss.at[i],self.rs.at[i],self.mate)
    def across(self): return send(self.fbuf,self.ybuf,self.ss.at[2],self.rs.at[2],self.far)
    def pair(self,far_part,own_part,base=None):
        self.pair_far(far_part)
        self.pair_own(own_part,base)
    def pair_far(self,far_part):
        self.to_mate(1,self.fbuf).wait_recv()
        def far_rows(r): self.fbuf[r,:]=(far_part[r,:].astype(F32)+self.rbuf[1,r,:].astype(F32)).astype(BF)
        each_rows(self.per,far_rows)
        self.across().start()
    def pair_own(self,own_part,base=None):
        self.to_mate(0,self.fbuf).wait_recv()
        def own_rows(r):
            v=own_part[r,:].astype(F32)+self.rbuf[0,r,:].astype(F32)
            self.acc[r,:]=v if base is None else v+base[r,:]
        each_rows(self.per,own_rows)
    def result(self,f):
        self.across().wait_recv()
        each_rows(self.per,lambda r: f(r,self.acc[r,:]+self.ybuf[r,:].astype(F32)))
    def drain(self):
        self.to_mate(0,self.fbuf).wait_send(); self.to_mate(1,self.fbuf).wait_send(); self.across().wait_send()

def norm_bwd(v,gain,e):
    r=lax.rsqrt(jnp.mean(v*v,-1,keepdims=True)+EPS)
    vh=v*r
    ge=e*gain
    return r*(ge-vh*jnp.mean(vh*ge,-1,keepdims=True)),jnp.sum(e*vh,0,keepdims=True)
def mid_kernel(nc,att_ref,wo_ref,x_in,cot_ref,early_ref,late_ref,wg_ref,wu_ref,wd_ref,g_ref,
               hid_o,a_o,act_o,dg_o,du_o,op_o,da_o,dy_o,
               attv,wov,dyv,wgv,wuv,wdv,full,act_s,dg_s,du_s,op_s,da_s,acc,pbuf,rbuf,fbuf,ybuf,x_ref,hid_ref,lsem,osem,ss,rs,dsem):
    t,mate,far,diag=group()
    per=x_ref.shape[0]; r=per//nc; n=full.shape[0]
    ne=early_ref.shape[0]
    loads=[pltpu.make_async_copy(s,d,lsem.at[i]) for i,(s,d) in enumerate(((att_ref,attv),(wo_ref,wov),(cot_ref,rows_of(dyv,t,0,per,per)),(wg_ref,wgv),(wu_ref,wuv),(wd_ref,wdv),(early_ref,dyv.at[pl.ds(pl.multiple_of(far*per,per),ne)]),(late_ref,dyv.at[pl.ds(pl.multiple_of(far*per+ne,ne),per-ne)])))]
    xl=pltpu.make_async_copy(x_in,x_ref,lsem.at[9])
    for c in loads[:2]+[xl]+loads[2:]: c.start()
    greet([('tensor',mate),('tensor',far)])
    dys=[send(cot_ref,rows_of(dyv,t,0,per,per),dsem.at[0],dsem.at[1],mate),send(early_ref,dyv.at[pl.ds(pl.multiple_of(far*per,per),ne)],dsem.at[2],dsem.at[3],mate),send(late_ref,dyv.at[pl.ds(pl.multiple_of(far*per+ne,ne),per-ne)],dsem.at[4],dsem.at[5],mate)]
    outs=[(full,a_o),(act_s,act_o),(dg_s,dg_o),(du_s,du_o),(op_s,op_o),(da_s,da_o)]
    gain=vec(g_ref)
    def proj(b,j):
        return dot(rows_of(attv,b,j,r,per)[...],wov[...])
    def to_mate(i,j):
        return send(pbuf.at[i,pl.ds(pl.multiple_of(j*r,r),r)],rbuf.at[i,pl.ds(pl.multiple_of(j*r,r),r)],ss.at[i,j],rs.at[i,j],mate)
    def to_far(j):
        rr=pl.ds(pl.multiple_of(j*r,r),r)
        return send(fbuf.at[rr],ybuf.at[rr],ss.at[2,j],rs.at[2,j],far)
    def share(j,i,peer):
        return send(rows_of(full,t,j,r,per),rows_of(full,t,j,r,per),ss.at[i,j],rs.at[i,j],peer)
    def forward(j):
        return send(rows_of(full,far,j,r,per),rows_of(full,far,j,r,per),ss.at[5,j],rs.at[5,j],mate)
    loads[0].wait(); loads[1].wait(); xl.wait()
    def reduce(j,_):
        rr=pl.ds(pl.multiple_of(j*r,r),r)
        pbuf[1,rr,:]=proj(diag,j).astype(BF); to_mate(1,j).start()
        pbuf[0,rr,:]=proj(mate,j).astype(BF); to_mate(0,j).start()
        f=proj(far,j)
        to_mate(1,j).wait_recv()
        fbuf[rr,:]=(f+rbuf[1,rr,:].astype(F32)).astype(BF)
        to_far(j).start()
        @pl.when(j==0)
        def _():
            for c in dys: c.start()
        o=proj(t,j)
        to_mate(0,j).wait_recv()
        acc[rr,:]=o+rbuf[0,rr,:].astype(F32)+x_ref[rr,:].astype(F32)
        return 0
    lax.fori_loop(0,nc,reduce,0)
    for i in range(2,8): loads[i].wait()
    for c in dys: c.wait_recv()
    dyc=pltpu.make_async_copy(dyv,dy_o,lsem.at[8])
    dyc.start()
    def mlp_rows(b,j,m=1):
        rows=pl.ds(pl.multiple_of(b*per+j*r,r),m*r)
        a=full[rows,:]
        gate=dot(a,wgv[...]); up=dot(a,wuv[...])
        dact=dot(dyv[rows,:],wdv[...],NT)
        sig=1.0/(1.0+jnp.exp(-gate))
        sl=gate*sig
        act=(sl*up).astype(BF)
        act_s[rows,:]=act
        dg=(dact*up*(sig*(1.0+gate*(1.0-sig)))).astype(BF)
        du=(dact*sl).astype(BF)
        dg_s[rows,:]=dg; du_s[rows,:]=du
        op_s[rows,:]=dot(act,wdv[...]).astype(BF)
        da_s[rows,:]=(dot(dg,wgv[...],NT)+dot(du,wuv[...],NT)).astype(BF)
        for o,(s,d) in enumerate(outs):
            for z in range(m):
                part=pl.ds(pl.multiple_of(b*per+(j+z)*r,r),r)
                pltpu.make_async_copy(s.at[part],d.at[part],osem.at[o,b*nc+j+z]).start()
    def two(f): lax.fori_loop(0,2,lambda i,_: (f(i),0)[1],0)
    def near(jj):
        def chunk(i):
            j=2*jj+i
            rr=span(j,r)
            to_far(j).wait_recv()
            h=acc[rr,:]+ybuf[rr,:].astype(F32)
            hid_ref[rr,:]=h
            rows_of(full,t,j,r,per)[...]=(h*lax.rsqrt(jnp.mean(h*h,-1,keepdims=True)+EPS)*gain).astype(BF)
            share(j,3,far).start(); share(j,4,mate).start()
        two(chunk)
        def rows(i):
            @pl.when(i==1)
            def _():
                for z in range(2): share(2*jj+z,4,mate).wait_recv()
            mlp_rows(t+i*(mate-t),2*jj,2)
        two(rows)
    each(nc//2,near)
    hc=pltpu.make_async_copy(hid_ref,hid_o,lsem.at[10])
    hc.start()
    def arrive(j):
        share(j,3,far).wait_recv()
        forward(j).start()
    def away(j,m):
        for z in range(m): arrive(j+z)
        def rows(i):
            @pl.when(i==1)
            def _():
                for z in range(m): forward(j+z).wait_recv()
            mlp_rows(far+i*(diag-far),j,m)
        two(rows)
    each(nc//2-1,lambda jj: away(2*jj,2))
    each(2,lambda z: away(nc-2+z,1))
    def drain(j,_):
        to_mate(0,j).wait_send(); to_mate(1,j).wait_send(); to_far(j).wait_send()
        share(j,3,far).wait_send(); share(j,4,mate).wait_send(); forward(j).wait_send()
        return 0
    lax.fori_loop(0,nc,drain,0)
    def flush(i,_):
        rows=pl.ds(pl.multiple_of(i*r,r),r)
        for o,(s,d) in enumerate(outs):
            pltpu.make_async_copy(s.at[rows],d.at[rows],osem.at[o,i]).wait()
        return 0
    lax.fori_loop(0,n//r,flush,0)
    dyc.wait()
    hc.wait()
    for c in dys: c.wait_send()

def middle(att,wo,x,cot,early,late,wg,wu,wd,gain,nc,cid):
    n=att.shape[0]; per,d=x.shape; f=wg.shape[1]
    rows=[((n,d),BF),((n,f),BF),((n,f),BF),((n,f),BF),((n,d),BF),((n,d),BF)]
    return call(functools.partial(mid_kernel,nc),(att,wo,x,cot,early,late,wg,wu,wd,gain),[S_((per,d),F32)]+[S_(*s) for s in rows]+[S_((n,d),BF)],
        [pltpu.VMEM(s,BF) for s in (att.shape,wo.shape,(n,d),wg.shape,wu.shape,wd.shape)]+[pltpu.VMEM(*s) for s in rows]+
        [pltpu.VMEM((per,d),F32),pltpu.VMEM((2,per,d),BF),pltpu.VMEM((2,per,d),BF),pltpu.VMEM((per,d),BF),pltpu.VMEM((per,d),BF),pltpu.VMEM((per,d),BF),pltpu.VMEM((per,d),F32),
         D_((11,)),D_((6,4*nc)),D_((6,nc)),D_((6,nc)),D_((6,))],cid,'middle',[A_]*8,[A_,A_,A_,A_,A_,A_,A_,A_,A_,V_])
def post_kernel(d,fused,hid_in,cot_in,g_ref,wo_in,a_ref,dy_ref,act_ref,dg_ref,du_ref,da_ref,att_ref,
                dhid_o,gg_ref,dwg_ref,dwu_ref,both_ref,dout_o,
                av,ac,dyv,actv,dgv,duv,attv,full,doutv,parts,ownbuf,sbuf,recv,dhid_ref,hid_ref,cot_ref,wo_ref,lsem,osem,ss,rs,m0,m1,m2,m3,oacc,*rest):
    ids=t,mate,far,diag=group()
    per,dm=hid_ref.shape; n=full.shape[0]; f=dgv.shape[1]; rc=dm//d
    rs1=Scatter(ids,per,*rest[:6])
    whole=None if fused else rest[6]
    def make(k):
        if fused:
            for s in range(2): ownbuf[s]=dot(av[:,span(ring.chunk(s,k),rc)],(dgv,duv)[s][...],TN)
    ring=Ring(d,(m0,m1,m2,m3),make)
    nu=3
    w=f//nu
    for j in range(nu):
        for s,out in enumerate((dwg_ref,dwu_ref)):
            lo,hi=j*w,(j+1)*w
            def mine(k,s=s,lo=lo,hi=hi):
                if fused: return ownbuf[s,:,lo:hi]
                return whole[s,span(ring.chunk(s,k),rc),lo:hi].astype(F32)
            ring.add(s,rc,mine,sbuf.at[s,:,lo:hi],recv.at[s,:,:,lo:hi],out.at[:,lo:hi])
    c0=pl.multiple_of(ring.chunk(0,0)*rc,128) if fused else 0
    loads=[pltpu.make_async_copy(s,x,lsem.at[i]) for i,(s,x) in enumerate(((dg_ref,dgv),(a_ref.at[:,pl.ds(c0,128)],ac),(du_ref,duv),(a_ref,av),(dy_ref,dyv),(act_ref,actv),(att_ref,attv)))]
    blk=lambda ref,b: rows_of(ref,b,0,per,per)
    parts_=[pltpu.make_async_copy(blk(da_ref,b),parts.at[i],lsem.at[7+i]) for i,b in enumerate((far,t))]
    plain=[pltpu.make_async_copy(a,b,lsem.at[9+i]) for i,(a,b) in enumerate(((hid_in,hid_ref),(cot_in,cot_ref),(wo_in,wo_ref)))]
    for c in loads[:4]+parts_+loads[4:]+plain: c.start()
    greet([('tensor',mate),('tensor',far),('dp',ring.to[0]),('dp',ring.to[1])])
    rs1.to_mate(1,blk(da_ref,diag)).start(); rs1.to_mate(0,blk(da_ref,mate)).start()
    for c in loads[:3]: c.wait()
    if fused:
        for s in range(2): ownbuf[s]=dot(ac[...],(dgv,duv)[s][...],TN)
        ring.start()
        loads[3].wait()
        make(1)
    else:
        loads[3].wait()
        for s in range(2):
            def tile(i,s=s): whole[s,span(i,128),:]=dot(av[:,span(i,128)],(dgv,duv)[s][...],TN).astype(BF)
            each(dm//128,tile)
        ring.start()
    share=lambda i,p: send(blk(full,t),blk(full,t),ss.at[i],rs.at[i],p)
    onward=lambda: send(blk(full,far),blk(full,far),ss.at[2],rs.at[2],mate)
    def e1():
        for c in parts_: c.wait()
        rs1.pair(parts.at[0],parts.at[1])
    def e2():
        for c in plain: c.wait()
        gg_ref[...]=jnp.zeros_like(gg_ref)
        mine=blk(full,t)
        gain=vec(g_ref)
        def rows(r,da):
            dh,gg=norm_bwd(hid_ref[r,:],gain,da)
            dh=dh+cot_ref[r,:].astype(F32)
            dhid_ref[r,:]=dh; gg_ref[...]+=gg
            mine[r,:]=dh.astype(BF)
        rs1.result(rows)
        pltpu.make_async_copy(dhid_ref,dhid_o,osem.at[1]).start()
        share(0,far).start(); share(1,mate).start()
    rd,ro=f//d,wo_ref.shape[0]//d
    def put_rows(first,r,c,v):
        for j in range(d): both_ref[j*(rd+ro)+first:j*(rd+ro)+first+r,c]=v[j*r:(j+1)*r].astype(BF)
    def down(i):
        put_rows(0,rd,span(i,256),dot(actv[...],dyv[:,span(i,256)],TN))
    nd_=dm//256
    tt=256
    def dout_rows(b,last=False):
        def tile(i):
            rows=pl.ds(pl.multiple_of(b*per+i*tt,tt),tt)
            doutv[rows,:]=dot(full[rows,:],wo_ref[...],NT).astype(BF)
        each(per//tt,tile)
        if last: pltpu.make_async_copy(doutv,dout_o,osem.at[0]).start()
    def out_rows(b,last=False):
        rows=span(b,per)
        def out_tile(i):
            c=span(i,256)
            v=dot(attv[rows,:],full[rows,c],TN)
            if last: put_rows(rd,ro,c,oacc[:,c]+v)
            else: oacc[:,c]+=v
        each(dm//256,out_tile)
    def e3():
        loads[6].wait()
        oacc[...]=jnp.zeros_like(oacc)
        dout_rows(t)
    def e4():
        share(1,mate).wait_recv()
        dout_rows(mate)
    def e5():
        share(0,far).wait_recv()
        onward().start()
        dout_rows(far)
    def step(k):
        when_each(k,((1,e1),(d-1,e2)))
        ring.reduce_step(k)
        @pl.when(k==2)
        def _():
            for c in loads[4:6]: c.wait()
        pl.when((k>=2)&(k<2+nd_))(lambda: down(k-2))
    lax.fori_loop(1,d,lambda k,_: (step(k),0)[1],0)
    def gstep(k):
        ring.gather_step(k)
        when_each(k,((1,e3),(2,lambda: out_rows(t)),(3,e4),(4,lambda: out_rows(mate)),(d-3,e5),(d-2,lambda: out_rows(far))))
    lax.fori_loop(1,d,lambda k,_: (gstep(k),0)[1],0)
    onward().wait_recv()
    dout_rows(diag,True)
    out_rows(diag,True)
    ring.drain(); rs1.drain()
    share(0,far).wait_send(); share(1,mate).wait_send(); onward().wait_send()
    pltpu.make_async_copy(doutv,dout_o,osem.at[0]).wait()
    pltpu.make_async_copy(dhid_ref,dhid_o,osem.at[1]).wait()

def post(hid,cot,gain,wo,a2,dy,act,dg,du,dap,att,d,cid):
    per,dm=hid.shape; n=a2.shape[0]; f=act.shape[1]
    fused=(dm//d)%128==0
    M=pltpu.VMEM
    wo_=wo.shape[0]
    return call(functools.partial(post_kernel,d,fused),(hid,cot,gain,wo,a2,dy,act,dg,du,dap,att),
        [S_((per,dm),F32),S_((1,dm),F32),S_((dm,f),BF),S_((dm,f),BF),S_((f+wo_,dm),BF),S_((n,wo_),BF)],
        [M((n,dm),BF),M((n,128),BF),M((n,dm),BF),M((n,f),BF),M((n,f),BF),M((n,f),BF),M((n,wo_),BF),M((n,dm),BF),M((n,wo_),BF),M((2,per,dm),BF),
         M((2,dm//d,f),F32),M((2,dm//d,f),BF),M((2,d-1,dm//d,f),BF),M((per,dm),F32),M((per,dm),F32),M((per,dm),BF),M(wo.shape,BF),D_((12,)),D_((2,)),D_((3,)),D_((3,))]+[D_((6,d-1))]*4+[M((wo_,dm),F32)]+Scatter.scratch(per,dm)+([] if fused else [M((2,dm,f),BF)]),
        cid,'post',[A_]+[V_]*4+[A_],[A_,A_,V_,A_]+[A_]*7)
LATE=4
def rot_norm_bwd(dt,xh,r,gain,cos,sin):
    h=HD//2
    du=dt*cos-jnp.concatenate([dt[h:],dt[:h]],0)*sin
    ge=du*gain
    return r*(ge-xh*jnp.mean(xh*ge,0,keepdims=True)),du*xh

def tail_kernel(d,nt,nr,fused,bq,bk,scale,x_in,g_ref,gq_ref,gk_ref,gm_ref,wq_in,wk_in,wv_in,pos_ref,lse_ref,r_ref,both_ref,
                q_ref,k_ref,v_ref,do_ref,att_ref,xh_ref,cos_ref,sin_ref,a_ref,op_ref,hid_ref,dhid_ref,
                out_o,dx_o,dwq_o,dwk_o,dwv_o,both_o,ga_o,gm_o,gq_o,gk_o,
                x_ref,wq_ref,wk_ref,wv_ref,dx_ref,u1,kv,vv,attv,xhv,cosv,sinv,dj,dka,dva,dqa,qs,os_,kt,dd,gacc,gcol,ac,
                pbuf,farbuf,ownbuf,gbuf,grecv,bothv,outv,b2,r2,b3,r3,lsem,gs,gr,*sems):
    ids=t,mate,far,diag=group()
    per,dm=x_ref.shape; n=u1.shape[0]
    p,(t0,t1,t2,t3),rest=sems[0],sems[1:5],sems[5:]
    wq,wk,wv,wo=attv.shape[1],kv.shape[1],vv.shape[1],attv.shape[1]
    rc=dm//d
    sc=Scatter(ids,per,*rest[:6]); so=Scatter(ids,per,*rest[6:12])
    whole=None if fused else rest[12]
    blk=lambda ref,b: rows_of(ref,b,0,per,per)
    loads=[pltpu.make_async_copy(s,x,lsem.at[i]) for i,(s,x) in enumerate(((q_ref,u1.at[:,0:wq]),(k_ref,kv),(v_ref,vv),(do_ref,u1.at[:,wq:2*wq]),(att_ref,attv),(xh_ref,xhv),(cos_ref,cosv),(sin_ref,sinv)))]
    h=dm//2; w1=h//nr
    rr=both_ref.shape[0]//d
    def first_ring(y):
        ring=Ring(d,[p.at[i,y] for i in range(4)])
        for s in range(2):
            cs=pl.ds(pl.multiple_of(s*h+y*w1,w1),w1); bs=pl.ds(pl.multiple_of(y*w1,w1),w1)
            ring.add(s,rr,lambda k,s=s,cs=cs,ring=ring: both_ref[span(ring.chunk(s,k),rr),cs].astype(F32),b2.at[s,:,bs],r2.at[s,:,:,bs],bothv.at[:,cs])
        return ring
    first=first_ring(0)
    def make(k):
        if fused:
            c=first.chunk(0,k); e=first.chunk(1,k)
            ownbuf[0]=dot(u1[:,span(c,rc)],dj[:,0:wq],TN)
            ownbuf[1]=dot(u1[:,span(e,rc)],dj[:,wq:2*wq],TN)
    second=Ring(d,(t0,t1,t2,t3),make)
    w2=128
    for lo in range(0,wq,w2):
        for s in range(2):
            out=dwq_o.at[:,lo:lo+w2] if s==0 else (dwk_o.at[:,lo:lo+w2] if lo<wk else dwv_o.at[:,lo-wk:lo-wk+w2])
            def mine(k,s=s,lo=lo):
                if fused: return ownbuf[s,:,lo:lo+w2]
                return whole[s,span(second.chunk(s,k),rc),lo:lo+w2].astype(F32)
            second.add(s,rc,mine,b3.at[s,:,lo:lo+w2],r3.at[s,:,:,lo:lo+w2],out)
    c0=pl.multiple_of(first.chunk(0,0)*rc,128) if fused else 0
    later=[pltpu.make_async_copy(a_ref.at[:,pl.ds(c0,128)],ac,lsem.at[8]),pltpu.make_async_copy(dhid_ref,dx_ref,lsem.at[9]),
           pltpu.make_async_copy(blk(op_ref,far),pbuf.at[0],lsem.at[10]),pltpu.make_async_copy(blk(op_ref,t),pbuf.at[1],lsem.at[11]),pltpu.make_async_copy(hid_ref,so.acc,lsem.at[12])]
    weights=[pltpu.make_async_copy(a,b,lsem.at[16+i]) for i,(a,b) in enumerate(((x_in,x_ref),(wq_in,wq_ref),(wk_in,wk_ref),(wv_in,wv_ref)))]
    for c in loads+later+weights: c.start()
    steps=[]
    for axis,m in (('tensor',nt),('dp',d)):
        b=1
        while b<m:
            steps.append((axis,b)); b*=2
    def partner(axis,b):
        me=lax.axis_index(axis)
        return me+b-2*b*lax.rem(me//b,2)
    greet([('tensor',mate),('tensor',far),('dp',first.to[0]),('dp',first.to[1])]+[(a,partner(a,b)) for a,b in steps])
    each(nr,lambda y: first_ring(y).start())
    so.to_mate(1,blk(op_ref,diag)).start(); so.to_mate(0,blk(op_ref,mate)).start()
    def pair_out():
        for c in later[2:]: c.wait()
        so.pair(pbuf.at[0],pbuf.at[1],so.acc)
    def finish_out():
        def rows(r,v): outv[r,:]=v.astype(BF)
        so.result(rows)
    for i,ref in enumerate((gq_ref,gk_ref)): gcol[i]=jnp.broadcast_to(vec(ref),(HD,HD)).T
    gacc[...]=jnp.zeros_like(gacc)
    for c in loads[:5]: c.wait()
    groups=wk//HD; ratio=wq//wk; nb=n//bq; jb=bq//bk
    c2=scale*LOG2E
    total=2*nr*(d-1)
    assert bq==2*bk and LONGEST%bk==0
    back=LONGEST//bk
    first_key=lambda i: jnp.maximum(jb*i-back,0)
    sizes=[jb*(i+1)-max(jb*i-back,0) for i in range(nb)]
    per_group=sum(sizes)
    full=[i for i in range(nb) if jb*i<=back]
    iters=groups*(per_group+nb*ratio)
    hot=iters+LATE
    def before(i):
        u=jnp.minimum(i,len(full))
        return jb*u*(u+1)//2+(i-u)*(jb+back)
    hooks=iters
    def hook(it):
        when_each(it,((2,pair_out),(iters-1,finish_out)))
        for z in range(-(-total//iters)):
            m=it*total//hot+1+z
            pl.when(m<=(it+1)*total//hot)(lambda: first_ring(lax.rem(m-1,nr)).any_step((m-1)//nr+1))
    def lane_tiles(dt,head,gi,cols,put):
        for z in range(dt.shape[1]//HD):
            cs=pl.ds(pl.multiple_of(cols+z*HD,HD),HD)
            dx,gg=rot_norm_bwd(dt[:,z*HD:(z+1)*HD]*scale,xhv[span(head,HD),cs].astype(F32),r_ref[head,:,cs],gcol[gi],cosv[:,cs],sinv[:,cs])
            gacc[gi]+=gg
            put(cs,dx.T.astype(BF))
    def one_group(g):
        gl=pl.multiple_of(g*HD,HD)
        kcols=pl.ds(gl,HD)
        def prep(i):
            kt[:,span(i,bq)]=kv[span(i,bq),kcols].T
            dka[span(i,bq),:]=jnp.zeros((bq,HD),F32); dva[span(i,bq),:]=jnp.zeros((bq,HD),F32)
        each(nb,prep)
        qcol=[pl.ds(pl.multiple_of(g*ratio*HD+x*HD,HD),HD) for x in range(ratio)]
        dcol=[pl.ds(pl.multiple_of(wq+g*ratio*HD+x*HD,HD),HD) for x in range(ratio)]
        def q_block(i):
            rows=span(i,bq)
            hb=bq//2
            wide=ratio*bq
            cq=[lax.broadcasted_iota(jnp.int32,(1,hb),1)+i*bq+y*hb for y in range(2)]
            cols=jnp.concatenate([cq[y] for y in range(2) for x in range(ratio)],1)
            sts=cols-jnp.concatenate([pos_ref[:,pl.ds(pl.multiple_of(i*bq+y*hb,hb),hb)] for y in range(2) for x in range(ratio)],1)
            one=jnp.ones((8,HD),BF)
            for y in range(2):
                for x in range(ratio):
                    at=slice((y*ratio+x)*hb,(y*ratio+x+1)*hb)
                    rh=pl.ds(pl.multiple_of(i*bq+y*hb,hb),hb)
                    qx=u1[rh,qcol[x]]; ox=u1[rh,dcol[x]]
                    qs[at,:]=qx; os_[at,:]=ox
                    pr=ox.astype(F32)*attv[rh,qcol[x]].astype(F32)
                    hi=pr.astype(BF); lo=(pr-hi.astype(F32)).astype(BF)
                    dd[:,at]=dot(one,hi,NT)+dot(one,lo,NT)
                    dd[0:1,wide+at.start:wide+at.stop]=lse_ref[g*ratio+x,:,rh]
            dqa[...]=jnp.zeros_like(dqa)
            def key_block(j,lo,hi,causal):
                b=span(j,bk)
                kb=kv[b,kcols]
                cs=slice(lo,hi)
                s=dot(kb,qs[cs,:],NT)
                keys=lax.broadcasted_iota(jnp.int32,(bk,1),0)+j*bk
                m=sts[:,cs]<=keys
                if causal: m=m&(cols[:,cs]>=keys)
                p=jnp.where(m,jnp.exp2(s*c2-dd[0:1,wide+lo:wide+hi]),0.0)
                ds=(p*(dot(vv[b,kcols],os_[cs,:],NT)-dd[0:1,cs])).astype(BF)
                dva[b,:]+=dot(p.astype(BF),os_[cs,:])
                dka[b,:]+=dot(ds,qs[cs,:])
                dqa[:,cs]+=dot(kt[:,b],ds)
            def finish(x):
                if x==0:
                    @pl.when((g==0)&(i==0))
                    def _():
                        for c in loads[5:]: c.wait()
                def put(cs,v,x=x): dj[cs,qcol[x]]=v
                lane_tiles(jnp.concatenate([dqa[:,(y*ratio+x)*hb:(y*ratio+x+1)*hb] for y in range(2)],1),g*ratio+x,0,i*bq,put)
            j0,j1=first_key(i),(i+1)*jb
            def slot(j,_):
                far_back=(jb*i>=back)&(j==jb*i-back)
                pl.when(far_back)(lambda: key_block(j,0,wide//2,False))
                pl.when((j<jb*i)&jnp.logical_not(far_back))(lambda: key_block(j,0,wide,False))
                pl.when(j==jb*i)(lambda: key_block(j,0,wide,True))
                pl.when(j==jb*i+1)(lambda: key_block(j,wide//2,wide,True))
                for x in range(ratio): pl.when(j==j1+x)(lambda x=x: finish(x))
                hook(g*(per_group+nb*ratio)+before(i)+i*ratio+j-j0)
                return 0
            lax.fori_loop(j0,j1+ratio,slot,0)
        each(nb,q_block)
        def fin(i):
            rows=span(i,bq)
            dj[rows,pl.ds(pl.multiple_of(wq+wk+gl,HD),HD)]=dva[rows,:].astype(BF)
            def put(cs,v): dj[cs,pl.ds(pl.multiple_of(wq+gl,HD),HD)]=v
            lane_tiles(dka[rows,:].T,wq//HD+g,1,i*bq,put)
        each(nb,fin)
    each(groups,one_group)
    lax.fori_loop(iters*total//hot+1,total+1,lambda m,_: (first_ring(lax.rem(m-1,nr)).any_step((m-1)//nr+1),0)[1],0)
    saves=[pltpu.make_async_copy(bothv,both_o,lsem.at[14]),pltpu.make_async_copy(outv,out_o,lsem.at[15])]
    for c in saves: c.start()
    al=pltpu.make_async_copy(a_ref,u1,lsem.at[13])
    al.start()
    for c in later[:2]+weights: c.wait()
    if fused:
        ownbuf[0]=dot(ac[...],dj[:,0:wq],TN); ownbuf[1]=dot(ac[...],dj[:,wq:2*wq],TN)
    else:
        al.wait()
        for s in range(2):
            def tile(i,s=s): whole[s,span(i,128),:]=dot(u1[:,span(i,128)],dj[:,s*wq:(s+1)*wq],TN).astype(BF)
            each(dm//128,tile)
    second.start()
    if fused:
        al.wait()
        make(1)
    tp=256
    def part(b,ref,i):
        def tile(j):
            rows=pl.ds(pl.multiple_of(b*per+j*tp,tp),tp)
            v=dot(dj[rows,0:wq],wq_ref[...],NT)+dot(dj[rows,wq:wq+wk],wk_ref[...],NT)+dot(dj[rows,wq+wk:2*wq],wv_ref[...],NT)
            ref[i,span(j,tp),:]=v.astype(BF)
        each(per//tp,tile)
    part(diag,pbuf,1)
    sc.to_mate(1,pbuf.at[1]).start()
    part(far,farbuf,0)
    sc.pair_far(farbuf.at[0])
    def e0():
        part(mate,pbuf,0)
        sc.to_mate(0,pbuf.at[0]).start()
    def e1():
        part(t,farbuf,1)
        sc.pair_own(farbuf.at[1])
    def e2():
        gain=vec(g_ref)
        gbuf[:,0:dm]=jnp.zeros((1,dm),F32)
        gbuf[:,dm:2*dm]=gm_ref[...]
        gbuf[:,2*dm:2*dm+HD]=jnp.sum(gacc[0].T,0,keepdims=True)
        gbuf[:,2*dm+HD:2*dm+2*HD]=jnp.sum(gacc[1].T,0,keepdims=True)
        def rows(r,e):
            dv,gg=norm_bwd(x_ref[r,:].astype(F32),gain,e)
            dx_ref[r,:]+=dv
            gbuf[:,0:dm]+=gg
        sc.result(rows)
        pltpu.make_async_copy(dx_ref,dx_o,lsem.at[20]).start()
    def step(k):
        second.reduce_step(k)
        when_each(k,((1,e0),(2,e1)))
    lax.fori_loop(1,d,lambda k,_: (step(k),0)[1],0)
    cps=[send(grecv.at[2*i+1],grecv.at[2*i],gs.at[i],gr.at[i],partner(a,b),a) for i,(a,b) in enumerate(steps)]
    def turn(i):
        def f():
            if i==0: e2()
            else:
                cps[i-1].wait_recv()
                gbuf[...]+=grecv[2*i-2]
            if i<len(steps):
                grecv[2*i+1]=gbuf[...]
                cps[i].start()
        return f
    def gstep(k):
        when_each(k,[(i+2,turn(i)) for i in range(min(len(steps)+1,d-2))])
        second.gather_step(k)
    lax.fori_loop(1,d,lambda k,_: (gstep(k),0)[1],0)
    for i in range(d-2,len(steps)+1): turn(i)()
    ga_o[...]=gbuf[:,0:dm]; gm_o[...]=gbuf[:,dm:2*dm]; gq_o[...]=gbuf[:,2*dm:2*dm+HD]; gk_o[...]=gbuf[:,2*dm+HD:2*dm+2*HD]
    each(nr,lambda y: first_ring(y).drain())
    second.drain(); sc.drain(); so.drain()
    for c in cps: c.wait_send()
    for c in saves+[pltpu.make_async_copy(dx_ref,dx_o,lsem.at[20])]: c.wait()

def tail(x,g,gq,gk,gm,wq,wk,wv,pos,lse,r,both,q,k,v,do,att,xh,cos,sin,a1,op,hid,dhid,d,nt,bq,bk,scale,cid):
    per,dm=x.shape; n=a1.shape[0]
    nq,nk,nv=q.shape[1],k.shape[1],v.shape[1]
    assert nq==nk+nv
    fused=(dm//d)%128==0
    M=pltpu.VMEM
    ns=sum((s-1).bit_length() for s in (d,nt))
    ratio=nq//nk; rc=dm//d; h=dm//2
    row=lambda c: S_((1,c),F32)
    rr=both.shape[0]//d; nr=4
    ins=(x,g,gq,gk,gm,wq,wk,wv,pos,lse,r,both,q,k,v,do,att,xh,cos,sin,a1,op,hid,dhid)
    return call(functools.partial(tail_kernel,d,nt,nr,fused,bq,bk,scale),ins,
        [S_((per,dm),BF),S_((per,dm),F32),S_((dm,nq),BF),S_((dm,nk),BF),S_((dm,nv),BF),S_(both.shape,BF),row(dm),row(dm),row(HD),row(HD)],
        [M(x.shape,BF),M(wq.shape,BF),M(wk.shape,BF),M(wv.shape,BF),M((per,dm),F32),M((n,2*nq),BF),M((n,nk),BF),M((n,nv),BF),M((n,nq),BF),M(xh.shape,BF),M(cos.shape,F32),M(sin.shape,F32),M((n,2*nq),BF),M((n,HD),F32),M((n,HD),F32),
         M((HD,ratio*bq),F32),M((ratio*bq,HD),BF),M((ratio*bq,HD),BF),M((HD,n),BF),M((8,2*ratio*bq),F32),M((2,HD,HD),F32),M((2,HD,HD),F32),M((n,128),BF),
         M((2,per,dm),BF),M((2,per,dm),BF),M((2,rc,nq),F32),M((1,2*dm+2*HD),F32),M((2*ns,1,2*dm+2*HD),F32),
         M(both.shape,BF),M((per,dm),BF),M((2,rr,h),BF),M((2,d-1,rr,h),BF),M((2,rc,nq),BF),M((2,d-1,rc,nq),BF),
         D_((21,)),D_((ns,)),D_((ns,))]+[D_((4,nr,2,d-1))]+[D_((2*nq//128,d-1))]*4+Scatter.scratch(per,dm)*2+([] if fused else [M((2,dm,nq),BF)]),
        cid,'tail',[A_,A_]+[V_]*3+[A_]+[V_]*4,[A_]+[V_]*4+[A_]*3+[V_]*4+[A_]*12)
def widen_kernel(split,ng,*refs):
    n=(len(refs)-1)//2
    for a,b in zip(refs[:n-ng-1],refs[n:]): b[...]=a[...].astype(b.dtype)
    both=refs[n-ng-1]; down,out=refs[2*n-ng-1:2*n-ng+1]
    for a,b in zip(refs[n-ng:n],refs[-ng:]): b[...]=a[...].reshape(-1)
    rd,ro=split
    for c in range(both.shape[0]//(rd+ro)):
        p=c*(rd+ro)
        down[c*rd:(c+1)*rd,:]=both[p:p+rd,:].astype(F32); out[c*ro:(c+1)*ro,:]=both[p+rd:p+rd+ro,:].astype(F32)

def widen(arrays,plain,both,gains,rows,chunks,steps=4):
    spec=lambda n,w: pl.BlockSpec((n//steps,w),lambda i:(i,0))
    w=both.shape[1]
    ins=[spec(*a.shape) for a in arrays+plain]
    return pl.pallas_call(functools.partial(widen_kernel,(rows//chunks,(both.shape[0]-rows)//chunks),len(gains)),grid=(steps,),in_specs=ins+[spec(*both.shape)]+[V_]*len(gains),out_specs=ins+[spec(rows,w),spec(both.shape[0]-rows,w)]+[V_]*len(gains),
        out_shape=[S_(a.shape,F32) for a in arrays]+[S_(a.shape,a.dtype) for a in plain]+[S_((rows,w),F32),S_((both.shape[0]-rows,w),F32)]+[S_((g.shape[1],),F32) for g in gains],name='widen')(*arrays,*plain,both,*gains)

def local(nd,nt,tokens,w_query,w_key,w_value,w_out,w_gate,w_up,w_down,norm_attn,norm_mlp,norm_query,norm_key,cotangent,segments,positions):
    scale=HD**-0.5
    ne=cotangent.shape[0]//4
    a1,q,k,v,xh,r,cos,sin,early,late=front(tokens,cotangent,positions,jnp.asarray(FREQS[:,None]),norm_attn,norm_query,norm_key,w_query,w_key,w_value,ne,4,1)
    late=lax.ppermute(late,'tensor',[(i,(i+2)%nt) for i in range(nt)])
    att,lse=attn_fwd(q,k,v,positions,512,512,scale)
    att,late=lax.optimization_barrier((att,late))
    hid,a2,act,dg,du,outp,dap,dy=middle(att,w_out,tokens,cotangent,early,late,w_gate,w_up,w_down,norm_mlp,4,2)
    dhid,gm,dwg,dwu,both,dout=post(hid,cotangent,norm_mlp,w_out,a2,dy,act,dg,du,dap,att,nd,3)
    output,d_tokens,dwq,dwk,dwv,both,ga,gm,gq,gk=tail(tokens,norm_attn,norm_query,norm_key,gm,w_query,w_key,w_value,positions,lse,r,both,
        q,k,v,dout,att,xh,cos,sin,a1,outp,hid,dhid,nd,nt,512,256,scale,4)
    dwq,dwk,dwv,dwg,dwu,output,d_tokens,dwd,dwo,ga,gm,gq,gk=widen((dwq,dwk,dwv,dwg,dwu),(output,d_tokens),both,(ga,gm,gq,gk),w_down.shape[0],nd)
    return (output,d_tokens,dwq,dwk,dwv,dwo,dwg,dwu,dwd,ga,gm,gq,gk)

def solution(mesh):
    nd,nt=mesh.shape['dp'],mesh.shape['tensor']
    row=P(('dp','tensor'),None); col=P(None,'tensor'); rw=P('tensor',None)
    return jax.shard_map(functools.partial(local,nd,nt),mesh=mesh,
        in_specs=(row,col,col,col,rw,col,col,rw,P(),P(),P(),P(),row,P('dp',None),P('dp',None)),
        out_specs=(row,row,col,col,col,rw,col,col,rw,P(),P(),P(),P()),check_vma=False)
```

```python
import functools, math
import numpy as np
import jax, jax.numpy as jnp
from jax import lax
from jax.sharding import PartitionSpec as P
from jax.experimental import pallas as pl
from jax.experimental.pallas import tpu as pltpu
HD=128
EPS=1e-6
F32=jnp.float32; BF=jnp.bfloat16
NT=(((1,),(1,)),((),()))
TN=(((0,),(0,)),((),()))
NN=(((1,),(0,)),((),()))
LOG2E=math.log2(math.e)
THETA=1000000.0
LONGEST=1024
FREQS=(THETA**(-np.arange(0,HD,2,dtype=np.float64)/HD)).astype(np.float32)
MESH=pl.DeviceIdType.MESH
D_=pltpu.SemaphoreType.DMA
S_=jax.ShapeDtypeStruct
V_=pl.BlockSpec(memory_space=pltpu.VMEM); A_=pl.BlockSpec(memory_space=pl.ANY)

def dot(a,b,dims=NN): return lax.dot_general(a,b,dims,preferred_element_type=F32)

def vec(ref): return ref[...].astype(F32).reshape(1,-1)

def group():
    t=lax.axis_index('tensor')
    mate=t+1-2*lax.rem(t,2)
    return t,mate,lax.rem(t+2,4),lax.rem(mate+2,4)

def greet(peers):
    barrier=pltpu.get_barrier_semaphore()
    for axis,p in peers:
        pl.semaphore_signal(barrier,inc=1,device_id={axis:p},device_id_type=MESH)
    pl.semaphore_wait(barrier,len(peers))

def send(src,dst,ss,rs,peer,axis='tensor'):
    return pltpu.make_async_remote_copy(src_ref=src,dst_ref=dst,send_sem=ss,recv_sem=rs,device_id={axis:peer},device_id_type=MESH)

def span(i,step,mult=None): return pl.ds(pl.multiple_of(i*step,mult or step),step)

def rows_of(ref,b,j,r,per): return ref.at[pl.ds(pl.multiple_of(b*per+j*r,r),r)]

def each(n,f):
    def body(i,_):
        f(i)
        return 0
    lax.fori_loop(0,n,body,0)

def each_rows(n,f,step=64): each(n//step,lambda i: f(span(i,step)))

def when_each(k,table):
    for at,f in table: pl.when(k==at)(f)

def call(kernel,ins,outs,scratch,cid,name,out_specs,in_specs,limit=67043328):
    return pl.pallas_call(kernel,in_specs=in_specs,out_specs=out_specs,out_shape=outs,scratch_shapes=scratch,
        compiler_params=pltpu.CompilerParams(collective_id=cid,has_side_effects=True,vmem_limit_bytes=limit),name=name)(*ins)

def attn_fwd_kernel(bq,bk,ratio,scale,pos_ref,q_ref,k_ref,v_ref,prow_ref,o_ref,l_ref,vx_ref,acc_ref):
    i=pl.program_id(1)
    n=k_ref.shape[0]
    @pl.when(i==0)
    def _():
        vx_ref[:,:HD]=v_ref[...]
        vx_ref[:,HD:]=jnp.ones((n,HD),BF)
    q=q_ref[...]
    qs=jnp.concatenate([q[:,h*HD:(h+1)*HD] for h in range(ratio)],0)
    rows=lax.rem(lax.broadcasted_iota(jnp.int32,(ratio*bq,1),0),bq)+i*bq
    start=jnp.broadcast_to(prow_ref[...].astype(F32),(HD,bq)).T[:,0:1].astype(jnp.int32)
    start=rows-jnp.concatenate([start]*ratio,0)
    acc_ref[...]=jnp.zeros_like(acc_ref)
    c=scale*LOG2E
    def step(j,_):
        b=pl.multiple_of(j*bk,bk)
        s=dot(qs,k_ref[pl.ds(b,bk),:],NT)
        cols=lax.broadcasted_iota(jnp.int32,(1,bk),1)+b
        m=(rows>=cols)&(start<=cols)
        e=jnp.where(m,jnp.exp2(s*c),0.0).astype(BF)
        acc_ref[...]+=dot(e,vx_ref[pl.ds(b,bk),:])
        return 0
    lax.fori_loop((i*bq-pos_ref[i*bq])//bk,(i*bq+bq-1)//bk+1,step,0)
    a=acc_ref[...]
    l=a[:,HD:]
    o=(a[:,:HD]/l).astype(BF)
    lt=jnp.log2(l).T[0:1]
    for h in range(ratio):
        o_ref[:,h*HD:(h+1)*HD]=o[h*bq:(h+1)*bq]
        l_ref[h]=lt[:,h*bq:(h+1)*bq]

def attn_fwd(q,k,v,pos,bq,bk,scale):
    n,wq=q.shape; g=k.shape[1]//HD; ratio=wq//HD//g
    gs=pltpu.PrefetchScalarGridSpec(num_scalar_prefetch=1,grid=(g,n//bq),
        in_specs=[pl.BlockSpec((bq,ratio*HD),lambda g,i,p:(i,g)),
                  pl.BlockSpec((n,HD),lambda g,i,p:(0,g)),
                  pl.BlockSpec((n,HD),lambda g,i,p:(0,g)),
                  pl.BlockSpec((1,bq),lambda g,i,p:(0,i))],
        out_specs=[pl.BlockSpec((bq,ratio*HD),lambda g,i,p:(i,g)),
                   pl.BlockSpec((ratio,1,bq),lambda g,i,p:(g,0,i))],
        scratch_shapes=[pltpu.VMEM((n,2*HD),BF),pltpu.VMEM((ratio*bq,2*HD),F32)])
    return pl.pallas_call(functools.partial(attn_fwd_kernel,bq,bk,ratio,scale),grid_spec=gs,
        out_shape=[S_((n,wq),BF),S_((g*ratio,1,n),F32)],name='attn_fwd')(pos[0],q,k,v,pos)
def front_kernel(nc,x_ref,cot_ref,pos_ref,fr_ref,g_ref,gq_ref,gk_ref,wq_in,wk_in,wv_in,
                 a_o,q_o,k_o,v_o,xh_o,r_o,cos_o,sin_o,early_o,late_o,
                 xf,a_s,q_s,k_s,v_s,xh_s,r_s,cost,sint,cosn,sinn,wq_ref,wk_ref,wv_ref,lsem,osem,ss,rs,es):
    t,mate,far,diag=group()
    per=x_ref.shape[0]; r=per//nc; n=xf.shape[0]; half=HD//2
    outs=[(a_s,a_o,0),(q_s,q_o,0),(k_s,k_o,0),(v_s,v_o,0),(xh_s,xh_o,1),(r_s,r_o,2)]
    own=pltpu.make_async_copy(x_ref,rows_of(xf,t,0,per,per),lsem)
    own.start()
    weights=[pltpu.make_async_copy(a,b,es.at[3+i]) for i,(a,b) in enumerate(((wq_in,wq_ref),(wk_in,wk_ref),(wv_in,wv_ref)))]
    for c in weights: c.start()
    greet([('tensor',mate),('tensor',far)])
    across=lambda j: send(x_ref.at[span(j,r)],rows_of(xf,t,j,r,per),ss.at[0,j],rs.at[0,j],far)
    beside=lambda j: send(x_ref.at[span(j,r)],rows_of(xf,t,j,r,per),ss.at[1,j],rs.at[1,j],mate)
    onward=lambda j: send(rows_of(xf,far,j,r,per),rows_of(xf,far,j,r,per),ss.at[2,j],rs.at[2,j],mate)
    each(nc,lambda j: across(j).start())
    each(nc,lambda j: beside(j).start())
    early=send(cot_ref.at[0:early_o.shape[0]],early_o,es.at[0],es.at[1],far)
    keep=pltpu.make_async_copy(cot_ref.at[early_o.shape[0]:per],late_o,es.at[2])
    keep.start()
    gain,gq,gk=vec(g_ref),vec(gq_ref),vec(gk_ref)
    tt=256
    def table(i):
        c=span(i,tt)
        ang=fr_ref[...]*pos_ref[:,c].astype(F32)
        co,si=jnp.cos(ang),jnp.sin(ang)
        ct=jnp.concatenate([co,co],0); st=jnp.concatenate([-si,si],0)
        cost[:,c]=ct; sint[:,c]=st
        cosn[c,:]=ct.T; sinn[c,:]=st.T
    each(n//tt,table)
    tabs=[pltpu.make_async_copy(cost,cos_o,osem.at[6,0]),pltpu.make_async_copy(sint,sin_o,osem.at[7,0])]
    for c in tabs: c.start()
    def out_copy(o,i):
        s,d,ax=outs[o]
        c=span(i,r)
        at=(c,(slice(None),c),(slice(None),slice(None),c))[ax]
        return pltpu.make_async_copy(s.at[at],d.at[at],osem.at[o,i])
    def tile(b,j):
        p=pl.multiple_of(b*per+j*r,r)
        rows=pl.ds(p,r)
        x=xf[rows,:].astype(F32)
        a=(x*lax.rsqrt(jnp.mean(x*x,-1,keepdims=True)+EPS)*gain).astype(BF)
        a_s[rows,:]=a
        v_s[rows,:]=dot(a,wv_ref[...]).astype(BF)
        cos=cosn[rows,:]; sin=sinn[rows,:]
        h0=0
        for w_ref,g,dst in ((wq_ref,gq,q_s),(wk_ref,gk,k_s)):
            raw=dot(a,w_ref[...])
            for h in range(raw.shape[1]//HD):
                rh=raw[:,h*HD:(h+1)*HD]
                u=rh*lax.rsqrt(jnp.mean(rh*rh,-1,keepdims=True)+EPS)*g
                dst[rows,h*HD:(h+1)*HD]=(u*cos+pltpu.roll(u,half,1)*sin).astype(BF)
                rt=rh.T
                rr=lax.rsqrt(jnp.mean(rt*rt,0,keepdims=True)+EPS)
                xh_s[(h0+h)*HD:(h0+h+1)*HD,rows]=(rt*rr).astype(BF)
                r_s[h0+h,:,rows]=rr
            h0+=raw.shape[1]//HD
        for o in range(6): out_copy(o,b*nc+j).start()
    for c in [own]+weights: c.wait()
    each(nc,lambda j: tile(t,j))
    each(nc,lambda j: beside(j).wait_recv())
    each(nc,lambda j: tile(mate,j))
    def body(j):
        across(j).wait_recv()
        pl.when(j==nc-1)(lambda: early.start())
        onward(j).start()
        tile(far,j)
        onward(j).wait_recv()
        tile(diag,j)
    each(nc,body)
    def drain(j):
        across(j).wait_send(); beside(j).wait_send(); onward(j).wait_send()
    each(nc,drain)
    def flush(i):
        for o in range(6): out_copy(o,i).wait()
    each(n//r,flush)
    for c in tabs: c.wait()
    early.wait()
    keep.wait()

def front(x,cot,pos,freqs,gain,gq,gk,wq,wk,wv,first,nc,cid):
    n=4*x.shape[0]; d=x.shape[1]
    wide=wq.shape[1]+wk.shape[1]
    shapes=[((n,d),BF),((n,wq.shape[1]),BF),((n,wk.shape[1]),BF),((n,wv.shape[1]),BF),((wide,n),BF),((wide//HD,1,n),F32),((HD,n),F32),((HD,n),F32)]
    return call(functools.partial(front_kernel,nc),(x,cot,pos,freqs,gain,gq,gk,wq,wk,wv),[S_(*s) for s in shapes]+[S_((first,d),BF),S_((x.shape[0]-first,d),BF)],
        [pltpu.VMEM((n,d),BF)]+[pltpu.VMEM(*s) for s in shapes]+[pltpu.VMEM((n,HD),F32)]*2+[pltpu.VMEM(w.shape,BF) for w in (wq,wk,wv)]+[D_,D_((8,4*nc)),D_((3,nc)),D_((3,nc)),D_((6,))],cid,'front',[A_]*10,[A_]*2+[V_]*5+[A_]*3)
def ring_neighbours(d):
    me=lax.axis_index('dp')
    half=d//2
    odd=lax.rem(me,2); up=me//2
    pos=odd*(d-1-2*up)+up
    def at(p):
        hi=p//half
        return hi*(2*(d-1-p)+1)+(1-hi)*2*p
    return pos,at(lax.rem(pos+1,d)),at(lax.rem(pos+d-1,d))

class Ring:
    def __init__(self,d,sems,make=None):
        self.d,self.sems,self.make=d,sems,make
        self.pos,right,left=ring_neighbours(d)
        self.to=(right,left)
        self.units=[]
    def add(self,s,rc,mine,sbuf,recv,out): self.units.append((s,rc,mine,sbuf,recv,out))
    def chunk(self,s,k): return lax.rem(self.pos-k+2*self.d,self.d) if s==0 else lax.rem(self.pos+k,self.d)
    def rs(self,u,k,src):
        return send(src,self.units[u][4].at[k],self.sems[0].at[u,k],self.sems[1].at[u,k],self.to[self.units[u][0]],'dp')
    def ag(self,u,k,c):
        s,rc,_,_,_,out=self.units[u]
        ref=out.at[span(c,rc)]
        return send(ref,ref,self.sems[2].at[u,k],self.sems[3].at[u,k],self.to[s],'dp')
    def start(self):
        for u,(s,rc,mine,sbuf,recv,out) in enumerate(self.units):
            sbuf[...]=mine(0).astype(BF)
            self.rs(u,0,sbuf).start()
    def reduce_step(self,k):
        for u,(s,rc,mine,sbuf,recv,out) in enumerate(self.units):
            self.rs(u,k-1,sbuf).wait_recv()
            val=(mine(k)+recv[k-1].astype(F32)).astype(BF)
            @pl.when(k<self.d-1)
            def _():
                recv[k-1]=val
                self.rs(u,k,recv.at[k-1]).start()
            @pl.when(k==self.d-1)
            def _():
                c=self.chunk(s,k)
                out[span(c,rc),:]=val
                self.ag(u,0,c).start()
        if self.make: pl.when(k<self.d-1)(lambda: self.make(k+1))
    def gather_step(self,k):
        for u,(s,rc,mine,sbuf,recv,out) in enumerate(self.units):
            c=self.chunk(s,k-1)
            self.ag(u,k-1,c).wait_recv()
            @pl.when(k<self.d-1)
            def _(): self.ag(u,k,c).start()
    def any_step(self,m):
        pl.when(m<self.d)(lambda: self.reduce_step(m))
        pl.when(m>=self.d)(lambda: self.gather_step(m-self.d+1))
    def drain(self):
        def body(k):
            for u,(s,rc,mine,sbuf,recv,out) in enumerate(self.units):
                self.rs(u,k,sbuf).wait_send()
                self.ag(u,k,0).wait_send()
        each(self.d-1,body)

class Scatter:
    def __init__(self,ids,per,rbuf,fbuf,ybuf,acc,ss,rs):
        self.t,self.mate,self.far,self.diag=ids
        self.per=per; self.rbuf,self.fbuf,self.ybuf,self.acc,self.ss,self.rs=rbuf,fbuf,ybuf,acc,ss,rs
    @staticmethod
    def scratch(per,w): return [pltpu.VMEM((2,per,w),BF),pltpu.VMEM((per,w),BF),pltpu.VMEM((per,w),BF),pltpu.VMEM((per,w),F32),D_((3,)),D_((3,))]
    def to_mate(self,i,src): return send(src,self.rbuf.at[i],self.ss.at[i],self.rs.at[i],self.mate)
    def across(self): return send(self.fbuf,self.ybuf,self.ss.at[2],self.rs.at[2],self.far)
    def pair(self,far_part,own_part,base=None):
        self.pair_far(far_part)
        self.pair_own(own_part,base)
    def pair_far(self,far_part):
        self.to_mate(1,self.fbuf).wait_recv()
        def far_rows(r): self.fbuf[r,:]=(far_part[r,:].astype(F32)+self.rbuf[1,r,:].astype(F32)).astype(BF)
        each_rows(self.per,far_rows)
        self.across().start()
    def pair_own(self,own_part,base=None):
        self.to_mate(0,self.fbuf).wait_recv()
        def own_rows(r):
            v=own_part[r,:].astype(F32)+self.rbuf[0,r,:].astype(F32)
            self.acc[r,:]=v if base is None else v+base[r,:]
        each_rows(self.per,own_rows)
    def result(self,f):
        self.across().wait_recv()
        each_rows(self.per,lambda r: f(r,self.acc[r,:]+self.ybuf[r,:].astype(F32)))
    def drain(self):
        self.to_mate(0,self.fbuf).wait_send(); self.to_mate(1,self.fbuf).wait_send(); self.across().wait_send()

def norm_bwd(v,gain,e):
    r=lax.rsqrt(jnp.mean(v*v,-1,keepdims=True)+EPS)
    vh=v*r
    ge=e*gain
    return r*(ge-vh*jnp.mean(vh*ge,-1,keepdims=True)),jnp.sum(e*vh,0,keepdims=True)
def mid_kernel(nc,att_ref,wo_ref,x_in,cot_ref,early_ref,late_ref,wg_ref,wu_ref,wd_ref,g_ref,
               hid_o,a_o,act_o,dg_o,du_o,op_o,da_o,dy_o,
               attv,wov,dyv,wgv,wuv,wdv,full,act_s,dg_s,du_s,op_s,da_s,acc,pbuf,rbuf,fbuf,ybuf,x_ref,hid_ref,lsem,osem,ss,rs,dsem):
    t,mate,far,diag=group()
    per=x_ref.shape[0]; r=per//nc; n=full.shape[0]
    ne=early_ref.shape[0]
    loads=[pltpu.make_async_copy(s,d,lsem.at[i]) for i,(s,d) in enumerate(((att_ref,attv),(wo_ref,wov),(cot_ref,rows_of(dyv,t,0,per,per)),(wg_ref,wgv),(wu_ref,wuv),(wd_ref,wdv),(early_ref,dyv.at[pl.ds(pl.multiple_of(far*per,per),ne)]),(late_ref,dyv.at[pl.ds(pl.multiple_of(far*per+ne,ne),per-ne)])))]
    xl=pltpu.make_async_copy(x_in,x_ref,lsem.at[9])
    for c in loads[:2]+[xl]+loads[2:]: c.start()
    greet([('tensor',mate),('tensor',far)])
    dys=[send(cot_ref,rows_of(dyv,t,0,per,per),dsem.at[0],dsem.at[1],mate),send(early_ref,dyv.at[pl.ds(pl.multiple_of(far*per,per),ne)],dsem.at[2],dsem.at[3],mate),send(late_ref,dyv.at[pl.ds(pl.multiple_of(far*per+ne,ne),per-ne)],dsem.at[4],dsem.at[5],mate)]
    outs=[(full,a_o),(act_s,act_o),(dg_s,dg_o),(du_s,du_o),(op_s,op_o),(da_s,da_o)]
    gain=vec(g_ref)
    def proj(b,j):
        return dot(rows_of(attv,b,j,r,per)[...],wov[...])
    def to_mate(i,j):
        return send(pbuf.at[i,pl.ds(pl.multiple_of(j*r,r),r)],rbuf.at[i,pl.ds(pl.multiple_of(j*r,r),r)],ss.at[i,j],rs.at[i,j],mate)
    def to_far(j):
        rr=pl.ds(pl.multiple_of(j*r,r),r)
        return send(fbuf.at[rr],ybuf.at[rr],ss.at[2,j],rs.at[2,j],far)
    def share(j,i,peer):
        return send(rows_of(full,t,j,r,per),rows_of(full,t,j,r,per),ss.at[i,j],rs.at[i,j],peer)
    def forward(j):
        return send(rows_of(full,far,j,r,per),rows_of(full,far,j,r,per),ss.at[5,j],rs.at[5,j],mate)
    loads[0].wait(); loads[1].wait(); xl.wait()
    def reduce(j,_):
        rr=pl.ds(pl.multiple_of(j*r,r),r)
        pbuf[1,rr,:]=proj(diag,j).astype(BF); to_mate(1,j).start()
        pbuf[0,rr,:]=proj(mate,j).astype(BF); to_mate(0,j).start()
        f=proj(far,j)
        to_mate(1,j).wait_recv()
        fbuf[rr,:]=(f+rbuf[1,rr,:].astype(F32)).astype(BF)
        to_far(j).start()
        @pl.when(j==0)
        def _():
            for c in dys: c.start()
        o=proj(t,j)
        to_mate(0,j).wait_recv()
        acc[rr,:]=o+rbuf[0,rr,:].astype(F32)+x_ref[rr,:].astype(F32)
        return 0
    lax.fori_loop(0,nc,reduce,0)
    for i in range(2,8): loads[i].wait()
    for c in dys: c.wait_recv()
    dyc=pltpu.make_async_copy(dyv,dy_o,lsem.at[8])
    dyc.start()
    def mlp_rows(b,j,m=1):
        rows=pl.ds(pl.multiple_of(b*per+j*r,r),m*r)
        a=full[rows,:]
        gate=dot(a,wgv[...]); up=dot(a,wuv[...])
        dact=dot(dyv[rows,:],wdv[...],NT)
        sig=1.0/(1.0+jnp.exp(-gate))
        sl=gate*sig
        act=(sl*up).astype(BF)
        act_s[rows,:]=act
        dg=(dact*up*(sig*(1.0+gate*(1.0-sig)))).astype(BF)
        du=(dact*sl).astype(BF)
        dg_s[rows,:]=dg; du_s[rows,:]=du
        op_s[rows,:]=dot(act,wdv[...]).astype(BF)
        da_s[rows,:]=(dot(dg,wgv[...],NT)+dot(du,wuv[...],NT)).astype(BF)
        for o,(s,d) in enumerate(outs):
            for z in range(m):
                part=pl.ds(pl.multiple_of(b*per+(j+z)*r,r),r)
                pltpu.make_async_copy(s.at[part],d.at[part],osem.at[o,b*nc+j+z]).start()
    def two(f): lax.fori_loop(0,2,lambda i,_: (f(i),0)[1],0)
    def near(jj):
        def chunk(i):
            j=2*jj+i
            rr=span(j,r)
            to_far(j).wait_recv()
            h=acc[rr,:]+ybuf[rr,:].astype(F32)
            hid_ref[rr,:]=h
            rows_of(full,t,j,r,per)[...]=(h*lax.rsqrt(jnp.mean(h*h,-1,keepdims=True)+EPS)*gain).astype(BF)
            share(j,3,far).start(); share(j,4,mate).start()
        two(chunk)
        def rows(i):
            @pl.when(i==1)
            def _():
                for z in range(2): share(2*jj+z,4,mate).wait_recv()
            mlp_rows(t+i*(mate-t),2*jj,2)
        two(rows)
    each(nc//2,near)
    hc=pltpu.make_async_copy(hid_ref,hid_o,lsem.at[10])
    hc.start()
    def arrive(j):
        share(j,3,far).wait_recv()
        forward(j).start()
    def away(j,m):
        for z in range(m): arrive(j+z)
        def rows(i):
            @pl.when(i==1)
            def _():
                for z in range(m): forward(j+z).wait_recv()
            mlp_rows(far+i*(diag-far),j,m)
        two(rows)
    each(nc//2-1,lambda jj: away(2*jj,2))
    each(2,lambda z: away(nc-2+z,1))
    def drain(j,_):
        to_mate(0,j).wait_send(); to_mate(1,j).wait_send(); to_far(j).wait_send()
        share(j,3,far).wait_send(); share(j,4,mate).wait_send(); forward(j).wait_send()
        return 0
    lax.fori_loop(0,nc,drain,0)
    def flush(i,_):
        rows=pl.ds(pl.multiple_of(i*r,r),r)
        for o,(s,d) in enumerate(outs):
            pltpu.make_async_copy(s.at[rows],d.at[rows],osem.at[o,i]).wait()
        return 0
    lax.fori_loop(0,n//r,flush,0)
    dyc.wait()
    hc.wait()
    for c in dys: c.wait_send()

def middle(att,wo,x,cot,early,late,wg,wu,wd,gain,nc,cid):
    n=att.shape[0]; per,d=x.shape; f=wg.shape[1]
    rows=[((n,d),BF),((n,f),BF),((n,f),BF),((n,f),BF),((n,d),BF),((n,d),BF)]
    return call(functools.partial(mid_kernel,nc),(att,wo,x,cot,early,late,wg,wu,wd,gain),[S_((per,d),F32)]+[S_(*s) for s in rows]+[S_((n,d),BF)],
        [pltpu.VMEM(s,BF) for s in (att.shape,wo.shape,(n,d),wg.shape,wu.shape,wd.shape)]+[pltpu.VMEM(*s) for s in rows]+
        [pltpu.VMEM((per,d),F32),pltpu.VMEM((2,per,d),BF),pltpu.VMEM((2,per,d),BF),pltpu.VMEM((per,d),BF),pltpu.VMEM((per,d),BF),pltpu.VMEM((per,d),BF),pltpu.VMEM((per,d),F32),
         D_((11,)),D_((6,4*nc)),D_((6,nc)),D_((6,nc)),D_((6,))],cid,'middle',[A_]*8,[A_,A_,A_,A_,A_,A_,A_,A_,A_,V_])
def post_kernel(d,fused,hid_in,cot_in,g_ref,wo_in,a_ref,dy_ref,act_ref,dg_ref,du_ref,da_ref,att_ref,
                dhid_o,gg_ref,dwg_o,dwu_o,both_ref,dout_o,
                av,ac,dyv,actv,dgv,duv,attv,full,doutv,parts,ownbuf,sbuf,recv,dhid_ref,hid_ref,cot_ref,wo_ref,dwg_ref,dwu_ref,wsem,lsem,osem,ss,rs,m0,m1,m2,m3,oacc,*rest):
    ids=t,mate,far,diag=group()
    per,dm=hid_ref.shape; n=full.shape[0]; f=dgv.shape[1]; rc=dm//d
    rs1=Scatter(ids,per,*rest[:6])
    whole=None if fused else rest[6]
    def make(k):
        if fused:
            for s in range(2): ownbuf[s]=dot(av[:,span(ring.chunk(s,k),rc)],(dgv,duv)[s][...],TN)
    ring=Ring(d,(m0,m1,m2,m3),make)
    nu=3
    w=f//nu
    for j in range(nu):
        for s,out in enumerate((dwg_ref,dwu_ref)):
            lo,hi=j*w,(j+1)*w
            def mine(k,s=s,lo=lo,hi=hi):
                if fused: return ownbuf[s,:,lo:hi]
                return whole[s,span(ring.chunk(s,k),rc),lo:hi].astype(F32)
            ring.add(s,rc,mine,sbuf.at[s,:,lo:hi],recv.at[s,:,:,lo:hi],out.at[:,lo:hi])
    c0=pl.multiple_of(ring.chunk(0,0)*rc,128) if fused else 0
    loads=[pltpu.make_async_copy(s,x,lsem.at[i]) for i,(s,x) in enumerate(((dg_ref,dgv),(a_ref.at[:,pl.ds(c0,128)],ac),(du_ref,duv),(a_ref,av),(dy_ref,dyv),(act_ref,actv),(att_ref,attv)))]
    blk=lambda ref,b: rows_of(ref,b,0,per,per)
    parts_=[pltpu.make_async_copy(blk(da_ref,b),parts.at[i],lsem.at[7+i]) for i,b in enumerate((far,t))]
    plain=[pltpu.make_async_copy(a,b,lsem.at[9+i]) for i,(a,b) in enumerate(((hid_in,hid_ref),(cot_in,cot_ref),(wo_in,wo_ref)))]
    for c in loads[:4]+parts_+loads[4:]+plain: c.start()
    greet([('tensor',mate),('tensor',far),('dp',ring.to[0]),('dp',ring.to[1])])
    rs1.to_mate(1,blk(da_ref,diag)).start(); rs1.to_mate(0,blk(da_ref,mate)).start()
    for c in loads[:3]: c.wait()
    if fused:
        for s in range(2): ownbuf[s]=dot(ac[...],(dgv,duv)[s][...],TN)
        ring.start()
        loads[3].wait()
        make(1)
    else:
        loads[3].wait()
        for s in range(2):
            def tile(i,s=s): whole[s,span(i,128),:]=dot(av[:,span(i,128)],(dgv,duv)[s][...],TN).astype(BF)
            each(dm//128,tile)
        ring.start()
    share=lambda i,p: send(blk(full,t),blk(full,t),ss.at[i],rs.at[i],p)
    onward=lambda: send(blk(full,far),blk(full,far),ss.at[2],rs.at[2],mate)
    def e1():
        for c in parts_: c.wait()
        rs1.pair(parts.at[0],parts.at[1])
    def e2():
        for c in plain: c.wait()
        gg_ref[...]=jnp.zeros_like(gg_ref)
        mine=blk(full,t)
        gain=vec(g_ref)
        def rows(r,da):
            dh,gg=norm_bwd(hid_ref[r,:],gain,da)
            dh=dh+cot_ref[r,:].astype(F32)
            dhid_ref[r,:]=dh; gg_ref[...]+=gg
            mine[r,:]=dh.astype(BF)
        rs1.result(rows)
        pltpu.make_async_copy(dhid_ref,dhid_o,osem.at[1]).start()
        share(0,far).start(); share(1,mate).start()
    rd,ro=f//d,wo_ref.shape[0]//d
    def put_rows(first,r,c,v):
        for j in range(d): both_ref[j*(rd+ro)+first:j*(rd+ro)+first+r,c]=v[j*r:(j+1)*r].astype(BF)
    def down(i):
        put_rows(0,rd,span(i,256),dot(actv[...],dyv[:,span(i,256)],TN))
    nd_=dm//256
    tt=256
    def dout_rows(b,last=False):
        def tile(i):
            rows=pl.ds(pl.multiple_of(b*per+i*tt,tt),tt)
            doutv[rows,:]=dot(full[rows,:],wo_ref[...],NT).astype(BF)
        each(per//tt,tile)
        if last: pltpu.make_async_copy(doutv,dout_o,osem.at[0]).start()
    def out_rows(b,last=False):
        rows=span(b,per)
        def out_tile(i):
            c=span(i,256)
            v=dot(attv[rows,:],full[rows,c],TN)
            if last: put_rows(rd,ro,c,oacc[:,c]+v)
            else: oacc[:,c]+=v
        each(dm//256,out_tile)
    def e3():
        loads[6].wait()
        oacc[...]=jnp.zeros_like(oacc)
        dout_rows(t)
    def e4():
        share(1,mate).wait_recv()
        dout_rows(mate)
    def e5():
        share(0,far).wait_recv()
        onward().start()
        dout_rows(far)
    def step(k):
        when_each(k,((1,e1),(d-1,e2)))
        ring.reduce_step(k)
        @pl.when(k==2)
        def _():
            for c in loads[4:6]: c.wait()
        pl.when((k>=2)&(k<2+nd_))(lambda: down(k-2))
    lax.fori_loop(1,d,lambda k,_: (step(k),0)[1],0)
    def save(s,c):
        rows=span(c,rc)
        return pltpu.make_async_copy((dwg_ref,dwu_ref)[s].at[rows],(dwg_o,dwu_o)[s].at[rows],wsem.at[s,c])
    for s in range(2): save(s,ring.chunk(s,d-1)).start()
    def gstep(k):
        ring.gather_step(k)
        for s in range(2): save(s,ring.chunk(s,k-1)).start()
        when_each(k,((1,e3),(2,lambda: out_rows(t)),(3,e4),(4,lambda: out_rows(mate)),(d-3,e5),(d-2,lambda: out_rows(far))))
    lax.fori_loop(1,d,lambda k,_: (gstep(k),0)[1],0)
    onward().wait_recv()
    dout_rows(diag,True)
    out_rows(diag,True)
    ring.drain(); rs1.drain()
    def saved(c):
        for s in range(2): save(s,c).wait()
    each(d,saved)
    share(0,far).wait_send(); share(1,mate).wait_send(); onward().wait_send()
    pltpu.make_async_copy(doutv,dout_o,osem.at[0]).wait()
    pltpu.make_async_copy(dhid_ref,dhid_o,osem.at[1]).wait()

def post(hid,cot,gain,wo,a2,dy,act,dg,du,dap,att,d,cid):
    per,dm=hid.shape; n=a2.shape[0]; f=act.shape[1]
    fused=(dm//d)%128==0
    M=pltpu.VMEM
    wo_=wo.shape[0]
    return call(functools.partial(post_kernel,d,fused),(hid,cot,gain,wo,a2,dy,act,dg,du,dap,att),
        [S_((per,dm),F32),S_((1,dm),F32),S_((dm,f),BF),S_((dm,f),BF),S_((f+wo_,dm),BF),S_((n,wo_),BF)],
        [M((n,dm),BF),M((n,128),BF),M((n,dm),BF),M((n,f),BF),M((n,f),BF),M((n,f),BF),M((n,wo_),BF),M((n,dm),BF),M((n,wo_),BF),M((2,per,dm),BF),
         M((2,dm//d,f),F32),M((2,dm//d,f),BF),M((2,d-1,dm//d,f),BF),M((per,dm),F32),M((per,dm),F32),M((per,dm),BF),M(wo.shape,BF),M((dm,f),BF),M((dm,f),BF),D_((2,d)),D_((12,)),D_((2,)),D_((3,)),D_((3,))]+[D_((6,d-1))]*4+[M((wo_,dm),F32)]+Scatter.scratch(per,dm)+([] if fused else [M((2,dm,f),BF)]),
        cid,'post',[A_,V_,A_,A_,V_,A_],[A_,A_,V_,A_]+[A_]*7)
LATE=4
def rot_norm_bwd(dt,xh,r,gain,cos,sin):
    h=HD//2
    du=dt*cos-jnp.concatenate([dt[h:],dt[:h]],0)*sin
    ge=du*gain
    return r*(ge-xh*jnp.mean(xh*ge,0,keepdims=True)),du*xh

def tail_kernel(d,nt,nr,fused,bq,bk,scale,x_in,g_ref,gq_ref,gk_ref,gm_ref,wq_in,wk_in,wv_in,pos_ref,lse_ref,r_ref,both_in,
                q_ref,k_ref,v_ref,do_ref,att_ref,xh_ref,cos_ref,sin_ref,a_ref,op_ref,hid_ref,dhid_ref,
                out_o,dx_o,dwq_o,dwk_o,dwv_o,both_o,ga_o,gm_o,gq_o,gk_o,
                both_ref,x_ref,wq_ref,wk_ref,wv_ref,dx_ref,u1,kv,vv,attv,xhv,cosv,sinv,dj,dka,dva,dqa,qs,os_,kt,dd,gacc,gcol,ac,
                pbuf,farbuf,ownbuf,gbuf,grecv,bothv,outv,b2,r2,b3,r3,lsem,gs,gr,*sems):
    ids=t,mate,far,diag=group()
    per,dm=x_ref.shape; n=u1.shape[0]
    p,(t0,t1,t2,t3),rest=sems[0],sems[1:5],sems[5:]
    wq,wk,wv,wo=attv.shape[1],kv.shape[1],vv.shape[1],attv.shape[1]
    rc=dm//d
    sc=Scatter(ids,per,*rest[:6]); so=Scatter(ids,per,*rest[6:12])
    whole=None if fused else rest[12]
    blk=lambda ref,b: rows_of(ref,b,0,per,per)
    loads=[pltpu.make_async_copy(s,x,lsem.at[i]) for i,(s,x) in enumerate(((q_ref,u1.at[:,0:wq]),(k_ref,kv),(v_ref,vv),(do_ref,u1.at[:,wq:2*wq]),(att_ref,attv),(xh_ref,xhv),(cos_ref,cosv),(sin_ref,sinv)))]
    h=dm//2; w1=h//nr
    rr=both_ref.shape[0]//d
    def first_ring(y):
        ring=Ring(d,[p.at[i,y] for i in range(4)])
        for s in range(2):
            cs=pl.ds(pl.multiple_of(s*h+y*w1,w1),w1); bs=pl.ds(pl.multiple_of(y*w1,w1),w1)
            ring.add(s,rr,lambda k,s=s,cs=cs,ring=ring: both_ref[span(ring.chunk(s,k),rr),cs].astype(F32),b2.at[s,:,bs],r2.at[s,:,:,bs],bothv.at[:,cs])
        return ring
    first=first_ring(0)
    def make(k):
        if fused:
            c=first.chunk(0,k); e=first.chunk(1,k)
            ownbuf[0]=dot(u1[:,span(c,rc)],dj[:,0:wq],TN)
            ownbuf[1]=dot(u1[:,span(e,rc)],dj[:,wq:2*wq],TN)
    second=Ring(d,(t0,t1,t2,t3),make)
    w2=128
    for lo in range(0,wq,w2):
        for s in range(2):
            out=dwq_o.at[:,lo:lo+w2] if s==0 else (dwk_o.at[:,lo:lo+w2] if lo<wk else dwv_o.at[:,lo-wk:lo-wk+w2])
            def mine(k,s=s,lo=lo):
                if fused: return ownbuf[s,:,lo:lo+w2]
                return whole[s,span(second.chunk(s,k),rc),lo:lo+w2].astype(F32)
            second.add(s,rc,mine,b3.at[s,:,lo:lo+w2],r3.at[s,:,:,lo:lo+w2],out)
    c0=pl.multiple_of(first.chunk(0,0)*rc,128) if fused else 0
    later=[pltpu.make_async_copy(a_ref.at[:,pl.ds(c0,128)],ac,lsem.at[8]),pltpu.make_async_copy(dhid_ref,dx_ref,lsem.at[9]),
           pltpu.make_async_copy(blk(op_ref,far),pbuf.at[0],lsem.at[10]),pltpu.make_async_copy(blk(op_ref,t),pbuf.at[1],lsem.at[11]),pltpu.make_async_copy(hid_ref,so.acc,lsem.at[12])]
    weights=[pltpu.make_async_copy(a,b,lsem.at[16+i]) for i,(a,b) in enumerate(((x_in,x_ref),(wq_in,wq_ref),(wk_in,wk_ref),(wv_in,wv_ref)))]
    mine=pltpu.make_async_copy(both_in,both_ref,lsem.at[21])
    for c in [mine]+loads+later+weights: c.start()
    steps=[]
    for axis,m in (('tensor',nt),('dp',d)):
        b=1
        while b<m:
            steps.append((axis,b)); b*=2
    def partner(axis,b):
        me=lax.axis_index(axis)
        return me+b-2*b*lax.rem(me//b,2)
    greet([('tensor',mate),('tensor',far),('dp',first.to[0]),('dp',first.to[1])]+[(a,partner(a,b)) for a,b in steps])
    mine.wait()
    each(nr,lambda y: first_ring(y).start())
    so.to_mate(1,blk(op_ref,diag)).start(); so.to_mate(0,blk(op_ref,mate)).start()
    def pair_out():
        for c in later[2:]: c.wait()
        so.pair(pbuf.at[0],pbuf.at[1],so.acc)
    def finish_out():
        def rows(r,v): outv[r,:]=v.astype(BF)
        so.result(rows)
    for i,ref in enumerate((gq_ref,gk_ref)): gcol[i]=jnp.broadcast_to(vec(ref),(HD,HD)).T
    gacc[...]=jnp.zeros_like(gacc)
    for c in loads[:5]: c.wait()
    groups=wk//HD; ratio=wq//wk; nb=n//bq; jb=bq//bk
    c2=scale*LOG2E
    total=2*nr*(d-1)
    assert bq==2*bk and LONGEST%bk==0
    back=LONGEST//bk
    first_key=lambda i: jnp.maximum(jb*i-back,0)
    sizes=[jb*(i+1)-max(jb*i-back,0) for i in range(nb)]
    per_group=sum(sizes)
    full=[i for i in range(nb) if jb*i<=back]
    iters=groups*(per_group+nb*ratio)
    hot=iters+LATE
    def before(i):
        u=jnp.minimum(i,len(full))
        return jb*u*(u+1)//2+(i-u)*(jb+back)
    hooks=iters
    def hook(it):
        when_each(it,((2,pair_out),(iters-1,finish_out)))
        for z in range(-(-total//iters)):
            m=it*total//hot+1+z
            pl.when(m<=(it+1)*total//hot)(lambda: first_ring(lax.rem(m-1,nr)).any_step((m-1)//nr+1))
    def lane_tiles(dt,head,gi,cols,put):
        for z in range(dt.shape[1]//HD):
            cs=pl.ds(pl.multiple_of(cols+z*HD,HD),HD)
            dx,gg=rot_norm_bwd(dt[:,z*HD:(z+1)*HD]*scale,xhv[span(head,HD),cs].astype(F32),r_ref[head,:,cs],gcol[gi],cosv[:,cs],sinv[:,cs])
            gacc[gi]+=gg
            put(cs,dx.T.astype(BF))
    def one_group(g):
        gl=pl.multiple_of(g*HD,HD)
        kcols=pl.ds(gl,HD)
        def prep(i):
            kt[:,span(i,bq)]=kv[span(i,bq),kcols].T
            dka[span(i,bq),:]=jnp.zeros((bq,HD),F32); dva[span(i,bq),:]=jnp.zeros((bq,HD),F32)
        each(nb,prep)
        qcol=[pl.ds(pl.multiple_of(g*ratio*HD+x*HD,HD),HD) for x in range(ratio)]
        dcol=[pl.ds(pl.multiple_of(wq+g*ratio*HD+x*HD,HD),HD) for x in range(ratio)]
        def q_block(i):
            rows=span(i,bq)
            hb=bq//2
            wide=ratio*bq
            cq=[lax.broadcasted_iota(jnp.int32,(1,hb),1)+i*bq+y*hb for y in range(2)]
            cols=jnp.concatenate([cq[y] for y in range(2) for x in range(ratio)],1)
            sts=cols-jnp.concatenate([pos_ref[:,pl.ds(pl.multiple_of(i*bq+y*hb,hb),hb)] for y in range(2) for x in range(ratio)],1)
            one=jnp.ones((8,HD),BF)
            for y in range(2):
                for x in range(ratio):
                    at=slice((y*ratio+x)*hb,(y*ratio+x+1)*hb)
                    rh=pl.ds(pl.multiple_of(i*bq+y*hb,hb),hb)
                    qx=u1[rh,qcol[x]]; ox=u1[rh,dcol[x]]
                    qs[at,:]=qx; os_[at,:]=ox
                    pr=ox.astype(F32)*attv[rh,qcol[x]].astype(F32)
                    hi=pr.astype(BF); lo=(pr-hi.astype(F32)).astype(BF)
                    dd[:,at]=dot(one,hi,NT)+dot(one,lo,NT)
                    dd[0:1,wide+at.start:wide+at.stop]=lse_ref[g*ratio+x,:,rh]
            dqa[...]=jnp.zeros_like(dqa)
            def key_block(j,lo,hi,causal):
                b=span(j,bk)
                kb=kv[b,kcols]
                cs=slice(lo,hi)
                s=dot(kb,qs[cs,:],NT)
                keys=lax.broadcasted_iota(jnp.int32,(bk,1),0)+j*bk
                m=sts[:,cs]<=keys
                if causal: m=m&(cols[:,cs]>=keys)
                p=jnp.where(m,jnp.exp2(s*c2-dd[0:1,wide+lo:wide+hi]),0.0)
                ds=(p*(dot(vv[b,kcols],os_[cs,:],NT)-dd[0:1,cs])).astype(BF)
                dva[b,:]+=dot(p.astype(BF),os_[cs,:])
                dka[b,:]+=dot(ds,qs[cs,:])
                dqa[:,cs]+=dot(kt[:,b],ds)
            def finish(x):
                if x==0:
                    @pl.when((g==0)&(i==0))
                    def _():
                        for c in loads[5:]: c.wait()
                def put(cs,v,x=x): dj[cs,qcol[x]]=v
                lane_tiles(jnp.concatenate([dqa[:,(y*ratio+x)*hb:(y*ratio+x+1)*hb] for y in range(2)],1),g*ratio+x,0,i*bq,put)
            j0,j1=first_key(i),(i+1)*jb
            def slot(j,_):
                far_back=(jb*i>=back)&(j==jb*i-back)
                pl.when(far_back)(lambda: key_block(j,0,wide//2,False))
                pl.when((j<jb*i)&jnp.logical_not(far_back))(lambda: key_block(j,0,wide,False))
                pl.when(j==jb*i)(lambda: key_block(j,0,wide,True))
                pl.when(j==jb*i+1)(lambda: key_block(j,wide//2,wide,True))
                for x in range(ratio): pl.when(j==j1+x)(lambda x=x: finish(x))
                hook(g*(per_group+nb*ratio)+before(i)+i*ratio+j-j0)
                return 0
            lax.fori_loop(j0,j1+ratio,slot,0)
        each(nb,q_block)
        def fin(i):
            rows=span(i,bq)
            dj[rows,pl.ds(pl.multiple_of(wq+wk+gl,HD),HD)]=dva[rows,:].astype(BF)
            def put(cs,v): dj[cs,pl.ds(pl.multiple_of(wq+gl,HD),HD)]=v
            lane_tiles(dka[rows,:].T,wq//HD+g,1,i*bq,put)
        each(nb,fin)
    each(groups,one_group)
    lax.fori_loop(iters*total//hot+1,total+1,lambda m,_: (first_ring(lax.rem(m-1,nr)).any_step((m-1)//nr+1),0)[1],0)
    saves=[pltpu.make_async_copy(bothv,both_o,lsem.at[14]),pltpu.make_async_copy(outv,out_o,lsem.at[15])]
    for c in saves: c.start()
    al=pltpu.make_async_copy(a_ref,u1,lsem.at[13])
    al.start()
    for c in later[:2]+weights: c.wait()
    if fused:
        ownbuf[0]=dot(ac[...],dj[:,0:wq],TN); ownbuf[1]=dot(ac[...],dj[:,wq:2*wq],TN)
    else:
        al.wait()
        for s in range(2):
            def tile(i,s=s): whole[s,span(i,128),:]=dot(u1[:,span(i,128)],dj[:,s*wq:(s+1)*wq],TN).astype(BF)
            each(dm//128,tile)
    second.start()
    if fused:
        al.wait()
        make(1)
    tp=256
    def part(b,ref,i):
        def tile(j):
            rows=pl.ds(pl.multiple_of(b*per+j*tp,tp),tp)
            v=dot(dj[rows,0:wq],wq_ref[...],NT)+dot(dj[rows,wq:wq+wk],wk_ref[...],NT)+dot(dj[rows,wq+wk:2*wq],wv_ref[...],NT)
            ref[i,span(j,tp),:]=v.astype(BF)
        each(per//tp,tile)
    part(diag,pbuf,1)
    sc.to_mate(1,pbuf.at[1]).start()
    part(far,farbuf,0)
    sc.pair_far(farbuf.at[0])
    def e0():
        part(mate,pbuf,0)
        sc.to_mate(0,pbuf.at[0]).start()
    def e1():
        part(t,farbuf,1)
        sc.pair_own(farbuf.at[1])
    def e2():
        gain=vec(g_ref)
        gbuf[:,0:dm]=jnp.zeros((1,dm),F32)
        gbuf[:,dm:2*dm]=gm_ref[...]
        gbuf[:,2*dm:2*dm+HD]=jnp.sum(gacc[0].T,0,keepdims=True)
        gbuf[:,2*dm+HD:2*dm+2*HD]=jnp.sum(gacc[1].T,0,keepdims=True)
        def rows(r,e):
            dv,gg=norm_bwd(x_ref[r,:].astype(F32),gain,e)
            dx_ref[r,:]+=dv
            gbuf[:,0:dm]+=gg
        sc.result(rows)
        pltpu.make_async_copy(dx_ref,dx_o,lsem.at[20]).start()
    def step(k):
        second.reduce_step(k)
        when_each(k,((1,e0),(2,e1)))
    lax.fori_loop(1,d,lambda k,_: (step(k),0)[1],0)
    cps=[send(grecv.at[2*i+1],grecv.at[2*i],gs.at[i],gr.at[i],partner(a,b),a) for i,(a,b) in enumerate(steps)]
    def turn(i):
        def f():
            if i==0: e2()
            else:
                cps[i-1].wait_recv()
                gbuf[...]+=grecv[2*i-2]
            if i<len(steps):
                grecv[2*i+1]=gbuf[...]
                cps[i].start()
        return f
    def gstep(k):
        when_each(k,[(i+2,turn(i)) for i in range(min(len(steps)+1,d-2))])
        second.gather_step(k)
    lax.fori_loop(1,d,lambda k,_: (gstep(k),0)[1],0)
    for i in range(d-2,len(steps)+1): turn(i)()
    ga_o[...]=gbuf[:,0:dm]; gm_o[...]=gbuf[:,dm:2*dm]; gq_o[...]=gbuf[:,2*dm:2*dm+HD]; gk_o[...]=gbuf[:,2*dm+HD:2*dm+2*HD]
    each(nr,lambda y: first_ring(y).drain())
    second.drain(); sc.drain(); so.drain()
    for c in cps: c.wait_send()
    for c in saves+[pltpu.make_async_copy(dx_ref,dx_o,lsem.at[20])]: c.wait()

def tail(x,g,gq,gk,gm,wq,wk,wv,pos,lse,r,both,q,k,v,do,att,xh,cos,sin,a1,op,hid,dhid,d,nt,bq,bk,scale,cid):
    per,dm=x.shape; n=a1.shape[0]
    nq,nk,nv=q.shape[1],k.shape[1],v.shape[1]
    assert nq==nk+nv
    fused=(dm//d)%128==0
    M=pltpu.VMEM
    ns=sum((s-1).bit_length() for s in (d,nt))
    ratio=nq//nk; rc=dm//d; h=dm//2
    row=lambda c: S_((1,c),F32)
    rr=both.shape[0]//d; nr=4
    ins=(x,g,gq,gk,gm,wq,wk,wv,pos,lse,r,both,q,k,v,do,att,xh,cos,sin,a1,op,hid,dhid)
    return call(functools.partial(tail_kernel,d,nt,nr,fused,bq,bk,scale),ins,
        [S_((per,dm),BF),S_((per,dm),F32),S_((dm,nq),BF),S_((dm,nk),BF),S_((dm,nv),BF),S_(both.shape,BF),row(dm),row(dm),row(HD),row(HD)],
        [M(both.shape,BF),M(x.shape,BF),M(wq.shape,BF),M(wk.shape,BF),M(wv.shape,BF),M((per,dm),F32),M((n,2*nq),BF),M((n,nk),BF),M((n,nv),BF),M((n,nq),BF),M(xh.shape,BF),M(cos.shape,F32),M(sin.shape,F32),M((n,2*nq),BF),M((n,HD),F32),M((n,HD),F32),
         M((HD,ratio*bq),F32),M((ratio*bq,HD),BF),M((ratio*bq,HD),BF),M((HD,n),BF),M((8,2*ratio*bq),F32),M((2,HD,HD),F32),M((2,HD,HD),F32),M((n,128),BF),
         M((2,per,dm),BF),M((2,per,dm),BF),M((2,rc,nq),F32),M((1,2*dm+2*HD),F32),M((2*ns,1,2*dm+2*HD),F32),
         M(both.shape,BF),M((per,dm),BF),M((2,rr,h),BF),M((2,d-1,rr,h),BF),M((2,rc,nq),BF),M((2,d-1,rc,nq),BF),
         D_((22,)),D_((ns,)),D_((ns,))]+[D_((4,nr,2,d-1))]+[D_((2*nq//128,d-1))]*4+Scatter.scratch(per,dm)*2+([] if fused else [M((2,dm,nq),BF)]),
        cid,'tail',[A_,A_]+[V_]*3+[A_]+[V_]*4,[A_]+[V_]*4+[A_]*3+[V_]*3+[A_]*13)
def widen_kernel(split,ng,*refs):
    n=(len(refs)-1)//2
    for a,b in zip(refs[:n-ng-1],refs[n:]): b[...]=a[...].astype(b.dtype)
    both=refs[n-ng-1]; down,out=refs[2*n-ng-1:2*n-ng+1]
    for a,b in zip(refs[n-ng:n],refs[-ng:]): b[...]=a[...].reshape(-1)
    rd,ro=split
    for c in range(both.shape[0]//(rd+ro)):
        p=c*(rd+ro)
        down[c*rd:(c+1)*rd,:]=both[p:p+rd,:].astype(F32); out[c*ro:(c+1)*ro,:]=both[p+rd:p+rd+ro,:].astype(F32)

def widen(arrays,plain,both,gains,rows,chunks,steps=4):
    spec=lambda n,w: pl.BlockSpec((n//steps,w),lambda i:(i,0))
    w=both.shape[1]
    ins=[spec(*a.shape) for a in arrays+plain]
    return pl.pallas_call(functools.partial(widen_kernel,(rows//chunks,(both.shape[0]-rows)//chunks),len(gains)),grid=(steps,),in_specs=ins+[spec(*both.shape)]+[V_]*len(gains),out_specs=ins+[spec(rows,w),spec(both.shape[0]-rows,w)]+[V_]*len(gains),
        out_shape=[S_(a.shape,F32) for a in arrays]+[S_(a.shape,a.dtype) for a in plain]+[S_((rows,w),F32),S_((both.shape[0]-rows,w),F32)]+[S_((g.shape[1],),F32) for g in gains],name='widen')(*arrays,*plain,both,*gains)

def local(nd,nt,tokens,w_query,w_key,w_value,w_out,w_gate,w_up,w_down,norm_attn,norm_mlp,norm_query,norm_key,cotangent,segments,positions):
    scale=HD**-0.5
    ne=cotangent.shape[0]//4
    a1,q,k,v,xh,r,cos,sin,early,late=front(tokens,cotangent,positions,jnp.asarray(FREQS[:,None]),norm_attn,norm_query,norm_key,w_query,w_key,w_value,ne,4,1)
    late=lax.ppermute(late,'tensor',[(i,(i+2)%nt) for i in range(nt)])
    att,lse=attn_fwd(q,k,v,positions,512,512,scale)
    att,late=lax.optimization_barrier((att,late))
    hid,a2,act,dg,du,outp,dap,dy=middle(att,w_out,tokens,cotangent,early,late,w_gate,w_up,w_down,norm_mlp,4,2)
    dhid,gm,dwg,dwu,both,dout=post(hid,cotangent,norm_mlp,w_out,a2,dy,act,dg,du,dap,att,nd,3)
    output,d_tokens,dwq,dwk,dwv,both,ga,gm,gq,gk=tail(tokens,norm_attn,norm_query,norm_key,gm,w_query,w_key,w_value,positions,lse,r,both,
        q,k,v,dout,att,xh,cos,sin,a1,outp,hid,dhid,nd,nt,512,256,scale,4)
    dwq,dwk,dwv,dwg,dwu,output,d_tokens,dwd,dwo,ga,gm,gq,gk=widen((dwq,dwk,dwv,dwg,dwu),(output,d_tokens),both,(ga,gm,gq,gk),w_down.shape[0],nd)
    return (output,d_tokens,dwq,dwk,dwv,dwo,dwg,dwu,dwd,ga,gm,gq,gk)

def solution(mesh):
    nd,nt=mesh.shape['dp'],mesh.shape['tensor']
    row=P(('dp','tensor'),None); col=P(None,'tensor'); rw=P('tensor',None)
    return jax.shard_map(functools.partial(local,nd,nt),mesh=mesh,
        in_specs=(row,col,col,col,rw,col,col,rw,P(),P(),P(),P(),row,P('dp',None),P('dp',None)),
        out_specs=(row,row,col,col,col,rw,col,col,rw,P(),P(),P(),P()),check_vma=False)
```

```python
import functools, math
import numpy as np
import jax, jax.numpy as jnp
from jax import lax
from jax.sharding import PartitionSpec as P
from jax.experimental import pallas as pl
from jax.experimental.pallas import tpu as pltpu
HD=128
EPS=1e-6
F32=jnp.float32; BF=jnp.bfloat16
NT=(((1,),(1,)),((),()))
TN=(((0,),(0,)),((),()))
NN=(((1,),(0,)),((),()))
LOG2E=math.log2(math.e)
THETA=1000000.0
LONGEST=1024
FREQS=(THETA**(-np.arange(0,HD,2,dtype=np.float64)/HD)).astype(np.float32)
MESH=pl.DeviceIdType.MESH
D_=pltpu.SemaphoreType.DMA
S_=jax.ShapeDtypeStruct
V_=pl.BlockSpec(memory_space=pltpu.VMEM); A_=pl.BlockSpec(memory_space=pl.ANY)

def dot(a,b,dims=NN): return lax.dot_general(a,b,dims,preferred_element_type=F32)

def vec(ref): return ref[...].astype(F32).reshape(1,-1)

def group():
    t=lax.axis_index('tensor')
    mate=t+1-2*lax.rem(t,2)
    return t,mate,lax.rem(t+2,4),lax.rem(mate+2,4)

def greet(peers):
    barrier=pltpu.get_barrier_semaphore()
    for axis,p in peers:
        pl.semaphore_signal(barrier,inc=1,device_id={axis:p},device_id_type=MESH)
    pl.semaphore_wait(barrier,len(peers))

def send(src,dst,ss,rs,peer,axis='tensor'):
    return pltpu.make_async_remote_copy(src_ref=src,dst_ref=dst,send_sem=ss,recv_sem=rs,device_id={axis:peer},device_id_type=MESH)

def span(i,step,mult=None): return pl.ds(pl.multiple_of(i*step,mult or step),step)

def rows_of(ref,b,j,r,per): return ref.at[pl.ds(pl.multiple_of(b*per+j*r,r),r)]

def each(n,f):
    def body(i,_):
        f(i)
        return 0
    lax.fori_loop(0,n,body,0)

def each_rows(n,f,step=64): each(n//step,lambda i: f(span(i,step)))

def when_each(k,table):
    for at,f in table: pl.when(k==at)(f)

def call(kernel,ins,outs,scratch,cid,name,out_specs,in_specs,limit=67043328):
    return pl.pallas_call(kernel,in_specs=in_specs,out_specs=out_specs,out_shape=outs,scratch_shapes=scratch,
        compiler_params=pltpu.CompilerParams(collective_id=cid,has_side_effects=True,vmem_limit_bytes=limit),name=name)(*ins)

def attn_fwd_kernel(bq,bk,ratio,scale,pos_ref,q_ref,k_ref,v_ref,prow_ref,o_ref,l_ref,vx_ref,acc_ref):
    i=pl.program_id(1)
    n=k_ref.shape[0]
    @pl.when(i==0)
    def _():
        vx_ref[:,:HD]=v_ref[...]
        vx_ref[:,HD:]=jnp.ones((n,HD),BF)
    q=q_ref[...]
    qs=jnp.concatenate([q[:,h*HD:(h+1)*HD] for h in range(ratio)],0)
    rows=lax.rem(lax.broadcasted_iota(jnp.int32,(ratio*bq,1),0),bq)+i*bq
    start=jnp.broadcast_to(prow_ref[...].astype(F32),(HD,bq)).T[:,0:1].astype(jnp.int32)
    start=rows-jnp.concatenate([start]*ratio,0)
    acc_ref[...]=jnp.zeros_like(acc_ref)
    c=scale*LOG2E
    def step(j,_):
        b=pl.multiple_of(j*bk,bk)
        s=dot(qs,k_ref[pl.ds(b,bk),:],NT)
        cols=lax.broadcasted_iota(jnp.int32,(1,bk),1)+b
        m=(rows>=cols)&(start<=cols)
        e=jnp.where(m,jnp.exp2(s*c),0.0).astype(BF)
        acc_ref[...]+=dot(e,vx_ref[pl.ds(b,bk),:])
        return 0
    lax.fori_loop((i*bq-pos_ref[i*bq])//bk,(i*bq+bq-1)//bk+1,step,0)
    a=acc_ref[...]
    l=a[:,HD:]
    o=(a[:,:HD]/l).astype(BF)
    lt=jnp.log2(l).T[0:1]
    for h in range(ratio):
        o_ref[:,h*HD:(h+1)*HD]=o[h*bq:(h+1)*bq]
        l_ref[h]=lt[:,h*bq:(h+1)*bq]

def attn_fwd(q,k,v,pos,bq,bk,scale):
    n,wq=q.shape; g=k.shape[1]//HD; ratio=wq//HD//g
    gs=pltpu.PrefetchScalarGridSpec(num_scalar_prefetch=1,grid=(g,n//bq),
        in_specs=[pl.BlockSpec((bq,ratio*HD),lambda g,i,p:(i,g)),
                  pl.BlockSpec((n,HD),lambda g,i,p:(0,g)),
                  pl.BlockSpec((n,HD),lambda g,i,p:(0,g)),
                  pl.BlockSpec((1,bq),lambda g,i,p:(0,i))],
        out_specs=[pl.BlockSpec((bq,ratio*HD),lambda g,i,p:(i,g)),
                   pl.BlockSpec((ratio,1,bq),lambda g,i,p:(g,0,i))],
        scratch_shapes=[pltpu.VMEM((n,2*HD),BF),pltpu.VMEM((ratio*bq,2*HD),F32)])
    return pl.pallas_call(functools.partial(attn_fwd_kernel,bq,bk,ratio,scale),grid_spec=gs,
        out_shape=[S_((n,wq),BF),S_((g*ratio,1,n),F32)],name='attn_fwd')(pos[0],q,k,v,pos)
def front_kernel(nc,x_ref,cot_ref,pos_ref,fr_ref,g_ref,gq_ref,gk_ref,wq_in,wk_in,wv_in,
                 a_o,q_o,k_o,v_o,xh_o,r_o,cos_o,sin_o,early_o,late_o,
                 xf,a_s,q_s,k_s,v_s,xh_s,r_s,cost,sint,cosn,sinn,wq_ref,wk_ref,wv_ref,lsem,osem,ss,rs,es):
    t,mate,far,diag=group()
    per=x_ref.shape[0]; r=per//nc; n=xf.shape[0]; half=HD//2
    outs=[(a_s,a_o,0),(q_s,q_o,0),(k_s,k_o,0),(v_s,v_o,0),(xh_s,xh_o,1),(r_s,r_o,2)]
    own=pltpu.make_async_copy(x_ref,rows_of(xf,t,0,per,per),lsem)
    own.start()
    weights=[pltpu.make_async_copy(a,b,es.at[3+i]) for i,(a,b) in enumerate(((wq_in,wq_ref),(wk_in,wk_ref),(wv_in,wv_ref)))]
    for c in weights: c.start()
    greet([('tensor',mate),('tensor',far)])
    across=lambda j: send(x_ref.at[span(j,r)],rows_of(xf,t,j,r,per),ss.at[0,j],rs.at[0,j],far)
    beside=lambda j: send(x_ref.at[span(j,r)],rows_of(xf,t,j,r,per),ss.at[1,j],rs.at[1,j],mate)
    onward=lambda j: send(rows_of(xf,far,j,r,per),rows_of(xf,far,j,r,per),ss.at[2,j],rs.at[2,j],mate)
    each(nc,lambda j: across(j).start())
    each(nc,lambda j: beside(j).start())
    early=send(cot_ref.at[0:early_o.shape[0]],early_o,es.at[0],es.at[1],far)
    keep=pltpu.make_async_copy(cot_ref.at[early_o.shape[0]:per],late_o,es.at[2])
    keep.start()
    gain,gq,gk=vec(g_ref),vec(gq_ref),vec(gk_ref)
    tt=256
    def table(i):
        c=span(i,tt)
        ang=fr_ref[...]*pos_ref[:,c].astype(F32)
        co,si=jnp.cos(ang),jnp.sin(ang)
        ct=jnp.concatenate([co,co],0); st=jnp.concatenate([-si,si],0)
        cost[:,c]=ct; sint[:,c]=st
        cosn[c,:]=ct.T; sinn[c,:]=st.T
    each(n//tt,table)
    tabs=[pltpu.make_async_copy(cost,cos_o,osem.at[6,0]),pltpu.make_async_copy(sint,sin_o,osem.at[7,0])]
    for c in tabs: c.start()
    def out_copy(o,i):
        s,d,ax=outs[o]
        c=span(i,r)
        at=(c,(slice(None),c),(slice(None),slice(None),c))[ax]
        return pltpu.make_async_copy(s.at[at],d.at[at],osem.at[o,i])
    def tile(b,j):
        p=pl.multiple_of(b*per+j*r,r)
        rows=pl.ds(p,r)
        x=xf[rows,:].astype(F32)
        a=(x*lax.rsqrt(jnp.mean(x*x,-1,keepdims=True)+EPS)*gain).astype(BF)
        a_s[rows,:]=a
        v_s[rows,:]=dot(a,wv_ref[...]).astype(BF)
        cos=cosn[rows,:]; sin=sinn[rows,:]
        h0=0
        for w_ref,g,dst in ((wq_ref,gq,q_s),(wk_ref,gk,k_s)):
            raw=dot(a,w_ref[...])
            for h in range(raw.shape[1]//HD):
                rh=raw[:,h*HD:(h+1)*HD]
                u=rh*lax.rsqrt(jnp.mean(rh*rh,-1,keepdims=True)+EPS)*g
                dst[rows,h*HD:(h+1)*HD]=(u*cos+pltpu.roll(u,half,1)*sin).astype(BF)
                rt=rh.T
                rr=lax.rsqrt(jnp.mean(rt*rt,0,keepdims=True)+EPS)
                xh_s[(h0+h)*HD:(h0+h+1)*HD,rows]=(rt*rr).astype(BF)
                r_s[h0+h,:,rows]=rr
            h0+=raw.shape[1]//HD
        for o in range(6): out_copy(o,b*nc+j).start()
    for c in [own]+weights: c.wait()
    each(nc,lambda j: tile(t,j))
    each(nc,lambda j: beside(j).wait_recv())
    each(nc,lambda j: tile(mate,j))
    def body(j):
        across(j).wait_recv()
        pl.when(j==nc-2)(lambda: early.start())
        onward(j).start()
        tile(far,j)
        onward(j).wait_recv()
        tile(diag,j)
    each(nc,body)
    def drain(j):
        across(j).wait_send(); beside(j).wait_send(); onward(j).wait_send()
    each(nc,drain)
    def flush(i):
        for o in range(6): out_copy(o,i).wait()
    each(n//r,flush)
    for c in tabs: c.wait()
    early.wait()
    keep.wait()

def front(x,cot,pos,freqs,gain,gq,gk,wq,wk,wv,first,nc,cid):
    n=4*x.shape[0]; d=x.shape[1]
    wide=wq.shape[1]+wk.shape[1]
    shapes=[((n,d),BF),((n,wq.shape[1]),BF),((n,wk.shape[1]),BF),((n,wv.shape[1]),BF),((wide,n),BF),((wide//HD,1,n),F32),((HD,n),F32),((HD,n),F32)]
    return call(functools.partial(front_kernel,nc),(x,cot,pos,freqs,gain,gq,gk,wq,wk,wv),[S_(*s) for s in shapes]+[S_((first,d),BF),S_((x.shape[0]-first,d),BF)],
        [pltpu.VMEM((n,d),BF)]+[pltpu.VMEM(*s) for s in shapes]+[pltpu.VMEM((n,HD),F32)]*2+[pltpu.VMEM(w.shape,BF) for w in (wq,wk,wv)]+[D_,D_((8,4*nc)),D_((3,nc)),D_((3,nc)),D_((6,))],cid,'front',[A_]*10,[A_]*2+[V_]*5+[A_]*3)
def ring_neighbours(d):
    me=lax.axis_index('dp')
    half=d//2
    odd=lax.rem(me,2); up=me//2
    pos=odd*(d-1-2*up)+up
    def at(p):
        hi=p//half
        return hi*(2*(d-1-p)+1)+(1-hi)*2*p
    return pos,at(lax.rem(pos+1,d)),at(lax.rem(pos+d-1,d))

class Ring:
    def __init__(self,d,sems,make=None):
        self.d,self.sems,self.make=d,sems,make
        self.pos,right,left=ring_neighbours(d)
        self.to=(right,left)
        self.units=[]
    def add(self,s,rc,mine,sbuf,recv,out): self.units.append((s,rc,mine,sbuf,recv,out))
    def chunk(self,s,k): return lax.rem(self.pos-k+2*self.d,self.d) if s==0 else lax.rem(self.pos+k,self.d)
    def rs(self,u,k,src):
        return send(src,self.units[u][4].at[k],self.sems[0].at[u,k],self.sems[1].at[u,k],self.to[self.units[u][0]],'dp')
    def ag(self,u,k,c):
        s,rc,_,_,_,out=self.units[u]
        ref=out.at[span(c,rc)]
        return send(ref,ref,self.sems[2].at[u,k],self.sems[3].at[u,k],self.to[s],'dp')
    def start(self):
        for u,(s,rc,mine,sbuf,recv,out) in enumerate(self.units):
            sbuf[...]=mine(0).astype(BF)
            self.rs(u,0,sbuf).start()
    def reduce_step(self,k):
        for u,(s,rc,mine,sbuf,recv,out) in enumerate(self.units):
            self.rs(u,k-1,sbuf).wait_recv()
            val=(mine(k)+recv[k-1].astype(F32)).astype(BF)
            @pl.when(k<self.d-1)
            def _():
                recv[k-1]=val
                self.rs(u,k,recv.at[k-1]).start()
            @pl.when(k==self.d-1)
            def _():
                c=self.chunk(s,k)
                out[span(c,rc),:]=val
                self.ag(u,0,c).start()
        if self.make: pl.when(k<self.d-1)(lambda: self.make(k+1))
    def gather_step(self,k):
        for u,(s,rc,mine,sbuf,recv,out) in enumerate(self.units):
            c=self.chunk(s,k-1)
            self.ag(u,k-1,c).wait_recv()
            @pl.when(k<self.d-1)
            def _(): self.ag(u,k,c).start()
    def any_step(self,m):
        pl.when(m<self.d)(lambda: self.reduce_step(m))
        pl.when(m>=self.d)(lambda: self.gather_step(m-self.d+1))
    def drain(self):
        def body(k):
            for u,(s,rc,mine,sbuf,recv,out) in enumerate(self.units):
                self.rs(u,k,sbuf).wait_send()
                self.ag(u,k,0).wait_send()
        each(self.d-1,body)

class Scatter:
    def __init__(self,ids,per,rbuf,fbuf,ybuf,acc,ss,rs):
        self.t,self.mate,self.far,self.diag=ids
        self.per=per; self.rbuf,self.fbuf,self.ybuf,self.acc,self.ss,self.rs=rbuf,fbuf,ybuf,acc,ss,rs
    @staticmethod
    def scratch(per,w): return [pltpu.VMEM((2,per,w),BF),pltpu.VMEM((per,w),BF),pltpu.VMEM((per,w),BF),pltpu.VMEM((per,w),F32),D_((3,)),D_((3,))]
    def to_mate(self,i,src): return send(src,self.rbuf.at[i],self.ss.at[i],self.rs.at[i],self.mate)
    def across(self): return send(self.fbuf,self.ybuf,self.ss.at[2],self.rs.at[2],self.far)
    def pair(self,far_part,own_part,base=None):
        self.pair_far(far_part)
        self.pair_own(own_part,base)
    def pair_far(self,far_part):
        self.to_mate(1,self.fbuf).wait_recv()
        def far_rows(r): self.fbuf[r,:]=(far_part[r,:].astype(F32)+self.rbuf[1,r,:].astype(F32)).astype(BF)
        each_rows(self.per,far_rows)
        self.across().start()
    def pair_own(self,own_part,base=None):
        self.to_mate(0,self.fbuf).wait_recv()
        def own_rows(r):
            v=own_part[r,:].astype(F32)+self.rbuf[0,r,:].astype(F32)
            self.acc[r,:]=v if base is None else v+base[r,:]
        each_rows(self.per,own_rows)
    def result(self,f):
        self.across().wait_recv()
        each_rows(self.per,lambda r: f(r,self.acc[r,:]+self.ybuf[r,:].astype(F32)))
    def drain(self):
        self.to_mate(0,self.fbuf).wait_send(); self.to_mate(1,self.fbuf).wait_send(); self.across().wait_send()

def norm_bwd(v,gain,e):
    r=lax.rsqrt(jnp.mean(v*v,-1,keepdims=True)+EPS)
    vh=v*r
    ge=e*gain
    return r*(ge-vh*jnp.mean(vh*ge,-1,keepdims=True)),jnp.sum(e*vh,0,keepdims=True)
def mid_kernel(nc,att_ref,wo_ref,x_in,cot_ref,early_ref,late_ref,wg_ref,wu_ref,wd_ref,g_ref,
               hid_o,a_o,act_o,dg_o,du_o,op_o,da_o,dy_o,
               attv,wov,dyv,wgv,wuv,wdv,full,act_s,dg_s,du_s,op_s,da_s,acc,pbuf,rbuf,fbuf,ybuf,x_ref,hid_ref,lsem,osem,ss,rs,dsem):
    t,mate,far,diag=group()
    per=x_ref.shape[0]; r=per//nc; n=full.shape[0]
    ne=early_ref.shape[0]
    loads=[pltpu.make_async_copy(s,d,lsem.at[i]) for i,(s,d) in enumerate(((att_ref,attv),(wo_ref,wov),(cot_ref,rows_of(dyv,t,0,per,per)),(wg_ref,wgv),(wu_ref,wuv),(wd_ref,wdv),(early_ref,dyv.at[pl.ds(pl.multiple_of(far*per,per),ne)]),(late_ref,dyv.at[pl.ds(pl.multiple_of(far*per+ne,ne),per-ne)])))]
    xl=pltpu.make_async_copy(x_in,x_ref,lsem.at[9])
    for c in loads[:2]+[xl]+loads[2:]: c.start()
    greet([('tensor',mate),('tensor',far)])
    dys=[send(cot_ref,rows_of(dyv,t,0,per,per),dsem.at[0],dsem.at[1],mate),send(early_ref,dyv.at[pl.ds(pl.multiple_of(far*per,per),ne)],dsem.at[2],dsem.at[3],mate),send(late_ref,dyv.at[pl.ds(pl.multiple_of(far*per+ne,ne),per-ne)],dsem.at[4],dsem.at[5],mate)]
    outs=[(full,a_o),(act_s,act_o),(dg_s,dg_o),(du_s,du_o),(op_s,op_o),(da_s,da_o)]
    gain=vec(g_ref)
    def proj(b,j):
        return dot(rows_of(attv,b,j,r,per)[...],wov[...])
    def to_mate(i,j):
        return send(pbuf.at[i,pl.ds(pl.multiple_of(j*r,r),r)],rbuf.at[i,pl.ds(pl.multiple_of(j*r,r),r)],ss.at[i,j],rs.at[i,j],mate)
    def to_far(j):
        rr=pl.ds(pl.multiple_of(j*r,r),r)
        return send(fbuf.at[rr],ybuf.at[rr],ss.at[2,j],rs.at[2,j],far)
    def share(j,i,peer):
        return send(rows_of(full,t,j,r,per),rows_of(full,t,j,r,per),ss.at[i,j],rs.at[i,j],peer)
    def forward(j):
        return send(rows_of(full,far,j,r,per),rows_of(full,far,j,r,per),ss.at[5,j],rs.at[5,j],mate)
    loads[0].wait(); loads[1].wait(); xl.wait()
    def reduce(j,_):
        rr=pl.ds(pl.multiple_of(j*r,r),r)
        pbuf[1,rr,:]=proj(diag,j).astype(BF); to_mate(1,j).start()
        pbuf[0,rr,:]=proj(mate,j).astype(BF); to_mate(0,j).start()
        f=proj(far,j)
        to_mate(1,j).wait_recv()
        fbuf[rr,:]=(f+rbuf[1,rr,:].astype(F32)).astype(BF)
        to_far(j).start()
        @pl.when(j==0)
        def _():
            for c in dys: c.start()
        o=proj(t,j)
        to_mate(0,j).wait_recv()
        acc[rr,:]=o+rbuf[0,rr,:].astype(F32)+x_ref[rr,:].astype(F32)
        return 0
    lax.fori_loop(0,nc,reduce,0)
    for i in range(2,8): loads[i].wait()
    for c in dys: c.wait_recv()
    dyc=pltpu.make_async_copy(dyv,dy_o,lsem.at[8])
    dyc.start()
    def mlp_rows(b,j,m=1):
        rows=pl.ds(pl.multiple_of(b*per+j*r,r),m*r)
        a=full[rows,:]
        gate=dot(a,wgv[...]); up=dot(a,wuv[...])
        dact=dot(dyv[rows,:],wdv[...],NT)
        sig=1.0/(1.0+jnp.exp(-gate))
        sl=gate*sig
        act=(sl*up).astype(BF)
        act_s[rows,:]=act
        dg=(dact*up*(sig*(1.0+gate*(1.0-sig)))).astype(BF)
        du=(dact*sl).astype(BF)
        dg_s[rows,:]=dg; du_s[rows,:]=du
        op_s[rows,:]=dot(act,wdv[...]).astype(BF)
        da_s[rows,:]=(dot(dg,wgv[...],NT)+dot(du,wuv[...],NT)).astype(BF)
        for o,(s,d) in enumerate(outs):
            for z in range(m):
                part=pl.ds(pl.multiple_of(b*per+(j+z)*r,r),r)
                pltpu.make_async_copy(s.at[part],d.at[part],osem.at[o,b*nc+j+z]).start()
    def two(f): lax.fori_loop(0,2,lambda i,_: (f(i),0)[1],0)
    def near(jj):
        def chunk(i):
            j=2*jj+i
            rr=span(j,r)
            to_far(j).wait_recv()
            h=acc[rr,:]+ybuf[rr,:].astype(F32)
            hid_ref[rr,:]=h
            rows_of(full,t,j,r,per)[...]=(h*lax.rsqrt(jnp.mean(h*h,-1,keepdims=True)+EPS)*gain).astype(BF)
            share(j,3,far).start(); share(j,4,mate).start()
        two(chunk)
        def rows(i):
            @pl.when(i==1)
            def _():
                for z in range(2): share(2*jj+z,4,mate).wait_recv()
            mlp_rows(t+i*(mate-t),2*jj,2)
        two(rows)
    each(nc//2,near)
    hc=pltpu.make_async_copy(hid_ref,hid_o,lsem.at[10])
    hc.start()
    def arrive(j):
        share(j,3,far).wait_recv()
        forward(j).start()
    def away(j,m):
        for z in range(m): arrive(j+z)
        def rows(i):
            @pl.when(i==1)
            def _():
                for z in range(m): forward(j+z).wait_recv()
            mlp_rows(far+i*(diag-far),j,m)
        two(rows)
    each(nc//2-1,lambda jj: away(2*jj,2))
    each(2,lambda z: away(nc-2+z,1))
    def drain(j,_):
        to_mate(0,j).wait_send(); to_mate(1,j).wait_send(); to_far(j).wait_send()
        share(j,3,far).wait_send(); share(j,4,mate).wait_send(); forward(j).wait_send()
        return 0
    lax.fori_loop(0,nc,drain,0)
    def flush(i,_):
        rows=pl.ds(pl.multiple_of(i*r,r),r)
        for o,(s,d) in enumerate(outs):
            pltpu.make_async_copy(s.at[rows],d.at[rows],osem.at[o,i]).wait()
        return 0
    lax.fori_loop(0,n//r,flush,0)
    dyc.wait()
    hc.wait()
    for c in dys: c.wait_send()

def middle(att,wo,x,cot,early,late,wg,wu,wd,gain,nc,cid):
    n=att.shape[0]; per,d=x.shape; f=wg.shape[1]
    rows=[((n,d),BF),((n,f),BF),((n,f),BF),((n,f),BF),((n,d),BF),((n,d),BF)]
    return call(functools.partial(mid_kernel,nc),(att,wo,x,cot,early,late,wg,wu,wd,gain),[S_((per,d),F32)]+[S_(*s) for s in rows]+[S_((n,d),BF)],
        [pltpu.VMEM(s,BF) for s in (att.shape,wo.shape,(n,d),wg.shape,wu.shape,wd.shape)]+[pltpu.VMEM(*s) for s in rows]+
        [pltpu.VMEM((per,d),F32),pltpu.VMEM((2,per,d),BF),pltpu.VMEM((2,per,d),BF),pltpu.VMEM((per,d),BF),pltpu.VMEM((per,d),BF),pltpu.VMEM((per,d),BF),pltpu.VMEM((per,d),F32),
         D_((11,)),D_((6,4*nc)),D_((6,nc)),D_((6,nc)),D_((6,))],cid,'middle',[A_]*8,[A_,A_,A_,A_,A_,A_,A_,A_,A_,V_])
def post_kernel(d,fused,hid_in,cot_in,g_ref,wo_in,a_ref,dy_ref,act_ref,dg_ref,du_ref,da_ref,att_ref,
                dhid_o,gg_ref,dwg_o,dwu_o,both_ref,dout_o,
                av,ac,dyv,actv,dgv,duv,attv,full,doutv,parts,ownbuf,sbuf,recv,dhid_ref,hid_ref,cot_ref,wo_ref,dwg_ref,dwu_ref,wsem,lsem,osem,ss,rs,m0,m1,m2,m3,oacc,*rest):
    ids=t,mate,far,diag=group()
    per,dm=hid_ref.shape; n=full.shape[0]; f=dgv.shape[1]; rc=dm//d
    rs1=Scatter(ids,per,*rest[:6])
    whole=None if fused else rest[6]
    def make(k):
        if fused:
            for s in range(2): ownbuf[s]=dot(av[:,span(ring.chunk(s,k),rc)],(dgv,duv)[s][...],TN)
    ring=Ring(d,(m0,m1,m2,m3),make)
    nu=3
    w=f//nu
    for j in range(nu):
        for s,out in enumerate((dwg_ref,dwu_ref)):
            lo,hi=j*w,(j+1)*w
            def mine(k,s=s,lo=lo,hi=hi):
                if fused: return ownbuf[s,:,lo:hi]
                return whole[s,span(ring.chunk(s,k),rc),lo:hi].astype(F32)
            ring.add(s,rc,mine,sbuf.at[s,:,lo:hi],recv.at[s,:,:,lo:hi],out.at[:,lo:hi])
    c0=pl.multiple_of(ring.chunk(0,0)*rc,128) if fused else 0
    loads=[pltpu.make_async_copy(s,x,lsem.at[i]) for i,(s,x) in enumerate(((dg_ref,dgv),(a_ref.at[:,pl.ds(c0,128)],ac),(du_ref,duv),(a_ref,av),(dy_ref,dyv),(act_ref,actv),(att_ref,attv)))]
    blk=lambda ref,b: rows_of(ref,b,0,per,per)
    parts_=[pltpu.make_async_copy(blk(da_ref,b),parts.at[i],lsem.at[7+i]) for i,b in enumerate((far,t))]
    plain=[pltpu.make_async_copy(a,b,lsem.at[9+i]) for i,(a,b) in enumerate(((hid_in,hid_ref),(cot_in,cot_ref),(wo_in,wo_ref)))]
    for c in loads[:4]+parts_+loads[4:]+plain: c.start()
    greet([('tensor',mate),('tensor',far),('dp',ring.to[0]),('dp',ring.to[1])])
    rs1.to_mate(1,blk(da_ref,diag)).start(); rs1.to_mate(0,blk(da_ref,mate)).start()
    for c in loads[:3]: c.wait()
    if fused:
        for s in range(2): ownbuf[s]=dot(ac[...],(dgv,duv)[s][...],TN)
        ring.start()
        loads[3].wait()
        make(1)
    else:
        loads[3].wait()
        for s in range(2):
            def tile(i,s=s): whole[s,span(i,128),:]=dot(av[:,span(i,128)],(dgv,duv)[s][...],TN).astype(BF)
            each(dm//128,tile)
        ring.start()
    share=lambda i,p: send(blk(full,t),blk(full,t),ss.at[i],rs.at[i],p)
    onward=lambda: send(blk(full,far),blk(full,far),ss.at[2],rs.at[2],mate)
    def e1():
        for c in parts_: c.wait()
        rs1.pair(parts.at[0],parts.at[1])
    def e2():
        for c in plain: c.wait()
        gg_ref[...]=jnp.zeros_like(gg_ref)
        mine=blk(full,t)
        gain=vec(g_ref)
        def rows(r,da):
            dh,gg=norm_bwd(hid_ref[r,:],gain,da)
            dh=dh+cot_ref[r,:].astype(F32)
            dhid_ref[r,:]=dh; gg_ref[...]+=gg
            mine[r,:]=dh.astype(BF)
        rs1.result(rows)
        pltpu.make_async_copy(dhid_ref,dhid_o,osem.at[1]).start()
        share(0,far).start(); share(1,mate).start()
    rd,ro=f//d,wo_ref.shape[0]//d
    def put_rows(first,r,c,v):
        for j in range(d): both_ref[j*(rd+ro)+first:j*(rd+ro)+first+r,c]=v[j*r:(j+1)*r].astype(BF)
    def down(i):
        put_rows(0,rd,span(i,256),dot(actv[...],dyv[:,span(i,256)],TN))
    nd_=dm//256
    tt=256
    def dout_rows(b,last=False):
        def tile(i):
            rows=pl.ds(pl.multiple_of(b*per+i*tt,tt),tt)
            doutv[rows,:]=dot(full[rows,:],wo_ref[...],NT).astype(BF)
        each(per//tt,tile)
        if last: pltpu.make_async_copy(doutv,dout_o,osem.at[0]).start()
    def out_rows(b,last=False):
        rows=span(b,per)
        def out_tile(i):
            c=span(i,256)
            v=dot(attv[rows,:],full[rows,c],TN)
            if last: put_rows(rd,ro,c,oacc[:,c]+v)
            else: oacc[:,c]+=v
        each(dm//256,out_tile)
    def e3():
        loads[6].wait()
        oacc[...]=jnp.zeros_like(oacc)
        dout_rows(t)
    def e4():
        share(1,mate).wait_recv()
        dout_rows(mate)
    def e5():
        share(0,far).wait_recv()
        onward().start()
        dout_rows(far)
    def step(k):
        when_each(k,((1,e1),(d-1,e2)))
        ring.reduce_step(k)
        @pl.when(k==2)
        def _():
            for c in loads[4:6]: c.wait()
        pl.when((k>=2)&(k<2+nd_))(lambda: down(k-2))
    lax.fori_loop(1,d,lambda k,_: (step(k),0)[1],0)
    def save(s,c):
        rows=span(c,rc)
        return pltpu.make_async_copy((dwg_ref,dwu_ref)[s].at[rows],(dwg_o,dwu_o)[s].at[rows],wsem.at[s,c])
    for s in range(2): save(s,ring.chunk(s,d-1)).start()
    def gstep(k):
        ring.gather_step(k)
        for s in range(2): save(s,ring.chunk(s,k-1)).start()
        when_each(k,((1,e3),(2,lambda: out_rows(t)),(3,e4),(4,lambda: out_rows(mate)),(d-3,e5),(d-2,lambda: out_rows(far))))
    lax.fori_loop(1,d,lambda k,_: (gstep(k),0)[1],0)
    onward().wait_recv()
    dout_rows(diag,True)
    out_rows(diag,True)
    ring.drain(); rs1.drain()
    def saved(c):
        for s in range(2): save(s,c).wait()
    each(d,saved)
    share(0,far).wait_send(); share(1,mate).wait_send(); onward().wait_send()
    pltpu.make_async_copy(doutv,dout_o,osem.at[0]).wait()
    pltpu.make_async_copy(dhid_ref,dhid_o,osem.at[1]).wait()

def post(hid,cot,gain,wo,a2,dy,act,dg,du,dap,att,d,cid):
    per,dm=hid.shape; n=a2.shape[0]; f=act.shape[1]
    fused=(dm//d)%128==0
    M=pltpu.VMEM
    wo_=wo.shape[0]
    return call(functools.partial(post_kernel,d,fused),(hid,cot,gain,wo,a2,dy,act,dg,du,dap,att),
        [S_((per,dm),F32),S_((1,dm),F32),S_((dm,f),BF),S_((dm,f),BF),S_((f+wo_,dm),BF),S_((n,wo_),BF)],
        [M((n,dm),BF),M((n,128),BF),M((n,dm),BF),M((n,f),BF),M((n,f),BF),M((n,f),BF),M((n,wo_),BF),M((n,dm),BF),M((n,wo_),BF),M((2,per,dm),BF),
         M((2,dm//d,f),F32),M((2,dm//d,f),BF),M((2,d-1,dm//d,f),BF),M((per,dm),F32),M((per,dm),F32),M((per,dm),BF),M(wo.shape,BF),M((dm,f),BF),M((dm,f),BF),D_((2,d)),D_((12,)),D_((2,)),D_((3,)),D_((3,))]+[D_((6,d-1))]*4+[M((wo_,dm),F32)]+Scatter.scratch(per,dm)+([] if fused else [M((2,dm,f),BF)]),
        cid,'post',[A_,V_,A_,A_,V_,A_],[A_,A_,V_,A_]+[A_]*7)
LATE=4
def rot_norm_bwd(dt,xh,r,gain,cos,sin):
    h=HD//2
    du=dt*cos-jnp.concatenate([dt[h:],dt[:h]],0)*sin
    ge=du*gain
    return r*(ge-xh*jnp.mean(xh*ge,0,keepdims=True)),du*xh

def tail_kernel(d,nt,nr,fused,bq,bk,scale,x_in,g_ref,gq_ref,gk_ref,gm_ref,wq_in,wk_in,wv_in,pos_ref,lse_ref,r_ref,both_in,
                q_ref,k_ref,v_ref,do_ref,att_ref,xh_ref,cos_ref,sin_ref,a_ref,op_ref,hid_ref,dhid_ref,
                out_o,dx_o,dwq_o,dwk_o,dwv_o,both_o,ga_o,gm_o,gq_o,gk_o,
                both_ref,x_ref,wq_ref,wk_ref,wv_ref,dx_ref,u1,kv,vv,attv,xhv,cosv,sinv,dj,dka,dva,dqa,qs,os_,kt,dd,gacc,gcol,ac,
                pbuf,farbuf,ownbuf,gbuf,grecv,bothv,outv,b2,r2,b3,r3,lsem,gs,gr,*sems):
    ids=t,mate,far,diag=group()
    per,dm=x_ref.shape; n=u1.shape[0]
    p,(t0,t1,t2,t3),rest=sems[0],sems[1:5],sems[5:]
    wq,wk,wv,wo=attv.shape[1],kv.shape[1],vv.shape[1],attv.shape[1]
    rc=dm//d
    sc=Scatter(ids,per,*rest[:6]); so=Scatter(ids,per,*rest[6:12])
    whole=None if fused else rest[12]
    blk=lambda ref,b: rows_of(ref,b,0,per,per)
    loads=[pltpu.make_async_copy(s,x,lsem.at[i]) for i,(s,x) in enumerate(((q_ref,u1.at[:,0:wq]),(k_ref,kv),(v_ref,vv),(do_ref,u1.at[:,wq:2*wq]),(att_ref,attv),(xh_ref,xhv),(cos_ref,cosv),(sin_ref,sinv)))]
    h=dm//2; w1=h//nr
    rr=both_ref.shape[0]//d
    def first_ring(y):
        ring=Ring(d,[p.at[i,y] for i in range(4)])
        for s in range(2):
            cs=pl.ds(pl.multiple_of(s*h+y*w1,w1),w1); bs=pl.ds(pl.multiple_of(y*w1,w1),w1)
            ring.add(s,rr,lambda k,s=s,cs=cs,ring=ring: both_ref[span(ring.chunk(s,k),rr),cs].astype(F32),b2.at[s,:,bs],r2.at[s,:,:,bs],bothv.at[:,cs])
        return ring
    first=first_ring(0)
    def make(k):
        if fused:
            c=first.chunk(0,k); e=first.chunk(1,k)
            ownbuf[0]=dot(u1[:,span(c,rc)],dj[:,0:wq],TN)
            ownbuf[1]=dot(u1[:,span(e,rc)],dj[:,wq:2*wq],TN)
    second=Ring(d,(t0,t1,t2,t3),make)
    w2=128
    for lo in range(0,wq,w2):
        for s in range(2):
            out=dwq_o.at[:,lo:lo+w2] if s==0 else (dwk_o.at[:,lo:lo+w2] if lo<wk else dwv_o.at[:,lo-wk:lo-wk+w2])
            def mine(k,s=s,lo=lo):
                if fused: return ownbuf[s,:,lo:lo+w2]
                return whole[s,span(second.chunk(s,k),rc),lo:lo+w2].astype(F32)
            second.add(s,rc,mine,b3.at[s,:,lo:lo+w2],r3.at[s,:,:,lo:lo+w2],out)
    c0=pl.multiple_of(first.chunk(0,0)*rc,128) if fused else 0
    later=[pltpu.make_async_copy(a_ref.at[:,pl.ds(c0,128)],ac,lsem.at[8]),pltpu.make_async_copy(dhid_ref,dx_ref,lsem.at[9]),
           pltpu.make_async_copy(blk(op_ref,far),pbuf.at[0],lsem.at[10]),pltpu.make_async_copy(blk(op_ref,t),pbuf.at[1],lsem.at[11]),pltpu.make_async_copy(hid_ref,so.acc,lsem.at[12])]
    weights=[pltpu.make_async_copy(a,b,lsem.at[16+i]) for i,(a,b) in enumerate(((x_in,x_ref),(wq_in,wq_ref),(wk_in,wk_ref),(wv_in,wv_ref)))]
    mine=pltpu.make_async_copy(both_in,both_ref,lsem.at[21])
    for c in [mine]+loads+later+weights: c.start()
    steps=[]
    for axis,m in (('tensor',nt),('dp',d)):
        b=1
        while b<m:
            steps.append((axis,b)); b*=2
    def partner(axis,b):
        me=lax.axis_index(axis)
        return me+b-2*b*lax.rem(me//b,2)
    greet([('tensor',mate),('tensor',far),('dp',first.to[0]),('dp',first.to[1])]+[(a,partner(a,b)) for a,b in steps])
    mine.wait()
    each(nr,lambda y: first_ring(y).start())
    so.to_mate(1,blk(op_ref,diag)).start(); so.to_mate(0,blk(op_ref,mate)).start()
    def pair_out():
        for c in later[2:]: c.wait()
        so.pair(pbuf.at[0],pbuf.at[1],so.acc)
    def finish_out():
        def rows(r,v): outv[r,:]=v.astype(BF)
        so.result(rows)
    for i,ref in enumerate((gq_ref,gk_ref)): gcol[i]=jnp.broadcast_to(vec(ref),(HD,HD)).T
    gacc[...]=jnp.zeros_like(gacc)
    for c in loads[:5]: c.wait()
    groups=wk//HD; ratio=wq//wk; nb=n//bq; jb=bq//bk
    c2=scale*LOG2E
    total=2*nr*(d-1)
    assert bq==2*bk and LONGEST%bk==0
    back=LONGEST//bk
    first_key=lambda i: jnp.maximum(jb*i-back,0)
    sizes=[jb*(i+1)-max(jb*i-back,0) for i in range(nb)]
    per_group=sum(sizes)
    full=[i for i in range(nb) if jb*i<=back]
    iters=groups*(per_group+nb*ratio)
    hot=iters+LATE
    def before(i):
        u=jnp.minimum(i,len(full))
        return jb*u*(u+1)//2+(i-u)*(jb+back)
    hooks=iters
    def hook(it):
        when_each(it,((2,pair_out),(iters-1,finish_out)))
        for z in range(-(-total//iters)):
            m=it*total//hot+1+z
            pl.when(m<=(it+1)*total//hot)(lambda: first_ring(lax.rem(m-1,nr)).any_step((m-1)//nr+1))
    def lane_tiles(dt,head,gi,cols,put):
        for z in range(dt.shape[1]//HD):
            cs=pl.ds(pl.multiple_of(cols+z*HD,HD),HD)
            dx,gg=rot_norm_bwd(dt[:,z*HD:(z+1)*HD]*scale,xhv[span(head,HD),cs].astype(F32),r_ref[head,:,cs],gcol[gi],cosv[:,cs],sinv[:,cs])
            gacc[gi]+=gg
            put(cs,dx.T.astype(BF))
    def one_group(g):
        gl=pl.multiple_of(g*HD,HD)
        kcols=pl.ds(gl,HD)
        def prep(i):
            kt[:,span(i,bq)]=kv[span(i,bq),kcols].T
            dka[span(i,bq),:]=jnp.zeros((bq,HD),F32); dva[span(i,bq),:]=jnp.zeros((bq,HD),F32)
        each(nb,prep)
        qcol=[pl.ds(pl.multiple_of(g*ratio*HD+x*HD,HD),HD) for x in range(ratio)]
        dcol=[pl.ds(pl.multiple_of(wq+g*ratio*HD+x*HD,HD),HD) for x in range(ratio)]
        def q_block(i):
            rows=span(i,bq)
            hb=bq//2
            wide=ratio*bq
            cq=[lax.broadcasted_iota(jnp.int32,(1,hb),1)+i*bq+y*hb for y in range(2)]
            cols=jnp.concatenate([cq[y] for y in range(2) for x in range(ratio)],1)
            sts=cols-jnp.concatenate([pos_ref[:,pl.ds(pl.multiple_of(i*bq+y*hb,hb),hb)] for y in range(2) for x in range(ratio)],1)
            one=jnp.ones((8,HD),BF)
            for y in range(2):
                for x in range(ratio):
                    at=slice((y*ratio+x)*hb,(y*ratio+x+1)*hb)
                    rh=pl.ds(pl.multiple_of(i*bq+y*hb,hb),hb)
                    qx=u1[rh,qcol[x]]; ox=u1[rh,dcol[x]]
                    qs[at,:]=qx; os_[at,:]=ox
                    pr=ox.astype(F32)*attv[rh,qcol[x]].astype(F32)
                    hi=pr.astype(BF); lo=(pr-hi.astype(F32)).astype(BF)
                    dd[:,at]=dot(one,hi,NT)+dot(one,lo,NT)
                    dd[0:1,wide+at.start:wide+at.stop]=lse_ref[g*ratio+x,:,rh]
            dqa[...]=jnp.zeros_like(dqa)
            def key_block(j,lo,hi,causal):
                b=span(j,bk)
                kb=kv[b,kcols]
                cs=slice(lo,hi)
                s=dot(kb,qs[cs,:],NT)
                keys=lax.broadcasted_iota(jnp.int32,(bk,1),0)+j*bk
                m=sts[:,cs]<=keys
                if causal: m=m&(cols[:,cs]>=keys)
                p=jnp.where(m,jnp.exp2(s*c2-dd[0:1,wide+lo:wide+hi]),0.0)
                ds=(p*(dot(vv[b,kcols],os_[cs,:],NT)-dd[0:1,cs])).astype(BF)
                dva[b,:]+=dot(p.astype(BF),os_[cs,:])
                dka[b,:]+=dot(ds,qs[cs,:])
                dqa[:,cs]+=dot(kt[:,b],ds)
            def finish(x):
                if x==0:
                    @pl.when((g==0)&(i==0))
                    def _():
                        for c in loads[5:]: c.wait()
                def put(cs,v,x=x): dj[cs,qcol[x]]=v
                lane_tiles(jnp.concatenate([dqa[:,(y*ratio+x)*hb:(y*ratio+x+1)*hb] for y in range(2)],1),g*ratio+x,0,i*bq,put)
            j0,j1=first_key(i),(i+1)*jb
            def slot(j,_):
                far_back=(jb*i>=back)&(j==jb*i-back)
                pl.when(far_back)(lambda: key_block(j,0,wide//2,False))
                pl.when((j<jb*i)&jnp.logical_not(far_back))(lambda: key_block(j,0,wide,False))
                pl.when(j==jb*i)(lambda: key_block(j,0,wide,True))
                pl.when(j==jb*i+1)(lambda: key_block(j,wide//2,wide,True))
                for x in range(ratio): pl.when(j==j1+x)(lambda x=x: finish(x))
                hook(g*(per_group+nb*ratio)+before(i)+i*ratio+j-j0)
                return 0
            lax.fori_loop(j0,j1+ratio,slot,0)
        each(nb,q_block)
        def fin(i):
            rows=span(i,bq)
            dj[rows,pl.ds(pl.multiple_of(wq+wk+gl,HD),HD)]=dva[rows,:].astype(BF)
            def put(cs,v): dj[cs,pl.ds(pl.multiple_of(wq+gl,HD),HD)]=v
            lane_tiles(dka[rows,:].T,wq//HD+g,1,i*bq,put)
        each(nb,fin)
    each(groups,one_group)
    lax.fori_loop(iters*total//hot+1,total+1,lambda m,_: (first_ring(lax.rem(m-1,nr)).any_step((m-1)//nr+1),0)[1],0)
    saves=[pltpu.make_async_copy(bothv,both_o,lsem.at[14]),pltpu.make_async_copy(outv,out_o,lsem.at[15])]
    for c in saves: c.start()
    al=pltpu.make_async_copy(a_ref,u1,lsem.at[13])
    al.start()
    for c in later[:2]+weights: c.wait()
    if fused:
        ownbuf[0]=dot(ac[...],dj[:,0:wq],TN); ownbuf[1]=dot(ac[...],dj[:,wq:2*wq],TN)
    else:
        al.wait()
        for s in range(2):
            def tile(i,s=s): whole[s,span(i,128),:]=dot(u1[:,span(i,128)],dj[:,s*wq:(s+1)*wq],TN).astype(BF)
            each(dm//128,tile)
    second.start()
    if fused:
        al.wait()
        make(1)
    tp=256
    def part(b,ref,i):
        def tile(j):
            rows=pl.ds(pl.multiple_of(b*per+j*tp,tp),tp)
            v=dot(dj[rows,0:wq],wq_ref[...],NT)+dot(dj[rows,wq:wq+wk],wk_ref[...],NT)+dot(dj[rows,wq+wk:2*wq],wv_ref[...],NT)
            ref[i,span(j,tp),:]=v.astype(BF)
        each(per//tp,tile)
    part(diag,pbuf,1)
    sc.to_mate(1,pbuf.at[1]).start()
    part(far,farbuf,0)
    sc.pair_far(farbuf.at[0])
    def e0():
        part(mate,pbuf,0)
        sc.to_mate(0,pbuf.at[0]).start()
    def e1():
        part(t,farbuf,1)
        sc.pair_own(farbuf.at[1])
    def e2():
        gain=vec(g_ref)
        gbuf[:,0:dm]=jnp.zeros((1,dm),F32)
        gbuf[:,dm:2*dm]=gm_ref[...]
        gbuf[:,2*dm:2*dm+HD]=jnp.sum(gacc[0].T,0,keepdims=True)
        gbuf[:,2*dm+HD:2*dm+2*HD]=jnp.sum(gacc[1].T,0,keepdims=True)
        def rows(r,e):
            dv,gg=norm_bwd(x_ref[r,:].astype(F32),gain,e)
            dx_ref[r,:]+=dv
            gbuf[:,0:dm]+=gg
        sc.result(rows)
        pltpu.make_async_copy(dx_ref,dx_o,lsem.at[20]).start()
    def step(k):
        second.reduce_step(k)
        when_each(k,((1,e0),(2,e1)))
    lax.fori_loop(1,d,lambda k,_: (step(k),0)[1],0)
    cps=[send(grecv.at[2*i+1],grecv.at[2*i],gs.at[i],gr.at[i],partner(a,b),a) for i,(a,b) in enumerate(steps)]
    def turn(i):
        def f():
            if i==0: e2()
            else:
                cps[i-1].wait_recv()
                gbuf[...]+=grecv[2*i-2]
            if i<len(steps):
                grecv[2*i+1]=gbuf[...]
                cps[i].start()
        return f
    def gstep(k):
        when_each(k,[(i+2,turn(i)) for i in range(min(len(steps)+1,d-2))])
        second.gather_step(k)
    lax.fori_loop(1,d,lambda k,_: (gstep(k),0)[1],0)
    for i in range(d-2,len(steps)+1): turn(i)()
    ga_o[...]=gbuf[:,0:dm]; gm_o[...]=gbuf[:,dm:2*dm]; gq_o[...]=gbuf[:,2*dm:2*dm+HD]; gk_o[...]=gbuf[:,2*dm+HD:2*dm+2*HD]
    each(nr,lambda y: first_ring(y).drain())
    second.drain(); sc.drain(); so.drain()
    for c in cps: c.wait_send()
    for c in saves+[pltpu.make_async_copy(dx_ref,dx_o,lsem.at[20])]: c.wait()

def tail(x,g,gq,gk,gm,wq,wk,wv,pos,lse,r,both,q,k,v,do,att,xh,cos,sin,a1,op,hid,dhid,d,nt,bq,bk,scale,cid):
    per,dm=x.shape; n=a1.shape[0]
    nq,nk,nv=q.shape[1],k.shape[1],v.shape[1]
    assert nq==nk+nv
    fused=(dm//d)%128==0
    M=pltpu.VMEM
    ns=sum((s-1).bit_length() for s in (d,nt))
    ratio=nq//nk; rc=dm//d; h=dm//2
    row=lambda c: S_((1,c),F32)
    rr=both.shape[0]//d; nr=4
    ins=(x,g,gq,gk,gm,wq,wk,wv,pos,lse,r,both,q,k,v,do,att,xh,cos,sin,a1,op,hid,dhid)
    return call(functools.partial(tail_kernel,d,nt,nr,fused,bq,bk,scale),ins,
        [S_((per,dm),BF),S_((per,dm),F32),S_((dm,nq),BF),S_((dm,nk),BF),S_((dm,nv),BF),S_(both.shape,BF),row(dm),row(dm),row(HD),row(HD)],
        [M(both.shape,BF),M(x.shape,BF),M(wq.shape,BF),M(wk.shape,BF),M(wv.shape,BF),M((per,dm),F32),M((n,2*nq),BF),M((n,nk),BF),M((n,nv),BF),M((n,nq),BF),M(xh.shape,BF),M(cos.shape,F32),M(sin.shape,F32),M((n,2*nq),BF),M((n,HD),F32),M((n,HD),F32),
         M((HD,ratio*bq),F32),M((ratio*bq,HD),BF),M((ratio*bq,HD),BF),M((HD,n),BF),M((8,2*ratio*bq),F32),M((2,HD,HD),F32),M((2,HD,HD),F32),M((n,128),BF),
         M((2,per,dm),BF),M((2,per,dm),BF),M((2,rc,nq),F32),M((1,2*dm+2*HD),F32),M((2*ns,1,2*dm+2*HD),F32),
         M(both.shape,BF),M((per,dm),BF),M((2,rr,h),BF),M((2,d-1,rr,h),BF),M((2,rc,nq),BF),M((2,d-1,rc,nq),BF),
         D_((22,)),D_((ns,)),D_((ns,))]+[D_((4,nr,2,d-1))]+[D_((2*nq//128,d-1))]*4+Scatter.scratch(per,dm)*2+([] if fused else [M((2,dm,nq),BF)]),
        cid,'tail',[A_,A_]+[V_]*3+[A_]+[V_]*4,[A_]+[V_]*4+[A_]*3+[V_]*3+[A_]*13)
def widen_kernel(split,ng,*refs):
    n=(len(refs)-1)//2
    for a,b in zip(refs[:n-ng-1],refs[n:]): b[...]=a[...].astype(b.dtype)
    both=refs[n-ng-1]; down,out=refs[2*n-ng-1:2*n-ng+1]
    for a,b in zip(refs[n-ng:n],refs[-ng:]): b[...]=a[...].reshape(-1)
    rd,ro=split
    for c in range(both.shape[0]//(rd+ro)):
        p=c*(rd+ro)
        down[c*rd:(c+1)*rd,:]=both[p:p+rd,:].astype(F32); out[c*ro:(c+1)*ro,:]=both[p+rd:p+rd+ro,:].astype(F32)

def widen(arrays,plain,both,gains,rows,chunks,steps=4):
    spec=lambda n,w: pl.BlockSpec((n//steps,w),lambda i:(i,0))
    w=both.shape[1]
    ins=[spec(*a.shape) for a in arrays+plain]
    return pl.pallas_call(functools.partial(widen_kernel,(rows//chunks,(both.shape[0]-rows)//chunks),len(gains)),grid=(steps,),in_specs=ins+[spec(*both.shape)]+[V_]*len(gains),out_specs=ins+[spec(rows,w),spec(both.shape[0]-rows,w)]+[V_]*len(gains),
        out_shape=[S_(a.shape,F32) for a in arrays]+[S_(a.shape,a.dtype) for a in plain]+[S_((rows,w),F32),S_((both.shape[0]-rows,w),F32)]+[S_((g.shape[1],),F32) for g in gains],name='widen')(*arrays,*plain,both,*gains)

def local(nd,nt,tokens,w_query,w_key,w_value,w_out,w_gate,w_up,w_down,norm_attn,norm_mlp,norm_query,norm_key,cotangent,segments,positions):
    scale=HD**-0.5
    ne=cotangent.shape[0]//4
    a1,q,k,v,xh,r,cos,sin,early,late=front(tokens,cotangent,positions,jnp.asarray(FREQS[:,None]),norm_attn,norm_query,norm_key,w_query,w_key,w_value,ne,4,1)
    late=lax.ppermute(late,'tensor',[(i,(i+2)%nt) for i in range(nt)])
    att,lse=attn_fwd(q,k,v,positions,512,512,scale)
    att,late=lax.optimization_barrier((att,late))
    hid,a2,act,dg,du,outp,dap,dy=middle(att,w_out,tokens,cotangent,early,late,w_gate,w_up,w_down,norm_mlp,4,2)
    dhid,gm,dwg,dwu,both,dout=post(hid,cotangent,norm_mlp,w_out,a2,dy,act,dg,du,dap,att,nd,3)
    output,d_tokens,dwq,dwk,dwv,both,ga,gm,gq,gk=tail(tokens,norm_attn,norm_query,norm_key,gm,w_query,w_key,w_value,positions,lse,r,both,
        q,k,v,dout,att,xh,cos,sin,a1,outp,hid,dhid,nd,nt,512,256,scale,4)
    dwq,dwk,dwv,dwg,dwu,output,d_tokens,dwd,dwo,ga,gm,gq,gk=widen((dwq,dwk,dwv,dwg,dwu),(output,d_tokens),both,(ga,gm,gq,gk),w_down.shape[0],nd)
    return (output,d_tokens,dwq,dwk,dwv,dwo,dwg,dwu,dwd,ga,gm,gq,gk)

def solution(mesh):
    nd,nt=mesh.shape['dp'],mesh.shape['tensor']
    row=P(('dp','tensor'),None); col=P(None,'tensor'); rw=P('tensor',None)
    return jax.shard_map(functools.partial(local,nd,nt),mesh=mesh,
        in_specs=(row,col,col,col,rw,col,col,rw,P(),P(),P(),P(),row,P('dp',None),P('dp',None)),
        out_specs=(row,row,col,col,col,rw,col,col,rw,P(),P(),P(),P()),check_vma=False)
```
